512 devices in a mesh: gx: 16 (over z, core), gy: 8 (over y), gz: 4 (over x).
Axes of the slice: x: 4, y: 8, z: 8, core: 2. Of those that a mesh axis runs over, the one named last changes fastest.
Arguments:
- right_side: float32 [64, 16, 64, 512], P(None, 'gx', 'gy', 'gz'), may hold values from -180 to 180
- velocity: float32 [3, 16, 64, 512], P(None, 'gx', 'gy', 'gz'), may hold values from 0.1 to 1
- decay_rate: float32 [16, 64, 512], P('gx', 'gy', 'gz'), may hold values from 0.3 to 3
- perm_class: int32 [16, 64, 512], P('gx', 'gy', 'gz'), may hold values from 0 to 15
- conductivity: float32 [16], replicated, may hold values from 0.25 to 2.5
- well_cells: int32 [32], replicated, may hold values from 0 to 524287
- well_rate: float32 [32], replicated, may hold values from 4 to 16
Outputs:
- solution_field: float32 [64, 16, 64, 512], P(None, 'gx', 'gy', 'gz')
- residual: float32 [64, 16, 64, 512], P(None, 'gx', 'gy', 'gz')
The draws below stay inside these ranges and needn't reach their ends.
Inputs may be any that keep to these rules, and one draw needn't show every extreme that they name: `well_cells`: flat index (x * 64 + y) * 512 + z of a cell; two wells may share a cell.
All inputs are finite; a program needn't handle non-finite values.
Results may differ from the reference program's by a relative error of at most 0.0015.
Values sent between devices are 32-bit elements; how exact they have to be, the bound alone decides.
No kernel may reach another device: no remote copies, remote signals or barrier semaphores. Data moves between devices by JAX's collectives and lax.ppermute only.
A program may use at most 64 MiB of HBM per device.

```python
import math
import jax
import jax.numpy as jnp
from jax import lax

M = 64
ITERS = 2
NCLASS = 16
WELLS = 32
NX = 16
NY = 64
NZ = 512


def draw_right_side(key, part):
    key_list = jax.random.split(key, 3)
    column_scale = jnp.exp(jax.random.uniform(key_list[0], (M,), jnp.float32, math.log(0.5), math.log(5.0)))
    column_scale = jnp.where(jnp.arange(M) == 0, 5.0, column_scale)
    x_frac = jnp.arange(NX, dtype=jnp.float32) / max(NX - 1, 1)
    y_frac = jnp.arange(NY, dtype=jnp.float32) / max(NY - 1, 1)
    z_frac = jnp.arange(NZ, dtype=jnp.float32) / max(NZ - 1, 1)
    rise = jnp.exp(math.log(3.0) * (2.0 * x_frac[:, None, None] + y_frac[None, :, None] + z_frac[None, None, :]) / 2.0)
    shape = (M, NX, NY, NZ)
    rough = jax.random.uniform(key_list[1], shape, jnp.float32, 0.5, 1.5)
    core = jax.random.normal(key_list[2], shape, jnp.float32) * rough
    core = jnp.clip(core, -4.0, 4.0)
    value = column_scale[:, None, None, None] * rise[None] * core
    value = value.at[0, NX - 1, NY - 1, NZ - 1].set(180.0)
    value = value.at[0, NX - 1, NY - 1, NZ - 2].set(-180.0)
    return value.astype(jnp.float32)


def set_ends(values, own_key, least, top_value):
    index_at = [jax.random.randint(jax.random.fold_in(own_key, axis), (), 0, length) for axis, length in enumerate(values.shape)]
    longest = values.shape.index(max(values.shape))
    neighbour = index_at[:longest] + [(index_at[longest] + 1) % values.shape[longest]] + index_at[longest + 1:]
    return values.at[tuple(index_at)].set(least).at[tuple(neighbour)].set(top_value)


def block_levels(stream_key, extent, cuts, low, high):
    def one(position, parts):
        heights = jax.random.uniform(jax.random.fold_in(jax.random.fold_in(stream_key, 6), position), (parts,), jnp.float32, low / len(cuts), high / len(cuts))
        return jnp.repeat(jnp.exp(heights), extent[position] // parts).reshape((-1,) + (1,) * (len(extent) - position - 1))

    gain = one(*cuts[0])
    for cut in cuts[1:]:
        gain = gain * one(*cut)
    return gain


def setup_inputs(seed: int = 0) -> dict:
    arg_keys = jax.random.split(jax.random.key(seed), 8)
    right_side = draw_right_side(jax.random.fold_in(arg_keys[7], 71), 0)
    velocity = jnp.clip(jnp.exp(math.log(1.0) - 2.3025851 * jax.random.uniform(arg_keys[1], (3, NX, NY, NZ), jnp.float32) ** block_levels(arg_keys[1], (3, NX, NY, NZ), ((1, 16), (2, 8), (3, 4)), -0.2, 0.2)), 0.1, 1.0)
    decay_rate = jnp.clip(jnp.exp(math.log(3.0) - 2.3025851 * jax.random.uniform(arg_keys[2], (NX, NY, NZ), jnp.float32) ** block_levels(arg_keys[2], (NX, NY, NZ), ((0, 16), (1, 8), (2, 4)), -0.2, 0.2)), 0.3, 3.0)
    perm_class = set_ends(jax.random.randint(arg_keys[3], (NX, NY, NZ), 0, NCLASS), jax.random.fold_in(arg_keys[3], 1), 0, NCLASS - 1).astype(jnp.int32)
    conductivity = jnp.clip(jnp.exp(jax.random.uniform(arg_keys[4], (NCLASS,), jnp.float32, math.log(0.25), math.log(2.5))), 0.25, 2.5)
    well_cells = set_ends(jax.random.randint(arg_keys[5], (WELLS,), 0, NX * NY * NZ), jax.random.fold_in(arg_keys[5], 1), 0, (NX * NY * NZ) - 1).astype(jnp.int32)
    well_rate = jnp.clip(jnp.exp(jax.random.uniform(arg_keys[6], (WELLS,), jnp.float32, math.log(4.0), math.log(16.0))), 4.0, 16.0)
    return dict(right_side=right_side, velocity=velocity, decay_rate=decay_rate, perm_class=perm_class, conductivity=conductivity, well_cells=well_cells, well_rate=well_rate)


def gram_matrix(first_block, second_block):
    return jnp.einsum('aijk,bijk->ab', first_block, second_block, precision=lax.Precision.HIGHEST)

def combine(field, coefs):
    return jnp.einsum('ab,aijk->bijk', coefs, field, precision=lax.Precision.HIGHEST)

def solve_block(matrix, wanted):
    normal = jnp.dot(matrix.T, matrix, precision=lax.Precision.HIGHEST)
    target = jnp.dot(matrix.T, wanted, precision=lax.Precision.HIGHEST)
    factor = jnp.linalg.cholesky(normal)
    return jax.scipy.linalg.cho_solve((factor, True), target)

def face_terms(conduct, conduct_rim, velocity, decay_rate, well_sum):
    plus_faces = [0.5 * (conduct + conduct_rim[2:, 1:-1, 1:-1]), 0.5 * (conduct + conduct_rim[1:-1, 2:, 1:-1]), 0.5 * (conduct + conduct_rim[1:-1, 1:-1, 2:])]
    minus_faces = [0.5 * (conduct + conduct_rim[:-2, 1:-1, 1:-1]), 0.5 * (conduct + conduct_rim[1:-1, :-2, 1:-1]), 0.5 * (conduct + conduct_rim[1:-1, 1:-1, :-2])]
    diagonal_sum = decay_rate + well_sum
    for index in range(3):
        diagonal_sum = diagonal_sum + (velocity[index] + plus_faces[index] + minus_faces[index])
    upper_coefs = [velocity[index] + plus_faces[index] for index in range(3)]
    return (diagonal_sum, upper_coefs, minus_faces)

def apply_operator(field, padded, diagonal_sum, upper_coefs, lower_coefs):
    result = diagonal_sum * field
    result = result - (upper_coefs[0] * padded[:, 2:, 1:-1, 1:-1] + lower_coefs[0] * padded[:, :-2, 1:-1, 1:-1])
    result = result - (upper_coefs[1] * padded[:, 1:-1, 2:, 1:-1] + lower_coefs[1] * padded[:, 1:-1, :-2, 1:-1])
    result = result - (upper_coefs[2] * padded[:, 1:-1, 1:-1, 2:] + lower_coefs[2] * padded[:, 1:-1, 1:-1, :-2])
    return result

def reference(right_side, velocity, decay_rate, perm_class, conductivity, well_cells, well_rate):
    conduct = conductivity[perm_class]
    conduct_rim = jnp.pad(conduct, 1)
    well_sum = jnp.zeros((NX * NY * NZ,), jnp.float32).at[well_cells].add(well_rate).reshape(NX, NY, NZ)
    diagonal_sum, upper_coefs, lower_coefs = face_terms(conduct, conduct_rim, velocity, decay_rate, well_sum)

    def apply_block(field):
        padded = jnp.pad(field, ((0, 0), (1, 1), (1, 1), (1, 1)))
        return apply_operator(field, padded, diagonal_sum, upper_coefs, lower_coefs)
    shadow = right_side
    solution_field = jnp.zeros_like(right_side)
    residual = right_side
    direction = right_side
    for turn_index in range(ITERS):
        image_block = apply_block(direction)
        image_gram = gram_matrix(shadow, image_block)
        alpha_coef = solve_block(image_gram, gram_matrix(shadow, residual))
        half_step = residual - combine(image_block, alpha_coef)
        second = apply_block(half_step)
        omega_scale = jnp.sum(second * half_step) / jnp.sum(second * second)
        solution_field = solution_field + combine(direction, alpha_coef) + omega_scale * half_step
        residual = half_step - omega_scale * second
        if turn_index + 1 < ITERS:
            beta_coef = solve_block(image_gram, -gram_matrix(shadow, second))
            direction = residual + combine(direction - omega_scale * image_block, beta_coef)
    return (solution_field, residual)
```

```python
import functools

import jax
import jax.numpy as jnp
from jax import lax
from jax.experimental import pallas as pl
from jax.experimental.pallas import tpu as pltpu
from jax.sharding import PartitionSpec as P

SHIFT = 7.5
SCALE = 3.0
LEVELS = 5
M = 64
NEXTRA = 5
NF = M + NEXTRA
GROUPS = 16
NE = 5
HI = lax.Precision.HIGHEST


def iota_row():
    return lax.broadcasted_iota(jnp.int32, (8, 128), 0)


def iota_lane():
    return lax.broadcasted_iota(jnp.int32, (8, 128), 1)


def roll_lane(tile, shift):
    shift = shift % 128
    return tile if shift == 0 else pltpu.roll(tile, shift, 1)


def roll_row(tile, shift):
    shift = shift % 8
    return tile if shift == 0 else pltpu.roll(tile, shift, 0)


def swap_shift(first, second, roll, shift, mask):
    first, second = roll(first, shift), roll(second, shift)
    return jnp.where(mask, second, first), jnp.where(mask, first, second)


def tile(ref, index):
    if isinstance(index, int):
        return ref[8 * index : 8 * index + 8, :]
    return ref[pl.ds(pl.multiple_of(index * 8, 8), 8), :]


def put(ref, index, value):
    if isinstance(index, int):
        ref[8 * index : 8 * index + 8, :] = value
    else:
        ref[pl.ds(pl.multiple_of(index * 8, 8), 8), :] = value


def group_mask(lane, q):
    at = (lane + (4 - 8 * q)) & 127
    return at < 8


def pack_kernel(right_ref, vel_ref, decay_ref, class_ref, table_ref, zmsg_ref, conduct_ref):
    lane = iota_lane()
    classes = class_ref[...]
    conduct = jnp.zeros((8, 128), jnp.float32)
    for index in range(table_ref.shape[0]):
        conduct = jnp.where(classes == index, table_ref[index], conduct)
    conduct_ref[...] = conduct

    def packed(get):
        total = jnp.zeros((8, 128), jnp.float32)
        for q in range(GROUPS):
            value = get(q)
            if value is None:
                break
            total = jnp.where(group_mask(lane, q), roll_lane(value, 8 * q), total)
        return total

    for t in range(M // GROUPS):
        put(zmsg_ref, t, packed(lambda q, t=t: tile(right_ref, t * GROUPS + q)))
    extra = [tile(vel_ref, 0), tile(vel_ref, 1), tile(vel_ref, 2), decay_ref[...], conduct]
    put(zmsg_ref, NE - 1, packed(lambda q: extra[q] if q < NEXTRA else None))


def ymsg_kernel(
    right_ref, vel_ref, decay_ref, conduct_ref, low_ref, high_ref, up_ref, down_ref, edge_ref
):
    row, lane = iota_row(), iota_lane()
    edges = []
    for t in range(NE):
        edge = jnp.where((lane & 7) >= 4, tile(low_ref, t), tile(high_ref, t))
        put(edge_ref, t, edge)
        edges.append(edge)

    def source(index):
        if index < M:
            return tile(right_ref, index)
        if index < M + 3:
            return tile(vel_ref, index - M)
        if index == M + 3:
            return decay_ref[...]
        if index == M + 4:
            return conduct_ref[...]
        return edges[index - NF]

    lower = row < 4
    for g in range((NF + NE) // 2):
        first, second = source(2 * g), roll_row(source(2 * g + 1), 4)
        put(up_ref, g, jnp.where(lower, second, first))
        put(down_ref, g, jnp.where(lower, first, second))


X1 = 2 * M + 2 * NE + 2


def xmsg_kernel(right_ref, conduct_ref, edge_ref, below_ref, above_ref, msg_ref, extra_ref):
    row = iota_row()
    lower = row < 4
    for f in range(M):
        put(msg_ref, f, tile(right_ref, f))
    for t in range(NE):
        put(msg_ref, 2 * M + t, tile(edge_ref, t))
    put(msg_ref, 2 * M + 2 * NE, conduct_ref[...])
    for g in range((NF + NE) // 2):
        below, above = tile(below_ref, g), tile(above_ref, g)
        pair = (jnp.where(lower, above, below), roll_row(jnp.where(lower, below, above), 4))
        for half in range(2):
            index = 2 * g + half
            if index < M:
                put(msg_ref, M + index, pair[half])
            elif index < M + 4:
                put(extra_ref, index - M, pair[half])
            elif index == M + 4:
                put(msg_ref, 2 * M + 2 * NE + 1, pair[half])
            else:
                put(msg_ref, 2 * M + NE + index - NF, pair[half])


def coefficients(sizes, cells_ref, rate_ref, vel_ref, decay_ref, extra_ref, own_ref, left_ref, right_ref, coef_ref):
    row, lane = iota_row(), iota_lane()
    size_y, size_z = sizes
    at_x, at_y, at_z = lax.axis_index("gx"), lax.axis_index("gy"), lax.axis_index("gz")

    def parts(ref):
        base = 2 * M
        return [
            tile(ref, base + 2 * NE),
            tile(ref, base + 2 * NE + 1),
            roll_lane(tile(ref, base + NE - 1), -8 * 4),
            roll_lane(tile(ref, base + 2 * NE - 1), -8 * 4),
        ]

    edge_m, edge_y = tile(own_ref, 2 * M + NE - 1), tile(own_ref, 2 * M + 2 * NE - 1)

    def given(main, index):
        return [main, tile(extra_ref, index), roll_lane(edge_m, -8 * index), roll_lane(edge_y, -8 * index)]

    velocity = [given(tile(vel_ref, d), d) for d in range(3)]
    decay = given(decay_ref[...], 3)
    center, before, after = parts(own_ref), parts(left_ref), parts(right_ref)

    def shift_y(four, shift, mask):
        main, my = swap_shift(four[0], four[1], roll_row, shift, mask)
        edge, ey = swap_shift(four[2], four[3], roll_row, shift, mask)
        return [main, my, edge, ey]

    def shift_z(four, shift, mask):
        main, edge = swap_shift(four[0], four[2], roll_lane, shift, mask)
        my, ey = swap_shift(four[1], four[3], roll_lane, shift, mask)
        return [main, my, edge, ey]

    plus = [after, shift_y(center, -1, row == 7), shift_z(center, -1, lane == 127)]
    minus = [before, shift_y(center, 1, row == 0), shift_z(center, 1, lane == 0)]

    y_main = at_y * 8 + row
    y_my = at_y * 8 + jnp.where(row < 4, row + 8, row - 8)
    z_main = at_z * 128 + lane
    z_edge = at_z * 128 + jnp.where(lane < 64, lane + 128, lane - 128)
    for part, (y_at, z_at) in enumerate(((y_main, z_main), (y_my, z_main), (y_main, z_edge), (y_my, z_edge))):
        flat = (at_x * size_y + y_at) * size_z + z_at
        wells = jnp.zeros((8, 128), jnp.float32)
        for w in range(cells_ref.shape[0]):
            wells = wells + jnp.where(flat == cells_ref[w], rate_ref[w], 0.0)
        inside = (y_at >= 0) & (y_at < size_y) & (z_at >= 0) & (z_at < size_z)
        if part >= 2:
            inside = inside & ((lane < 4) | (lane >= 124))
        diagonal = decay[part] + wells
        upper, lower = [], []
        for d in range(3):
            plus_face = 0.5 * (center[part] + plus[d][part])
            minus_face = 0.5 * (center[part] + minus[d][part])
            diagonal = diagonal + (velocity[d][part] + plus_face + minus_face)
            upper.append(velocity[d][part] + plus_face)
            lower.append(minus_face)
        values = [(diagonal - SHIFT) * (1.0 / SCALE)]
        for d in range(3):
            values += [upper[d] * (-1.0 / SCALE), lower[d] * (-1.0 / SCALE)]
        for index, value in enumerate(values):
            value = jnp.where(inside, value, 0.0)
            if part >= 2:
                for shift in (8, 16, 32, 64):
                    value = value + roll_lane(value, shift)
            put(coef_ref, index * 4 + part, value)


def unpack_my(level, ref, t, q, base):
    if level == 1:
        return tile(ref, base + t * GROUPS + q)
    if level == 2:
        return roll_row(tile(ref, base + t * (GROUPS // 2) + q // 2), -4 * (q % 2))
    return roll_row(tile(ref, base + t * (GROUPS // 4) + q // 4), -2 * (q % 4))


def edge_base(level):
    return {1: 2 * M, 2: M + M // 2, 3: M + M // 4}[level]


def message_tiles(level):
    return {1: X1, 2: M + M // 2 + 8, 3: M + M // 4 + 4, 4: M}[level]


def step_body(level, coef_ref, main_ref, my_ref, my_base, em_ref, em_base, ey_ref, ey_base, left_ref, right_ref, out_ref, out_my_ref, out_e_ref):
    row, lane = iota_row(), iota_lane()
    row_0, row_7 = row == 0, row == 7
    lane_0, lane_127 = lane == 0, lane == 127
    with_my = level < 4
    with_ey = level < 3
    keep_2 = (row < 2) | (row >= 6)

    def coef(index, part):
        return tile(coef_ref, index * 4 + part)

    def apply(part, center, after, before, y_plus, y_minus, z_plus, z_minus):
        total = coef(0, part) * center
        if after is not None:
            total = total + (coef(1, part) * after + coef(2, part) * before)
        total = total + (coef(3, part) * y_plus + coef(4, part) * y_minus)
        return total + (coef(5, part) * z_plus + coef(6, part) * z_minus)

    def group(t, carry):
        em = tile(em_ref, em_base + t)
        ey = tile(ey_ref, ey_base + t) if with_my else None
        near_m = jnp.zeros((8, 128), jnp.float32)
        near_y = jnp.zeros((8, 128), jnp.float32)
        packed = None
        for q in range(GROUPS):
            f = t * GROUPS + q
            main, my = tile(main_ref, f), tile(my_ref, my_base + f)
            beside = roll_lane(em, -8 * q)
            z_plus = roll_lane(jnp.where(lane_0, beside, main), -1)
            z_minus = roll_lane(jnp.where(lane_127, beside, main), 1)
            y_plus, my_plus = swap_shift(main, my, roll_row, -1, row_7)
            y_minus, my_minus = swap_shift(main, my, roll_row, 1, row_0)
            result = apply(0, main, tile(right_ref, f), tile(left_ref, f), y_plus, y_minus, z_plus, z_minus)
            put(out_ref, f, result)
            if not with_my:
                continue
            at = ((lane + (1 - 8 * q)) & 127) < 2
            near_m = jnp.where(at, roll_lane(main, 8 * q), near_m)
            beside = roll_lane(ey, -8 * q)
            z_plus = roll_lane(jnp.where(lane_0, beside, my), -1)
            z_minus = roll_lane(jnp.where(lane_127, beside, my), 1)
            result = apply(
                1,
                my,
                unpack_my(level, right_ref, t, q, M),
                unpack_my(level, left_ref, t, q, M),
                my_plus,
                my_minus,
                z_plus,
                z_minus,
            )
            put(out_my_ref, f, result)
            if with_ey:
                near_y = jnp.where(at, roll_lane(my, 8 * q), near_y)
            if level == 1:
                packed = result if q % 2 == 0 else jnp.where(keep_2, packed, roll_row(result, 4))
                if q % 2 == 1:
                    put(out_ref, M + t * (GROUPS // 2) + q // 2, packed)
            elif level == 2:
                s = q % 4
                at_row = ((row + (1 - 2 * s)) & 7) < 2
                packed = result if s == 0 else jnp.where(at_row, roll_row(result, 2 * s), packed)
                if s == 3:
                    put(out_ref, M + t * (GROUPS // 4) + q // 4, packed)
        if with_my:
            seven, zero = (lane & 7) == 7, (lane & 7) == 0
            base = edge_base(level)
            em_plus, ey_plus = swap_shift(em, ey, roll_row, -1, row_7)
            em_minus, ey_minus = swap_shift(em, ey, roll_row, 1, row_0)
            z_plus = jnp.where(seven, roll_lane(near_m, -1), roll_lane(em, -1))
            z_minus = jnp.where(zero, roll_lane(near_m, 1), roll_lane(em, 1))
            result = apply(2, em, tile(right_ref, base + t), tile(left_ref, base + t), em_plus, em_minus, z_plus, z_minus)
            put(out_e_ref, t, result)
            if level < 3:
                put(out_ref, edge_base(level + 1) + t, result)
            if with_ey:
                z_plus = jnp.where(seven, roll_lane(near_y, -1), roll_lane(ey, -1))
                z_minus = jnp.where(zero, roll_lane(near_y, 1), roll_lane(ey, 1))
                base = base + (NE if level == 1 else 4)
                result = apply(3, ey, tile(right_ref, base + t), tile(left_ref, base + t), ey_plus, ey_minus, z_plus, z_minus)
                put(out_e_ref, 4 + t, result)
                if level == 1:
                    put(out_ref, edge_base(2) + 4 + t, result)
        return carry

    lax.fori_loop(0, M // GROUPS, group, 0)


def first_kernel(sizes, cells_ref, rate_ref, vel_ref, decay_ref, extra_ref, own_ref, left_ref, right_ref, coef_ref, out_ref, out_my_ref, out_e_ref):
    coefficients(sizes, cells_ref, rate_ref, vel_ref, decay_ref, extra_ref, own_ref, left_ref, right_ref, coef_ref)
    step_body(1, coef_ref, own_ref, own_ref, M, own_ref, 2 * M, own_ref, 2 * M + NE, left_ref, right_ref, out_ref, out_my_ref, out_e_ref)


def middle_kernel(level, coef_ref, own_ref, my_ref, e_ref, left_ref, right_ref, out_ref, out_my_ref, out_e_ref):
    step_body(level, coef_ref, own_ref, my_ref, 0, e_ref, 0, e_ref, 4, left_ref, right_ref, out_ref, out_my_ref, out_e_ref)


PAIRS = (
    ((0, 0), (0, 1)),
    ((0, 2), (0, 3)),
    ((1, 1), (1, 2)),
    ((1, 3), (1, 4)),
    ((2, 2), (2, 3)),
    ((3, 3), (3, 4)),
    ((4, 4), (2, 4)),
    ((0, 4), None),
)


def dot_nt(first, second):
    return lax.dot_general(first, second, (((1,), (1,)), ((), ())), precision=HI, preferred_element_type=jnp.float32)


def dot_tn(first, second):
    return lax.dot_general(first, second, (((0,), (0,)), ((), ())), precision=HI, preferred_element_type=jnp.float32)


def dot_nn(first, second):
    return lax.dot_general(first, second, (((1,), (0,)), ((), ())), precision=HI, preferred_element_type=jnp.float32)


def gram_kernel(coef_ref, own_ref, my_ref, e_ref, left_ref, right_ref, block_0, block_1, block_2, basis_ref, gram_ref, last_ref):
    step_body(4, coef_ref, own_ref, my_ref, 0, e_ref, 0, None, 0, left_ref, right_ref, last_ref, None, None)
    for level, ref in enumerate((block_0, block_1, block_2, own_ref, last_ref)):
        for y in range(8):
            basis_ref[M * level : M * (level + 1), 128 * y : 128 * (y + 1)] = ref[pl.ds(y, M, stride=8), :]
    full = dot_nt(basis_ref[...], basis_ref[...])
    for index, pair in enumerate(PAIRS):
        for half, at in enumerate(pair):
            if at is None:
                value = jnp.zeros((M, M), jnp.float32)
            else:
                value = full[M * at[0] : M * at[0] + M, M * at[1] : M * at[1] + M]
            gram_ref[M * index : M * (index + 1), M * half : M * (half + 1)] = value


def eliminate(matrix, wanted):
    both = jnp.concatenate([matrix, wanted], axis=1)
    rows = lax.broadcasted_iota(jnp.int32, both.shape, 0)
    for k in range(M):
        pivot_row = both[k : k + 1, :]
        scaled = pivot_row / pivot_row[:, k : k + 1]
        column = both[:, k : k + 1]
        both = jnp.where(rows == k, scaled, both - column * scaled)
    return both[:, M:]


def apply_levels(blocks):
    out = [SHIFT * b for b in blocks] + [None]
    for j, b in enumerate(blocks):
        out[j + 1] = SCALE * b if out[j + 1] is None else out[j + 1] + SCALE * b
    return out


def pad_levels(blocks, count):
    return list(blocks) + [jnp.zeros((M, M), jnp.float32)] * (count - len(blocks))


def final_kernel(gram_ref, basis_ref, field_ref, resid_ref, full_ref):
    for index, pair in enumerate(PAIRS):
        for half, at in enumerate(pair):
            if at is None:
                continue
            value = gram_ref[M * index : M * (index + 1), M * half : M * (half + 1)]
            full_ref[M * at[0] : M * at[0] + M, M * at[1] : M * at[1] + M] = value
            if at[0] != at[1]:
                full_ref[M * at[1] : M * at[1] + M, M * at[0] : M * at[0] + M] = value.T
    eye = jnp.where(
        lax.broadcasted_iota(jnp.int32, (M, M), 0) == lax.broadcasted_iota(jnp.int32, (M, M), 1), 1.0, 0.0
    ).astype(jnp.float32)

    def gram(levels, blocks):
        count = M * levels
        return dot_nn(full_ref[0:count, 0 : M * len(blocks)], jnp.concatenate(blocks, axis=0))

    def minimal(half, second):
        levels = len(second)
        product = gram(levels, second)
        cross = sum(product[M * j : M * j + M] * b for j, b in enumerate(half))
        square = sum(product[M * j : M * j + M] * b for j, b in enumerate(second))
        return jnp.sum(cross) / jnp.sum(square), product[0:M]

    image_gram = SHIFT * full_ref[0:M, 0:M] + SCALE * full_ref[0:M, M : 2 * M]
    inverse = eliminate(dot_tn(image_gram, image_gram), image_gram.T)
    alpha = dot_nn(inverse, full_ref[0:M, 0:M])
    half = [eye - SHIFT * alpha, -SCALE * alpha]
    second = apply_levels(half)
    omega, second_gram = minimal(half, second)
    field = [alpha + omega * half[0], omega * half[1]]
    resid = [half[0] - omega * second[0], half[1] - omega * second[1], -omega * second[2]]
    beta = -dot_nn(inverse, second_gram)
    direct = [
        resid[0] + (1.0 - omega * SHIFT) * beta,
        resid[1] - (omega * SCALE) * beta,
        resid[2],
    ]
    image = apply_levels(direct)
    stacked = jnp.concatenate(
        [jnp.concatenate(image, axis=0), jnp.concatenate(pad_levels(resid, 4), axis=0)], axis=1
    )
    both = dot_nn(full_ref[0:M, 0 : 4 * M], stacked)
    image_gram, resid_gram = both[:, 0:M], both[:, M:]
    inverse = eliminate(dot_tn(image_gram, image_gram), image_gram.T)
    alpha = dot_nn(inverse, resid_gram)
    product = dot_nn(jnp.concatenate(image + direct, axis=0), alpha)
    half = [r - product[M * j : M * j + M] for j, r in enumerate(pad_levels(resid, 4))]
    second = apply_levels(half)
    omega, _ = minimal(half, second)
    field = pad_levels(field, 4)
    moved = [product[M * (4 + j) : M * (5 + j)] for j in range(3)] + [None]
    field = [
        f + omega * h + (0.0 if m is None else m) for f, h, m in zip(field, half, moved)
    ]
    field = pad_levels(field, 5)
    resid = [h - omega * s for h, s in zip(pad_levels(half, 5), second)]
    coefs = jnp.concatenate([jnp.concatenate(field, axis=0), jnp.concatenate(resid, axis=0)], axis=1)
    for y in range(8):
        result = dot_tn(coefs, basis_ref[:, 128 * y : 128 * (y + 1)])
        field_ref[pl.ds(y, M, stride=8), :] = result[0:M]
        resid_ref[pl.ds(y, M, stride=8), :] = result[M:]


VMEM = pl.BlockSpec(memory_space=pltpu.VMEM)
SMEM = pl.BlockSpec(memory_space=pltpu.SMEM)


def f32(*shape):
    return jax.ShapeDtypeStruct(shape, jnp.float32)


def call(kernel, name, outs, specs, scratch=()):
    return pl.pallas_call(
        kernel,
        name=name,
        out_shape=outs,
        in_specs=specs,
        out_specs=tuple(VMEM for _ in outs) if isinstance(outs, tuple) else VMEM,
        scratch_shapes=list(scratch),
        compiler_params=pltpu.CompilerParams(vmem_limit_bytes=32 * 1024 * 1024),
    )


def from_sides(axis, up, down):
    count = lax.axis_size(axis)
    lower = lax.ppermute(up, axis, [(i, i + 1) for i in range(count - 1)])
    upper = lax.ppermute(down, axis, [(i + 1, i) for i in range(count - 1)])
    return lower, upper


def spread(values, axes):
    count = lax.axis_size(axes)
    return lax.all_to_all(jnp.broadcast_to(values, (count, *values.shape)), axes, 0, 0)


def per_device(right_side, velocity, decay_rate, perm_class, conductivity, well_cells, well_rate):
    sizes = (8 * lax.axis_size("gy"), 128 * lax.axis_size("gz"))
    block_0 = right_side.reshape(8 * M, 128)
    vel = velocity.reshape(24, 128)
    decay = decay_rate.reshape(8, 128)
    classes = perm_class.reshape(8, 128)

    zmsg, conduct = call(
        pack_kernel, "pack", (f32(8 * NE, 128), f32(8, 128)), [VMEM, VMEM, VMEM, VMEM, SMEM]
    )(block_0, vel, decay, classes, conductivity)
    low, high = from_sides("gz", zmsg, zmsg)
    tiles = 8 * ((NF + NE) // 2)
    up, down, edge = call(
        ymsg_kernel, "ymsg", (f32(tiles, 128), f32(tiles, 128), f32(8 * NE, 128)), [VMEM] * 6
    )(block_0, vel, decay, conduct, low, high)
    below, above = from_sides("gy", up, down)
    own, extra = call(xmsg_kernel, "xmsg", (f32(8 * X1, 128), f32(32, 128)), [VMEM] * 5)(
        block_0, conduct, edge, below, above
    )
    left, right = from_sides("gx", own, own)

    def outs(level):
        return (f32(8 * message_tiles(level + 1), 128), f32(8 * M, 128), f32(64, 128))

    coef, block_1, my, edges = call(
        functools.partial(first_kernel, sizes),
        "first",
        (f32(8 * 28, 128), *outs(1)),
        [SMEM, SMEM] + [VMEM] * 6,
    )(well_cells, well_rate, vel, decay, extra, own, left, right)
    left, right = from_sides("gx", block_1, block_1)
    block_2, my, edges = call(functools.partial(middle_kernel, 2), "second", outs(2), [VMEM] * 6)(
        coef, block_1, my, edges, left, right
    )
    left, right = from_sides("gx", block_2, block_2)
    block_3, my, edges = call(functools.partial(middle_kernel, 3), "third", outs(3), [VMEM] * 6)(
        coef, block_2, my, edges, left, right
    )
    left, right = from_sides("gx", block_3, block_3)
    basis, gram = call(
        gram_kernel,
        "gram",
        (f32(LEVELS * M, 1024), f32(8 * M, 128)),
        [VMEM] * 9,
        [pltpu.VMEM((8 * M, 128), jnp.float32)],
    )(coef, block_3, my, edges, left, right, block_0, block_1, block_2)

    plane = ("gy", "gz")
    count = lax.axis_size(plane)
    gram = lax.all_to_all(gram.reshape(count, -1, 128), plane, 0, 0)
    gram = jnp.sum(gram, axis=0)
    gram = jnp.sum(spread(gram, "gx"), axis=0)
    gram = spread(gram, plane).reshape(8 * M, 128)
    field, resid = call(
        final_kernel,
        "final",
        (f32(8 * M, 128), f32(8 * M, 128)),
        [VMEM, VMEM],
        [pltpu.VMEM((LEVELS * M, LEVELS * M), jnp.float32)],
    )(gram, basis)
    return field.reshape(right_side.shape), resid.reshape(right_side.shape)


def solution(mesh):
    placed = (
        P(None, "gx", "gy", "gz"),
        P(None, "gx", "gy", "gz"),
        P("gx", "gy", "gz"),
        P("gx", "gy", "gz"),
        P(),
        P(),
        P(),
    )
    return jax.shard_map(
        per_device,
        mesh=mesh,
        in_specs=placed,
        out_specs=(P(None, "gx", "gy", "gz"), P(None, "gx", "gy", "gz")),
        check_vma=False,
    )
```

```python
import functools

import jax
import jax.numpy as jnp
from jax import lax
from jax.experimental import pallas as pl
from jax.experimental.pallas import tpu as pltpu
from jax.sharding import PartitionSpec as P

SHIFT = 7.5
SCALE = 3.0
LEVELS = 5
M = 64
NEXTRA = 5
NF = M + NEXTRA
GROUPS = 16
NE = 5
HI = lax.Precision.HIGHEST


def iota_row():
    return lax.broadcasted_iota(jnp.int32, (8, 128), 0)


def iota_lane():
    return lax.broadcasted_iota(jnp.int32, (8, 128), 1)


def roll_lane(tile, shift):
    shift = shift % 128
    return tile if shift == 0 else pltpu.roll(tile, shift, 1)


def roll_row(tile, shift):
    shift = shift % 8
    return tile if shift == 0 else pltpu.roll(tile, shift, 0)


def swap_shift(first, second, roll, shift, mask):
    first, second = roll(first, shift), roll(second, shift)
    return jnp.where(mask, second, first), jnp.where(mask, first, second)


def tile(ref, index):
    if isinstance(index, int):
        return ref[8 * index : 8 * index + 8, :]
    return ref[pl.ds(pl.multiple_of(index * 8, 8), 8), :]


def put(ref, index, value):
    if isinstance(index, int):
        ref[8 * index : 8 * index + 8, :] = value
    else:
        ref[pl.ds(pl.multiple_of(index * 8, 8), 8), :] = value


def group_mask(lane, q):
    at = (lane + (4 - 8 * q)) & 127
    return at < 8


def pack_kernel(right_ref, vel_ref, decay_ref, class_ref, table_ref, zmsg_ref, conduct_ref):
    lane = iota_lane()
    classes = class_ref[...]
    conduct = jnp.zeros((8, 128), jnp.float32)
    for index in range(table_ref.shape[0]):
        conduct = jnp.where(classes == index, table_ref[index], conduct)
    conduct_ref[...] = conduct

    def packed(get):
        total = jnp.zeros((8, 128), jnp.float32)
        for q in range(GROUPS):
            value = get(q)
            if value is None:
                break
            total = jnp.where(group_mask(lane, q), roll_lane(value, 8 * q), total)
        return total

    for t in range(M // GROUPS):
        put(zmsg_ref, t, packed(lambda q, t=t: tile(right_ref, t * GROUPS + q)))
    extra = [tile(vel_ref, 0), tile(vel_ref, 1), tile(vel_ref, 2), decay_ref[...], conduct]
    put(zmsg_ref, NE - 1, packed(lambda q: extra[q] if q < NEXTRA else None))


def ymsg_kernel(
    right_ref, vel_ref, decay_ref, conduct_ref, low_ref, high_ref, up_ref, down_ref, edge_ref
):
    row, lane = iota_row(), iota_lane()
    edges = []
    for t in range(NE):
        edge = jnp.where((lane & 7) >= 4, tile(low_ref, t), tile(high_ref, t))
        put(edge_ref, t, edge)
        edges.append(edge)

    def source(index):
        if index < M:
            return tile(right_ref, index)
        if index < M + 3:
            return tile(vel_ref, index - M)
        if index == M + 3:
            return decay_ref[...]
        if index == M + 4:
            return conduct_ref[...]
        return edges[index - NF]

    lower = row < 4
    for g in range((NF + NE) // 2):
        first, second = source(2 * g), roll_row(source(2 * g + 1), 4)
        put(up_ref, g, jnp.where(lower, second, first))
        put(down_ref, g, jnp.where(lower, first, second))


X1 = 2 * M + 2 * NE + 2


def xmsg_kernel(right_ref, conduct_ref, edge_ref, below_ref, above_ref, msg_ref, extra_ref):
    row = iota_row()
    lower = row < 4
    for f in range(M):
        put(msg_ref, f, tile(right_ref, f))
    for t in range(NE):
        put(msg_ref, 2 * M + t, tile(edge_ref, t))
    put(msg_ref, 2 * M + 2 * NE, conduct_ref[...])
    for g in range((NF + NE) // 2):
        below, above = tile(below_ref, g), tile(above_ref, g)
        pair = (jnp.where(lower, above, below), roll_row(jnp.where(lower, below, above), 4))
        for half in range(2):
            index = 2 * g + half
            if index < M:
                put(msg_ref, M + index, pair[half])
            elif index < M + 4:
                put(extra_ref, index - M, pair[half])
            elif index == M + 4:
                put(msg_ref, 2 * M + 2 * NE + 1, pair[half])
            else:
                put(msg_ref, 2 * M + NE + index - NF, pair[half])


def coefficients(sizes, cells_ref, rate_ref, vel_ref, decay_ref, extra_ref, own_ref, left_ref, right_ref, coef_ref):
    row, lane = iota_row(), iota_lane()
    size_y, size_z = sizes
    at_x, at_y, at_z = lax.axis_index("gx"), lax.axis_index("gy"), lax.axis_index("gz")

    def parts(ref):
        base = 2 * M
        return [
            tile(ref, base + 2 * NE),
            tile(ref, base + 2 * NE + 1),
            roll_lane(tile(ref, base + NE - 1), -8 * 4),
            roll_lane(tile(ref, base + 2 * NE - 1), -8 * 4),
        ]

    edge_m, edge_y = tile(own_ref, 2 * M + NE - 1), tile(own_ref, 2 * M + 2 * NE - 1)

    def given(main, index):
        return [main, tile(extra_ref, index), roll_lane(edge_m, -8 * index), roll_lane(edge_y, -8 * index)]

    velocity = [given(tile(vel_ref, d), d) for d in range(3)]
    decay = given(decay_ref[...], 3)
    center, before, after = parts(own_ref), parts(left_ref), parts(right_ref)

    def shift_y(four, shift, mask):
        main, my = swap_shift(four[0], four[1], roll_row, shift, mask)
        edge, ey = swap_shift(four[2], four[3], roll_row, shift, mask)
        return [main, my, edge, ey]

    def shift_z(four, shift, mask):
        main, edge = swap_shift(four[0], four[2], roll_lane, shift, mask)
        my, ey = swap_shift(four[1], four[3], roll_lane, shift, mask)
        return [main, my, edge, ey]

    plus = [after, shift_y(center, -1, row == 7), shift_z(center, -1, lane == 127)]
    minus = [before, shift_y(center, 1, row == 0), shift_z(center, 1, lane == 0)]

    y_main = at_y * 8 + row
    y_my = at_y * 8 + jnp.where(row < 4, row + 8, row - 8)
    z_main = at_z * 128 + lane
    z_edge = at_z * 128 + jnp.where(lane < 64, lane + 128, lane - 128)
    for part, (y_at, z_at) in enumerate(((y_main, z_main), (y_my, z_main), (y_main, z_edge), (y_my, z_edge))):
        flat = (at_x * size_y + y_at) * size_z + z_at
        wells = jnp.zeros((8, 128), jnp.float32)
        for w in range(cells_ref.shape[0]):
            wells = wells + jnp.where(flat == cells_ref[w], rate_ref[w], 0.0)
        inside = (y_at >= 0) & (y_at < size_y) & (z_at >= 0) & (z_at < size_z)
        if part >= 2:
            inside = inside & ((lane < 4) | (lane >= 124))
        diagonal = decay[part] + wells
        upper, lower = [], []
        for d in range(3):
            plus_face = 0.5 * (center[part] + plus[d][part])
            minus_face = 0.5 * (center[part] + minus[d][part])
            diagonal = diagonal + (velocity[d][part] + plus_face + minus_face)
            upper.append(velocity[d][part] + plus_face)
            lower.append(minus_face)
        values = [(diagonal - SHIFT) * (1.0 / SCALE)]
        for d in range(3):
            values += [upper[d] * (-1.0 / SCALE), lower[d] * (-1.0 / SCALE)]
        for index, value in enumerate(values):
            value = jnp.where(inside, value, 0.0)
            if part >= 2:
                for shift in (8, 16, 32, 64):
                    value = value + roll_lane(value, shift)
            put(coef_ref, index * 4 + part, value)


def unpack_my(level, ref, t, q, base):
    if level == 1:
        return tile(ref, base + t * GROUPS + q)
    if level == 2:
        return roll_row(tile(ref, base + t * (GROUPS // 2) + q // 2), -4 * (q % 2))
    return roll_row(tile(ref, base + t * (GROUPS // 4) + q // 4), -2 * (q % 4))


def edge_base(level):
    return {1: 2 * M, 2: M + M // 2, 3: M + M // 4}[level]


def message_tiles(level):
    return {1: X1, 2: M + M // 2 + 8, 3: M + M // 4 + 4, 4: M}[level]


def step_body(level, coef_ref, main_ref, my_ref, my_base, em_ref, em_base, ey_ref, ey_base, left_ref, right_ref, out_ref, out_my_ref, out_e_ref):
    row, lane = iota_row(), iota_lane()
    row_0, row_7 = row == 0, row == 7
    lane_0, lane_127 = lane == 0, lane == 127
    with_my = level < 4
    with_ey = level < 3
    keep_2 = (row < 2) | (row >= 6)

    def coef(index, part):
        return tile(coef_ref, index * 4 + part)

    def apply(part, center, after, before, y_plus, y_minus, z_plus, z_minus):
        total = coef(0, part) * center
        if after is not None:
            total = total + (coef(1, part) * after + coef(2, part) * before)
        total = total + (coef(3, part) * y_plus + coef(4, part) * y_minus)
        return total + (coef(5, part) * z_plus + coef(6, part) * z_minus)

    def group(t, carry):
        em = tile(em_ref, em_base + t)
        ey = tile(ey_ref, ey_base + t) if with_my else None
        near_m = jnp.zeros((8, 128), jnp.float32)
        near_y = jnp.zeros((8, 128), jnp.float32)
        packed = None
        for q in range(GROUPS):
            f = t * GROUPS + q
            main, my = tile(main_ref, f), tile(my_ref, my_base + f)
            beside = roll_lane(em, -8 * q)
            z_plus = roll_lane(jnp.where(lane_0, beside, main), -1)
            z_minus = roll_lane(jnp.where(lane_127, beside, main), 1)
            y_plus, my_plus = swap_shift(main, my, roll_row, -1, row_7)
            y_minus, my_minus = swap_shift(main, my, roll_row, 1, row_0)
            result = apply(0, main, tile(right_ref, f), tile(left_ref, f), y_plus, y_minus, z_plus, z_minus)
            put(out_ref, f, result)
            if not with_my:
                continue
            at = ((lane + (1 - 8 * q)) & 127) < 2
            near_m = jnp.where(at, roll_lane(main, 8 * q), near_m)
            beside = roll_lane(ey, -8 * q)
            z_plus = roll_lane(jnp.where(lane_0, beside, my), -1)
            z_minus = roll_lane(jnp.where(lane_127, beside, my), 1)
            result = apply(
                1,
                my,
                unpack_my(level, right_ref, t, q, M),
                unpack_my(level, left_ref, t, q, M),
                my_plus,
                my_minus,
                z_plus,
                z_minus,
            )
            put(out_my_ref, f, result)
            if with_ey:
                near_y = jnp.where(at, roll_lane(my, 8 * q), near_y)
            if level == 1:
                packed = result if q % 2 == 0 else jnp.where(keep_2, packed, roll_row(result, 4))
                if q % 2 == 1:
                    put(out_ref, M + t * (GROUPS // 2) + q // 2, packed)
            elif level == 2:
                s = q % 4
                at_row = ((row + (1 - 2 * s)) & 7) < 2
                packed = result if s == 0 else jnp.where(at_row, roll_row(result, 2 * s), packed)
                if s == 3:
                    put(out_ref, M + t * (GROUPS // 4) + q // 4, packed)
        if with_my:
            seven, zero = (lane & 7) == 7, (lane & 7) == 0
            base = edge_base(level)
            em_plus, ey_plus = swap_shift(em, ey, roll_row, -1, row_7)
            em_minus, ey_minus = swap_shift(em, ey, roll_row, 1, row_0)
            z_plus = jnp.where(seven, roll_lane(near_m, -1), roll_lane(em, -1))
            z_minus = jnp.where(zero, roll_lane(near_m, 1), roll_lane(em, 1))
            result = apply(2, em, tile(right_ref, base + t), tile(left_ref, base + t), em_plus, em_minus, z_plus, z_minus)
            put(out_e_ref, t, result)
            if level < 3:
                put(out_ref, edge_base(level + 1) + t, result)
            if with_ey:
                z_plus = jnp.where(seven, roll_lane(near_y, -1), roll_lane(ey, -1))
                z_minus = jnp.where(zero, roll_lane(near_y, 1), roll_lane(ey, 1))
                base = base + (NE if level == 1 else 4)
                result = apply(3, ey, tile(right_ref, base + t), tile(left_ref, base + t), ey_plus, ey_minus, z_plus, z_minus)
                put(out_e_ref, 4 + t, result)
                if level == 1:
                    put(out_ref, edge_base(2) + 4 + t, result)
        return carry

    lax.fori_loop(0, M // GROUPS, group, 0)


def first_kernel(sizes, cells_ref, rate_ref, vel_ref, decay_ref, extra_ref, own_ref, left_ref, right_ref, coef_ref, out_ref, out_my_ref, out_e_ref):
    coefficients(sizes, cells_ref, rate_ref, vel_ref, decay_ref, extra_ref, own_ref, left_ref, right_ref, coef_ref)
    step_body(1, coef_ref, own_ref, own_ref, M, own_ref, 2 * M, own_ref, 2 * M + NE, left_ref, right_ref, out_ref, out_my_ref, out_e_ref)


def middle_kernel(level, coef_ref, own_ref, my_ref, e_ref, left_ref, right_ref, out_ref, out_my_ref, out_e_ref):
    step_body(level, coef_ref, own_ref, my_ref, 0, e_ref, 0, e_ref, 4, left_ref, right_ref, out_ref, out_my_ref, out_e_ref)


PAIRS = (
    ((0, 0), (0, 1)),
    ((0, 2), (0, 3)),
    ((1, 1), (1, 2)),
    ((1, 3), (1, 4)),
    ((2, 2), (2, 3)),
    ((3, 3), (3, 4)),
    ((4, 4), (2, 4)),
    ((0, 4), None),
)


def dot_nt(first, second):
    return lax.dot_general(first, second, (((1,), (1,)), ((), ())), precision=HI, preferred_element_type=jnp.float32)


def dot_tn(first, second):
    return lax.dot_general(first, second, (((0,), (0,)), ((), ())), precision=HI, preferred_element_type=jnp.float32)


def dot_nn(first, second):
    return lax.dot_general(first, second, (((1,), (0,)), ((), ())), precision=HI, preferred_element_type=jnp.float32)


def gram_kernel(coef_ref, own_ref, my_ref, e_ref, left_ref, right_ref, block_0, block_1, block_2, basis_ref, gram_ref, last_ref):
    step_body(4, coef_ref, own_ref, my_ref, 0, e_ref, 0, None, 0, left_ref, right_ref, last_ref, None, None)
    for level, ref in enumerate((block_0, block_1, block_2, own_ref, last_ref)):
        for y in range(8):
            basis_ref[M * level : M * (level + 1), 128 * y : 128 * (y + 1)] = ref[pl.ds(y, M, stride=8), :]
    full = dot_nt(basis_ref[...], basis_ref[...])
    for index, pair in enumerate(PAIRS):
        for half, at in enumerate(pair):
            if at is None:
                value = jnp.zeros((M, M), jnp.float32)
            else:
                value = full[M * at[0] : M * at[0] + M, M * at[1] : M * at[1] + M]
            gram_ref[M * index : M * (index + 1), M * half : M * (half + 1)] = value


def eliminate(matrix, wanted):
    both = jnp.concatenate([matrix, wanted], axis=1)
    tiles = [both[8 * i : 8 * i + 8, :] for i in range(M // 8)]
    rows = iota_row()

    def column(value, at):
        return jnp.broadcast_to(value[:, at : at + 1], (8, 128))

    for i in range(M // 8):
        columns = [[column(t, 8 * i + b) for b in range(8)] for t in tiles]
        row = [jnp.broadcast_to(tiles[i][a : a + 1, :], (8, 128)) for a in range(8)]
        small = [
            [jnp.broadcast_to(columns[i][b][a : a + 1, :], (8, 128)) for b in range(8)]
            for a in range(8)
        ]
        for p in range(8):
            inverse = 1.0 / small[p][p]
            for a in range(p + 1, 8):
                factor = small[a][p] * inverse
                row[a] = row[a] - factor * row[p]
                for b in range(p + 1, 8):
                    small[a][b] = small[a][b] - factor * small[p][b]
            row[p] = row[p] * inverse
            for b in range(p + 1, 8):
                small[p][b] = small[p][b] * inverse
        for p in range(7, 0, -1):
            for a in range(p):
                row[a] = row[a] - small[a][p] * row[p]
        for j in range(M // 8):
            if j == i:
                value = row[0]
                for b in range(1, 8):
                    value = jnp.where(rows == b, row[b], value)
            else:
                value = tiles[j]
                for b in range(8):
                    value = value - columns[j][b] * row[b]
            tiles[j] = value
    return jnp.concatenate(tiles, axis=0)[:, M:]


def apply_levels(blocks):
    out = [SHIFT * b for b in blocks] + [None]
    for j, b in enumerate(blocks):
        out[j + 1] = SCALE * b if out[j + 1] is None else out[j + 1] + SCALE * b
    return out


def pad_levels(blocks, count):
    return list(blocks) + [jnp.zeros((M, M), jnp.float32)] * (count - len(blocks))


def final_kernel(gram_ref, basis_ref, field_ref, resid_ref, full_ref):
    for index, pair in enumerate(PAIRS):
        for half, at in enumerate(pair):
            if at is None:
                continue
            value = gram_ref[M * index : M * (index + 1), M * half : M * (half + 1)]
            full_ref[M * at[0] : M * at[0] + M, M * at[1] : M * at[1] + M] = value
            if at[0] != at[1]:
                full_ref[M * at[1] : M * at[1] + M, M * at[0] : M * at[0] + M] = value.T
    eye = jnp.where(
        lax.broadcasted_iota(jnp.int32, (M, M), 0) == lax.broadcasted_iota(jnp.int32, (M, M), 1), 1.0, 0.0
    ).astype(jnp.float32)

    def gram(levels, blocks):
        count = M * levels
        return dot_nn(full_ref[0:count, 0 : M * len(blocks)], jnp.concatenate(blocks, axis=0))

    def minimal(half, second):
        levels = len(second)
        product = gram(levels, second)
        cross = sum(product[M * j : M * j + M] * b for j, b in enumerate(half))
        square = sum(product[M * j : M * j + M] * b for j, b in enumerate(second))
        return jnp.sum(cross) / jnp.sum(square), product[0:M]

    image_gram = SHIFT * full_ref[0:M, 0:M] + SCALE * full_ref[0:M, M : 2 * M]
    inverse = eliminate(dot_tn(image_gram, image_gram), image_gram.T)
    alpha = dot_nn(inverse, full_ref[0:M, 0:M])
    half = [eye - SHIFT * alpha, -SCALE * alpha]
    second = apply_levels(half)
    omega, second_gram = minimal(half, second)
    field = [alpha + omega * half[0], omega * half[1]]
    resid = [half[0] - omega * second[0], half[1] - omega * second[1], -omega * second[2]]
    beta = -dot_nn(inverse, second_gram)
    direct = [
        resid[0] + (1.0 - omega * SHIFT) * beta,
        resid[1] - (omega * SCALE) * beta,
        resid[2],
    ]
    image = apply_levels(direct)
    stacked = jnp.concatenate(
        [jnp.concatenate(image, axis=0), jnp.concatenate(pad_levels(resid, 4), axis=0)], axis=1
    )
    both = dot_nn(full_ref[0:M, 0 : 4 * M], stacked)
    image_gram, resid_gram = both[:, 0:M], both[:, M:]
    inverse = eliminate(dot_tn(image_gram, image_gram), image_gram.T)
    alpha = dot_nn(inverse, resid_gram)
    product = dot_nn(jnp.concatenate(image + direct, axis=0), alpha)
    half = [r - product[M * j : M * j + M] for j, r in enumerate(pad_levels(resid, 4))]
    second = apply_levels(half)
    omega, _ = minimal(half, second)
    field = pad_levels(field, 4)
    moved = [product[M * (4 + j) : M * (5 + j)] for j in range(3)] + [None]
    field = [
        f + omega * h + (0.0 if m is None else m) for f, h, m in zip(field, half, moved)
    ]
    field = pad_levels(field, 5)
    resid = [h - omega * s for h, s in zip(pad_levels(half, 5), second)]
    coefs = jnp.concatenate([jnp.concatenate(field, axis=0), jnp.concatenate(resid, axis=0)], axis=1)
    for y in range(8):
        result = dot_tn(coefs, basis_ref[:, 128 * y : 128 * (y + 1)])
        field_ref[pl.ds(y, M, stride=8), :] = result[0:M]
        resid_ref[pl.ds(y, M, stride=8), :] = result[M:]


VMEM = pl.BlockSpec(memory_space=pltpu.VMEM)
SMEM = pl.BlockSpec(memory_space=pltpu.SMEM)


def f32(*shape):
    return jax.ShapeDtypeStruct(shape, jnp.float32)


def call(kernel, name, outs, specs, scratch=()):
    return pl.pallas_call(
        kernel,
        name=name,
        out_shape=outs,
        in_specs=specs,
        out_specs=tuple(VMEM for _ in outs) if isinstance(outs, tuple) else VMEM,
        scratch_shapes=list(scratch),
        compiler_params=pltpu.CompilerParams(vmem_limit_bytes=32 * 1024 * 1024),
    )


def from_sides(axis, up, down):
    count = lax.axis_size(axis)
    lower = lax.ppermute(up, axis, [(i, i + 1) for i in range(count - 1)])
    upper = lax.ppermute(down, axis, [(i + 1, i) for i in range(count - 1)])
    return lower, upper


def spread(values, axes):
    count = lax.axis_size(axes)
    return lax.all_to_all(jnp.broadcast_to(values, (count, *values.shape)), axes, 0, 0)


def per_device(right_side, velocity, decay_rate, perm_class, conductivity, well_cells, well_rate):
    sizes = (8 * lax.axis_size("gy"), 128 * lax.axis_size("gz"))
    block_0 = right_side.reshape(8 * M, 128)
    vel = velocity.reshape(24, 128)
    decay = decay_rate.reshape(8, 128)
    classes = perm_class.reshape(8, 128)

    zmsg, conduct = call(
        pack_kernel, "pack", (f32(8 * NE, 128), f32(8, 128)), [VMEM, VMEM, VMEM, VMEM, SMEM]
    )(block_0, vel, decay, classes, conductivity)
    low, high = from_sides("gz", zmsg, zmsg)
    tiles = 8 * ((NF + NE) // 2)
    up, down, edge = call(
        ymsg_kernel, "ymsg", (f32(tiles, 128), f32(tiles, 128), f32(8 * NE, 128)), [VMEM] * 6
    )(block_0, vel, decay, conduct, low, high)
    below, above = from_sides("gy", up, down)
    own, extra = call(xmsg_kernel, "xmsg", (f32(8 * X1, 128), f32(32, 128)), [VMEM] * 5)(
        block_0, conduct, edge, below, above
    )
    left, right = from_sides("gx", own, own)

    def outs(level):
        return (f32(8 * message_tiles(level + 1), 128), f32(8 * M, 128), f32(64, 128))

    coef, block_1, my, edges = call(
        functools.partial(first_kernel, sizes),
        "first",
        (f32(8 * 28, 128), *outs(1)),
        [SMEM, SMEM] + [VMEM] * 6,
    )(well_cells, well_rate, vel, decay, extra, own, left, right)
    left, right = from_sides("gx", block_1, block_1)
    block_2, my, edges = call(functools.partial(middle_kernel, 2), "second", outs(2), [VMEM] * 6)(
        coef, block_1, my, edges, left, right
    )
    left, right = from_sides("gx", block_2, block_2)
    block_3, my, edges = call(functools.partial(middle_kernel, 3), "third", outs(3), [VMEM] * 6)(
        coef, block_2, my, edges, left, right
    )
    left, right = from_sides("gx", block_3, block_3)
    basis, gram = call(
        gram_kernel,
        "gram",
        (f32(LEVELS * M, 1024), f32(8 * M, 128)),
        [VMEM] * 9,
        [pltpu.VMEM((8 * M, 128), jnp.float32)],
    )(coef, block_3, my, edges, left, right, block_0, block_1, block_2)

    plane = ("gy", "gz")
    count = lax.axis_size(plane)
    gram = lax.all_to_all(gram.reshape(count, -1, 128), plane, 0, 0)
    gram = jnp.sum(gram, axis=0)
    gram = jnp.sum(spread(gram, "gx"), axis=0)
    gram = spread(gram, plane).reshape(8 * M, 128)
    field, resid = call(
        final_kernel,
        "final",
        (f32(8 * M, 128), f32(8 * M, 128)),
        [VMEM, VMEM],
        [pltpu.VMEM((LEVELS * M, LEVELS * M), jnp.float32)],
    )(gram, basis)
    return field.reshape(right_side.shape), resid.reshape(right_side.shape)


def solution(mesh):
    placed = (
        P(None, "gx", "gy", "gz"),
        P(None, "gx", "gy", "gz"),
        P("gx", "gy", "gz"),
        P("gx", "gy", "gz"),
        P(),
        P(),
        P(),
    )
    return jax.shard_map(
        per_device,
        mesh=mesh,
        in_specs=placed,
        out_specs=(P(None, "gx", "gy", "gz"), P(None, "gx", "gy", "gz")),
        check_vma=False,
    )
```

```python
import functools

import jax
import jax.numpy as jnp
from jax import lax
from jax.experimental import pallas as pl
from jax.experimental.pallas import tpu as pltpu
from jax.sharding import PartitionSpec as P

SHIFT = 7.5
SCALE = 3.0
LEVELS = 5
M = 64
HALF = M // 2
NEXTRA = 5
SLOT = HALF + NEXTRA
GROUPS = 16
TG = HALF // GROUPS
NE = 2 * TG + 1
HI = lax.Precision.HIGHEST


def iota_row():
    return lax.broadcasted_iota(jnp.int32, (8, 128), 0)


def iota_lane():
    return lax.broadcasted_iota(jnp.int32, (8, 128), 1)


def roll_lane(tile, shift):
    shift = shift % 128
    return tile if shift == 0 else pltpu.roll(tile, shift, 1)


def roll_row(tile, shift):
    shift = shift % 8
    return tile if shift == 0 else pltpu.roll(tile, shift, 0)


def swap_shift(first, second, roll, shift, mask):
    first, second = roll(first, shift), roll(second, shift)
    return jnp.where(mask, second, first), jnp.where(mask, first, second)


def tile(ref, index):
    if isinstance(index, int):
        return ref[8 * index : 8 * index + 8, :]
    return ref[pl.ds(pl.multiple_of(index * 8, 8), 8), :]


def put(ref, index, value):
    if isinstance(index, int):
        ref[8 * index : 8 * index + 8, :] = value
    else:
        ref[pl.ds(pl.multiple_of(index * 8, 8), 8), :] = value


def group_mask(lane, q):
    at = (lane + (4 - 8 * q)) & 127
    return at < 8


def core():
    return lax.rem(lax.axis_index("gx"), 2)


def pack_kernel(right_hbm, vel_hbm, decay_hbm, class_hbm, table_ref, send_ref, keep_ref, class_ref, sems):
    mine = pl.multiple_of(core() * 8 * HALF, 8)
    other = pl.multiple_of((1 - core()) * 8 * HALF, 8)
    copies = [
        (class_hbm, class_ref),
        (vel_hbm, keep_ref.at[pl.ds(8 * HALF, 24), :]),
        (decay_hbm, keep_ref.at[pl.ds(8 * (HALF + 3), 8), :]),
        (right_hbm.at[pl.ds(mine, 8 * HALF), :], keep_ref.at[pl.ds(0, 8 * HALF), :]),
        (right_hbm.at[pl.ds(other, 8 * HALF), :], send_ref.at[pl.ds(0, 8 * HALF), :]),
    ]
    copies = [pltpu.make_async_copy(src, dst, sems.at[i]) for i, (src, dst) in enumerate(copies)]
    for copy in copies:
        copy.start()
    for copy in copies:
        copy.wait()
    classes = class_ref[...]
    conduct = jnp.zeros((8, 128), jnp.float32)
    for index in range(table_ref.shape[0]):
        conduct = jnp.where(classes == index, table_ref[index], conduct)
    put(keep_ref, HALF + 4, conduct)
    put(send_ref, HALF + 4, conduct)
    for e in range(4):
        put(send_ref, HALF + e, tile(keep_ref, HALF + e))


def zmsg_kernel(keep_ref, got_ref, main_ref, zmsg_ref):
    lane = iota_lane()
    mine, other = core() * SLOT, (1 - core()) * SLOT
    for i in range(SLOT):
        put(main_ref, mine + i, tile(keep_ref, i))
        put(main_ref, other + i, tile(got_ref, i))

    def packed(indices):
        total = jnp.zeros((8, 128), jnp.float32)
        for q, index in enumerate(indices):
            total = jnp.where(group_mask(lane, q), roll_lane(tile(main_ref, index), 8 * q), total)
        return total

    for p in range(2):
        for t in range(TG):
            put(zmsg_ref, TG * p + t, packed([SLOT * p + GROUPS * t + q for q in range(GROUPS)]))
    put(zmsg_ref, NE - 1, packed([SLOT * p + HALF + e for p in range(2) for e in range(NEXTRA)]))


YPAIRS = (2 * SLOT + NE + 1) // 2


def ymsg_kernel(main_ref, low_ref, high_ref, up_ref, down_ref, edge_ref):
    row, lane = iota_row(), iota_lane()
    edges = []
    for t in range(NE):
        edge = jnp.where((lane & 7) >= 4, tile(low_ref, t), tile(high_ref, t))
        put(edge_ref, t, edge)
        edges.append(edge)

    def source(index):
        if index < 2 * SLOT:
            return tile(main_ref, index)
        return edges[min(index - 2 * SLOT, NE - 1)]

    lower = row < 4
    for g in range(YPAIRS):
        first, second = source(2 * g), roll_row(source(2 * g + 1), 4)
        put(up_ref, g, jnp.where(lower, second, first))
        put(down_ref, g, jnp.where(lower, first, second))


A_MY = SLOT
A_SECOND = 2 * SLOT
A_SECOND_MY = A_SECOND + HALF + 1
A_EDGE = A_SECOND_MY + HALF // 2 + 1
A_TILES = A_EDGE + 2 * NE
B_MY = HALF
B_EDGE = B_MY + HALF // 4
B_SECOND = B_EDGE + TG
B_TILES = B_SECOND + HALF


def xmsg_kernel(main_ref, edge_ref, below_ref, above_ref, my_ref, ey_ref, to_left_ref, to_right_ref):
    row = iota_row()
    lower = row < 4
    keep_2 = (row < 2) | (row >= 6)
    for g in range(YPAIRS):
        below, above = tile(below_ref, g), tile(above_ref, g)
        pair = (jnp.where(lower, above, below), roll_row(jnp.where(lower, below, above), 4))
        for half in range(2):
            index = 2 * g + half
            if index < 2 * SLOT:
                put(my_ref, index, pair[half])
                p, i = divmod(index, SLOT)
                put((to_left_ref, to_right_ref)[p], A_MY + i, pair[half])
                if i == SLOT - 1:
                    put((to_right_ref, to_left_ref)[p], A_SECOND_MY + HALF // 2, pair[half])
            elif index < 2 * SLOT + NE:
                put(ey_ref, index - 2 * SLOT, pair[half])
                for ref in (to_left_ref, to_right_ref):
                    put(ref, A_EDGE + NE + index - 2 * SLOT, pair[half])
    for p, (adjacent, second) in enumerate(((to_left_ref, to_right_ref), (to_right_ref, to_left_ref))):
        for i in range(SLOT):
            value = tile(main_ref, SLOT * p + i)
            put(adjacent, i, value)
            if i < HALF:
                put(second, A_SECOND + i, value)
            elif i == SLOT - 1:
                put(second, A_SECOND + HALF, value)
        for i in range(HALF // 2):
            value = jnp.where(
                keep_2,
                tile(my_ref, SLOT * p + 2 * i),
                roll_row(tile(my_ref, SLOT * p + 2 * i + 1), 4),
            )
            put(second, A_SECOND_MY + i, value)
    for t in range(NE):
        value = tile(edge_ref, t)
        put(to_left_ref, A_EDGE + t, value)
        put(to_right_ref, A_EDGE + t, value)


def plane_coefficients(sizes, cells_ref, rate_ref, conduct_ref, given_ref, coef_ref):
    row, lane = iota_row(), iota_lane()
    size_x, size_y, size_z = sizes
    first_x = lax.axis_index("gx") - core() - 1
    at_y, at_z = lax.axis_index("gy"), lax.axis_index("gz")
    y_main = at_y * 8 + row
    y_my = at_y * 8 + jnp.where(row < 4, row + 8, row - 8)
    z_main = at_z * 128 + lane
    z_edge = at_z * 128 + jnp.where(lane < 64, lane + 128, lane - 128)
    where = ((y_main, z_main), (y_my, z_main), (y_main, z_edge), (y_my, z_edge))

    def shift_y(four, shift, mask):
        main, my = swap_shift(four[0], four[1], roll_row, shift, mask)
        edge, ey = swap_shift(four[2], four[3], roll_row, shift, mask)
        return [main, my, edge, ey]

    def shift_z(four, shift, mask):
        main, edge = swap_shift(four[0], four[2], roll_lane, shift, mask)
        my, ey = swap_shift(four[1], four[3], roll_lane, shift, mask)
        return [main, my, edge, ey]

    def plane(s, carry):
        center = [tile(conduct_ref, (s + 1) * 4 + part) for part in range(4)]
        before = [tile(conduct_ref, s * 4 + part) for part in range(4)]
        after = [tile(conduct_ref, (s + 2) * 4 + part) for part in range(4)]
        plus = [after, shift_y(center, -1, row == 7), shift_z(center, -1, lane == 127)]
        minus = [before, shift_y(center, 1, row == 0), shift_z(center, 1, lane == 0)]
        at_x = first_x + s
        x_inside = (at_x >= 0) & (at_x < size_x)
        for part, (y_at, z_at) in enumerate(where):
            flat = (at_x * size_y + y_at) * size_z + z_at
            wells = jnp.zeros((8, 128), jnp.float32)
            for w in range(cells_ref.shape[0]):
                wells = wells + jnp.where(flat == cells_ref[w], rate_ref[w], 0.0)
            inside = (y_at >= 0) & (y_at < size_y) & (z_at >= 0) & (z_at < size_z) & x_inside
            if part >= 2:
                inside = inside & ((lane < 4) | (lane >= 124))
            given = [tile(given_ref, (s * 4 + e) * 4 + part) for e in range(4)]
            diagonal = given[3] + wells
            values = []
            for d in range(3):
                plus_face = 0.5 * (center[part] + plus[d][part])
                minus_face = 0.5 * (center[part] + minus[d][part])
                diagonal = diagonal + (given[d] + plus_face + minus_face)
                values += [(given[d] + plus_face) * (-1.0 / SCALE), minus_face * (-1.0 / SCALE)]
            for index, value in enumerate([(diagonal - SHIFT) * (1.0 / SCALE)] + values):
                value = jnp.where(inside, value, 0.0)
                if part >= 2:
                    for shift in (8, 16, 32, 64):
                        value = value + roll_lane(value, shift)
                put(coef_ref, (s * 7 + index) * 4 + part, value)
        return carry

    lax.fori_loop(0, 4, plane, 0)


def step(source, target, coef_ref, first, count, coef_shift, out_shift, with_my=True, with_em=True, with_ey=True):
    main_ref, my_ref, em_ref, ey_ref = source
    row, lane = iota_row(), iota_lane()
    row_0, row_7 = row == 0, row == 7
    lane_0, lane_127 = lane == 0, lane == 127

    def block(i, carry):
        s, t = first + lax.div(i, TG), lax.rem(i, TG)

        def apply(part, center, after, before, y_plus, y_minus, z_plus, z_minus):
            def coef(index):
                return tile(coef_ref, ((s + coef_shift) * 7 + index) * 4 + part)

            total = coef(0) * center + (coef(1) * after + coef(2) * before)
            total = total + (coef(3) * y_plus + coef(4) * y_minus)
            return total + (coef(5) * z_plus + coef(6) * z_minus)

        at_field, at_edge = s * HALF + t * GROUPS, s * TG + t
        out_field, out_edge = (s + out_shift) * HALF + t * GROUPS, (s + out_shift) * TG + t
        em = tile(em_ref, at_edge)
        ey = tile(ey_ref, at_edge) if with_em or with_my else None
        near_m = jnp.zeros((8, 128), jnp.float32)
        near_y = jnp.zeros((8, 128), jnp.float32)
        for q in range(GROUPS):
            f = at_field + q
            main, my = tile(main_ref, f), tile(my_ref, f)
            beside = roll_lane(em, -8 * q)
            z_plus = roll_lane(jnp.where(lane_0, beside, main), -1)
            z_minus = roll_lane(jnp.where(lane_127, beside, main), 1)
            y_plus, my_plus = swap_shift(main, my, roll_row, -1, row_7)
            y_minus, my_minus = swap_shift(main, my, roll_row, 1, row_0)
            after, before = tile(main_ref, f + HALF), tile(main_ref, f - HALF)
            put(target[0], out_field + q, apply(0, main, after, before, y_plus, y_minus, z_plus, z_minus))
            at = ((lane + (1 - 8 * q)) & 127) < 2
            if with_em:
                near_m = jnp.where(at, roll_lane(main, 8 * q), near_m)
            if with_ey:
                near_y = jnp.where(at, roll_lane(my, 8 * q), near_y)
            if with_my:
                beside = roll_lane(ey, -8 * q)
                z_plus = roll_lane(jnp.where(lane_0, beside, my), -1)
                z_minus = roll_lane(jnp.where(lane_127, beside, my), 1)
                after, before = tile(my_ref, f + HALF), tile(my_ref, f - HALF)
                put(target[1], out_field + q, apply(1, my, after, before, my_plus, my_minus, z_plus, z_minus))
        seven, zero = (lane & 7) == 7, (lane & 7) == 0
        if with_em:
            em_plus, ey_plus = swap_shift(em, ey, roll_row, -1, row_7)
            em_minus, ey_minus = swap_shift(em, ey, roll_row, 1, row_0)
            z_plus = jnp.where(seven, roll_lane(near_m, -1), roll_lane(em, -1))
            z_minus = jnp.where(zero, roll_lane(near_m, 1), roll_lane(em, 1))
            after, before = tile(em_ref, at_edge + TG), tile(em_ref, at_edge - TG)
            put(target[2], out_edge, apply(2, em, after, before, em_plus, em_minus, z_plus, z_minus))
        if with_ey:
            z_plus = jnp.where(seven, roll_lane(near_y, -1), roll_lane(ey, -1))
            z_minus = jnp.where(zero, roll_lane(near_y, 1), roll_lane(ey, 1))
            after, before = tile(ey_ref, at_edge + TG), tile(ey_ref, at_edge - TG)
            put(target[3], out_edge, apply(3, ey, after, before, ey_plus, ey_minus, z_plus, z_minus))
        return carry

    lax.fori_loop(0, count * TG, block, 0)


def copy_tiles(source, at, target, to, count):
    for i in range(count):
        put(target, to + i, tile(source, at + i))


def first_two_kernel(
    sizes,
    cells_ref,
    rate_ref,
    main_ref,
    edge_ref,
    my_ref,
    ey_ref,
    left_ref,
    right_ref,
    coef_ref,
    block_1_ref,
    block_2_ref,
    my_2_ref,
    em_2_ref,
    ey_2_ref,
    to_left_ref,
    to_right_ref,
    conduct_ref,
    given_ref,
    main_0,
    my_0,
    em_0,
    ey_0,
    main_1,
    my_1,
    em_1,
    ey_1,
):
    row = iota_row()
    for p in range(2):
        copy_tiles(main_ref, SLOT * p, main_0, HALF * (2 + p), HALF)
        copy_tiles(my_ref, SLOT * p, my_0, HALF * (2 + p), HALF)
        copy_tiles(edge_ref, TG * p, em_0, TG * (2 + p), TG)
        copy_tiles(ey_ref, TG * p, ey_0, TG * (2 + p), TG)
    extras = {2: (main_ref, HALF, my_ref, HALF, edge_ref, NE - 1, ey_ref, NE - 1, 0)}
    extras[3] = (main_ref, SLOT + HALF, my_ref, SLOT + HALF, edge_ref, NE - 1, ey_ref, NE - 1, NEXTRA)
    for ref, adjacent, second, p in ((left_ref, 1, 0, 1), (right_ref, 4, 5, 0)):
        copy_tiles(ref, 0, main_0, HALF * adjacent, HALF)
        copy_tiles(ref, A_MY, my_0, HALF * adjacent, HALF)
        copy_tiles(ref, A_SECOND, main_0, HALF * second, HALF)
        for i in range(HALF // 2):
            value = tile(ref, A_SECOND_MY + i)
            put(my_0, HALF * second + 2 * i, value)
            put(my_0, HALF * second + 2 * i + 1, roll_row(value, 4))
        for plane, at in ((adjacent, p), (second, 1 - p)):
            copy_tiles(ref, A_EDGE + TG * at, em_0, TG * plane, TG)
            copy_tiles(ref, A_EDGE + NE + TG * at, ey_0, TG * plane, TG)
        em_at, ey_at = A_EDGE + NE - 1, A_EDGE + 2 * NE - 1
        extras[adjacent] = (ref, HALF, ref, A_MY + HALF, ref, em_at, ref, ey_at, NEXTRA * p)
        for part, value in enumerate(
            (
                tile(ref, A_SECOND + HALF),
                tile(ref, A_SECOND_MY + HALF // 2),
                roll_lane(tile(ref, em_at), -8 * (NEXTRA * (1 - p) + 4)),
                roll_lane(tile(ref, ey_at), -8 * (NEXTRA * (1 - p) + 4)),
            )
        ):
            put(conduct_ref, 4 * second + part, value)
    for plane, (a, a_at, b, b_at, c, c_at, d, d_at, q) in extras.items():
        for e in range(NEXTRA):
            values = (
                tile(a, a_at + e),
                tile(b, b_at + e),
                roll_lane(tile(c, c_at), -8 * (q + e)),
                roll_lane(tile(d, d_at), -8 * (q + e)),
            )
            for part, value in enumerate(values):
                if e == NEXTRA - 1:
                    put(conduct_ref, 4 * plane + part, value)
                else:
                    put(given_ref, ((plane - 1) * 4 + e) * 4 + part, value)
    plane_coefficients(sizes, cells_ref, rate_ref, conduct_ref, given_ref, coef_ref)
    step((main_0, my_0, em_0, ey_0), (main_1, my_1, em_1, ey_1), coef_ref, 1, 4, -1, -1)
    copy_tiles(main_1, HALF, block_1_ref, 0, 2 * HALF)
    step((main_1, my_1, em_1, ey_1), (block_2_ref, my_2_ref, em_2_ref, ey_2_ref), coef_ref, 1, 2, 0, -1)
    for p, (adjacent, second) in enumerate(((to_left_ref, to_right_ref), (to_right_ref, to_left_ref))):
        for i in range(HALF):
            value = tile(block_2_ref, HALF * p + i)
            put(adjacent, i, value)
            put(second, B_SECOND + i, value)
        for i in range(HALF // 4):
            value = tile(my_2_ref, HALF * p + 4 * i)
            for k in range(1, 4):
                at_row = ((row + (1 - 2 * k)) & 7) < 2
                value = jnp.where(at_row, roll_row(tile(my_2_ref, HALF * p + 4 * i + k), 2 * k), value)
            put(adjacent, B_MY + i, value)
        copy_tiles(em_2_ref, TG * p, adjacent, B_EDGE, TG)


def last_two_kernel(
    coef_ref,
    block_1_ref,
    block_2_ref,
    my_2_ref,
    em_2_ref,
    ey_2_ref,
    left_ref,
    right_ref,
    keep_ref,
    send_ref,
    main_2,
    my_2,
    em_2,
    ey_2,
    main_3,
    my_3,
    em_3,
    main_4,
):
    copy_tiles(block_2_ref, 0, main_2, 2 * HALF, 2 * HALF)
    copy_tiles(my_2_ref, 0, my_2, 2 * HALF, 2 * HALF)
    copy_tiles(em_2_ref, 0, em_2, 2 * TG, 2 * TG)
    copy_tiles(ey_2_ref, 0, ey_2, 2 * TG, 2 * TG)
    for ref, adjacent, second in ((left_ref, 1, 0), (right_ref, 4, 5)):
        copy_tiles(ref, 0, main_2, HALF * adjacent, HALF)
        for i in range(HALF // 4):
            value = tile(ref, B_MY + i)
            for k in range(4):
                put(my_2, HALF * adjacent + 4 * i + k, roll_row(value, -2 * k))
        copy_tiles(ref, B_EDGE, em_2, TG * adjacent, TG)
        copy_tiles(ref, B_SECOND, main_2, HALF * second, HALF)
    source, target = (main_2, my_2, em_2, ey_2), (main_3, my_3, em_3, None)
    for plane in (1, 4):
        step(source, target, coef_ref, plane, 1, -1, -1, False, False, False)
    step(source, target, coef_ref, 2, 2, -1, -1, True, True, False)
    step((main_3, my_3, em_3, None), (main_4, None, None, None), coef_ref, 1, 2, 0, -1, False, False, False)
    mine, other = core() * HALF, (1 - core()) * HALF
    for level, (ref, base) in enumerate(((block_1_ref, 0), (block_2_ref, 0), (main_3, HALF), (main_4, 0))):
        for i in range(HALF):
            put(keep_ref, HALF * level + i, tile(ref, base + mine + i))
            put(send_ref, HALF * level + i, tile(ref, base + other + i))


PAIRS = (
    ((0, 0), (0, 1)),
    ((0, 2), (0, 3)),
    ((1, 1), (1, 2)),
    ((1, 3), (1, 4)),
    ((2, 2), (2, 3)),
    ((3, 3), (3, 4)),
    ((4, 4), (2, 4)),
    ((0, 4), None),
)


def dot_nt(first, second):
    return lax.dot_general(first, second, (((1,), (1,)), ((), ())), precision=HI, preferred_element_type=jnp.float32)


def dot_tn(first, second):
    return lax.dot_general(first, second, (((0,), (0,)), ((), ())), precision=HI, preferred_element_type=jnp.float32)


def dot_nn(first, second):
    return lax.dot_general(first, second, (((1,), (0,)), ((), ())), precision=HI, preferred_element_type=jnp.float32)


def gram_kernel(block_0, keep_ref, got_ref, basis_ref, gram_ref):
    mine, other = core() * HALF, (1 - core()) * HALF
    for y in range(8):
        lanes = slice(128 * y, 128 * (y + 1))
        basis_ref[0:M, lanes] = block_0[pl.ds(y, M, stride=8), :]
        for level in range(1, LEVELS):
            at = pl.ds(8 * HALF * (level - 1) + y, HALF, stride=8)
            basis_ref[pl.ds(pl.multiple_of(M * level + mine, 8), HALF), lanes] = keep_ref[at, :]
            basis_ref[pl.ds(pl.multiple_of(M * level + other, 8), HALF), lanes] = got_ref[at, :]
    full = dot_nt(basis_ref[...], basis_ref[...])
    for index, pair in enumerate(PAIRS):
        for half, at in enumerate(pair):
            if at is None:
                value = jnp.zeros((M, M), jnp.float32)
            else:
                value = full[M * at[0] : M * at[0] + M, M * at[1] : M * at[1] + M]
            gram_ref[M * index : M * (index + 1), M * half : M * (half + 1)] = value


def eliminate(matrix, wanted):
    both = jnp.concatenate([matrix, wanted], axis=1)
    tiles = [both[8 * i : 8 * i + 8, :] for i in range(M // 8)]
    rows = iota_row()

    def column(value, at):
        return jnp.broadcast_to(value[:, at : at + 1], (8, 128))

    for i in range(M // 8):
        columns = [[column(t, 8 * i + b) for b in range(8)] for t in tiles]
        row = [jnp.broadcast_to(tiles[i][a : a + 1, :], (8, 128)) for a in range(8)]
        small = [
            [jnp.broadcast_to(columns[i][b][a : a + 1, :], (8, 128)) for b in range(8)]
            for a in range(8)
        ]
        for p in range(8):
            inverse = 1.0 / small[p][p]
            for a in range(p + 1, 8):
                factor = small[a][p] * inverse
                row[a] = row[a] - factor * row[p]
                for b in range(p + 1, 8):
                    small[a][b] = small[a][b] - factor * small[p][b]
            row[p] = row[p] * inverse
            for b in range(p + 1, 8):
                small[p][b] = small[p][b] * inverse
        for p in range(7, 0, -1):
            for a in range(p):
                row[a] = row[a] - small[a][p] * row[p]
        for j in range(M // 8):
            if j == i:
                value = row[0]
                for b in range(1, 8):
                    value = jnp.where(rows == b, row[b], value)
            else:
                value = tiles[j]
                for b in range(8):
                    value = value - columns[j][b] * row[b]
            tiles[j] = value
    return jnp.concatenate(tiles, axis=0)[:, M:]


def apply_levels(blocks):
    out = [SHIFT * b for b in blocks] + [None]
    for j, b in enumerate(blocks):
        out[j + 1] = SCALE * b if out[j + 1] is None else out[j + 1] + SCALE * b
    return out


def pad_levels(blocks, count):
    return list(blocks) + [jnp.zeros((M, M), jnp.float32)] * (count - len(blocks))


def final_kernel(gram_ref, basis_ref, field_ref, resid_ref, full_ref):
    for index, pair in enumerate(PAIRS):
        for half, at in enumerate(pair):
            if at is None:
                continue
            value = gram_ref[M * index : M * (index + 1), M * half : M * (half + 1)]
            full_ref[M * at[0] : M * at[0] + M, M * at[1] : M * at[1] + M] = value
            if at[0] != at[1]:
                full_ref[M * at[1] : M * at[1] + M, M * at[0] : M * at[0] + M] = value.T
    eye = jnp.where(
        lax.broadcasted_iota(jnp.int32, (M, M), 0) == lax.broadcasted_iota(jnp.int32, (M, M), 1), 1.0, 0.0
    ).astype(jnp.float32)

    def gram(levels, blocks):
        count = M * levels
        return dot_nn(full_ref[0:count, 0 : M * len(blocks)], jnp.concatenate(blocks, axis=0))

    def minimal(half, second):
        levels = len(second)
        product = gram(levels, second)
        cross = sum(product[M * j : M * j + M] * b for j, b in enumerate(half))
        square = sum(product[M * j : M * j + M] * b for j, b in enumerate(second))
        return jnp.sum(cross) / jnp.sum(square), product[0:M]

    image_gram = SHIFT * full_ref[0:M, 0:M] + SCALE * full_ref[0:M, M : 2 * M]
    inverse = eliminate(dot_tn(image_gram, image_gram), image_gram.T)
    alpha = dot_nn(inverse, full_ref[0:M, 0:M])
    half = [eye - SHIFT * alpha, -SCALE * alpha]
    second = apply_levels(half)
    omega, second_gram = minimal(half, second)
    field = [alpha + omega * half[0], omega * half[1]]
    resid = [half[0] - omega * second[0], half[1] - omega * second[1], -omega * second[2]]
    beta = -dot_nn(inverse, second_gram)
    direct = [
        resid[0] + (1.0 - omega * SHIFT) * beta,
        resid[1] - (omega * SCALE) * beta,
        resid[2],
    ]
    image = apply_levels(direct)
    stacked = jnp.concatenate(
        [jnp.concatenate(image, axis=0), jnp.concatenate(pad_levels(resid, 4), axis=0)], axis=1
    )
    both = dot_nn(full_ref[0:M, 0 : 4 * M], stacked)
    image_gram, resid_gram = both[:, 0:M], both[:, M:]
    inverse = eliminate(dot_tn(image_gram, image_gram), image_gram.T)
    alpha = dot_nn(inverse, resid_gram)
    product = dot_nn(jnp.concatenate(image + direct, axis=0), alpha)
    half = [r - product[M * j : M * j + M] for j, r in enumerate(pad_levels(resid, 4))]
    second = apply_levels(half)
    omega, _ = minimal(half, second)
    field = pad_levels(field, 4)
    moved = [product[M * (4 + j) : M * (5 + j)] for j in range(3)] + [None]
    field = [
        f + omega * h + (0.0 if m is None else m) for f, h, m in zip(field, half, moved)
    ]
    field = pad_levels(field, 5)
    resid = [h - omega * s for h, s in zip(pad_levels(half, 5), second)]
    coefs = jnp.concatenate([jnp.concatenate(field, axis=0), jnp.concatenate(resid, axis=0)], axis=1)
    for y in range(8):
        result = dot_tn(coefs, basis_ref[:, 128 * y : 128 * (y + 1)])
        field_ref[pl.ds(y, M, stride=8), :] = result[0:M]
        resid_ref[pl.ds(y, M, stride=8), :] = result[M:]


VMEM = pl.BlockSpec(memory_space=pltpu.VMEM)
SMEM = pl.BlockSpec(memory_space=pltpu.SMEM)


def f32(*shape):
    return jax.ShapeDtypeStruct(shape, jnp.float32)


def call(kernel, name, outs, specs, scratch=()):
    return pl.pallas_call(
        kernel,
        name=name,
        out_shape=outs,
        in_specs=specs,
        out_specs=tuple(VMEM for _ in outs) if isinstance(outs, tuple) else VMEM,
        scratch_shapes=list(scratch),
        compiler_params=pltpu.CompilerParams(vmem_limit_bytes=32 * 1024 * 1024),
    )


def from_sides(axis, up, down, by=1):
    count = lax.axis_size(axis)
    lower = lax.ppermute(up, axis, [(i, i + by) for i in range(count - by)])
    upper = lax.ppermute(down, axis, [(i + by, i) for i in range(count - by)])
    return lower, upper


def spread(values, axes):
    count = lax.axis_size(axes)
    return lax.all_to_all(jnp.broadcast_to(values, (count, *values.shape)), axes, 0, 0)


def other_core(values):
    count = lax.axis_size("gx")
    return lax.ppermute(values, "gx", [(i, i ^ 1) for i in range(count)])


def tiles(count):
    return f32(8 * count, 128)


def scratch(*counts):
    return [pltpu.VMEM((8 * count, 128), jnp.float32) for count in counts]


def per_device(right_side, velocity, decay_rate, perm_class, conductivity, well_cells, well_rate):
    sizes = (lax.axis_size("gx"), 8 * lax.axis_size("gy"), 128 * lax.axis_size("gz"))
    block_0 = right_side.reshape(8 * M, 128)
    any_space = pl.BlockSpec(memory_space=pl.ANY)

    send, keep = call(
        pack_kernel,
        "pack",
        (tiles(SLOT), tiles(SLOT)),
        [any_space] * 4 + [SMEM],
        [pltpu.VMEM((8, 128), jnp.int32), pltpu.SemaphoreType.DMA((5,))],
    )(block_0, velocity.reshape(24, 128), decay_rate.reshape(8, 128), perm_class.reshape(8, 128), conductivity)
    got = other_core(send)
    main, zmsg = call(zmsg_kernel, "zmsg", (tiles(2 * SLOT), tiles(NE)), [VMEM] * 2)(keep, got)
    low, high = from_sides("gz", zmsg, zmsg)
    up, down, edge = call(ymsg_kernel, "ymsg", (tiles(YPAIRS), tiles(YPAIRS), tiles(NE)), [VMEM] * 3)(
        main, low, high
    )
    below, above = from_sides("gy", up, down)
    my, ey, to_left, to_right = call(
        xmsg_kernel, "xmsg", (tiles(2 * SLOT), tiles(NE), tiles(A_TILES), tiles(A_TILES)), [VMEM] * 4
    )(main, edge, below, above)
    left, right = from_sides("gx", to_right, to_left, 2)
    coef, block_1, block_2, my, em, ey, to_left, to_right = call(
        functools.partial(first_two_kernel, sizes),
        "first_two",
        (
            tiles(4 * 28),
            tiles(M),
            tiles(M),
            tiles(M),
            tiles(2 * TG),
            tiles(2 * TG),
            tiles(B_TILES),
            tiles(B_TILES),
        ),
        [SMEM, SMEM] + [VMEM] * 6,
        scratch(24, 64, 6 * HALF, 6 * HALF, 6 * TG, 6 * TG, 4 * HALF, 4 * HALF, 4 * TG, 4 * TG),
    )(well_cells, well_rate, main, edge, my, ey, left, right)
    left, right = from_sides("gx", to_right, to_left, 2)
    keep, send = call(
        last_two_kernel,
        "last_two",
        (tiles(4 * HALF), tiles(4 * HALF)),
        [VMEM] * 8,
        scratch(6 * HALF, 6 * HALF, 6 * TG, 6 * TG, 4 * HALF, 4 * HALF, 4 * TG, 2 * HALF),
    )(coef, block_1, block_2, my, em, ey, left, right)
    got = other_core(send)
    basis, gram = call(gram_kernel, "gram", (f32(LEVELS * M, 1024), f32(8 * M, 128)), [VMEM] * 3)(
        block_0, keep, got
    )

    plane = ("gy", "gz")
    count = lax.axis_size(plane)
    gram = lax.all_to_all(gram.reshape(count, -1, 128), plane, 0, 0)
    gram = jnp.sum(gram, axis=0)
    gram = jnp.sum(spread(gram, "gx"), axis=0)
    gram = spread(gram, plane).reshape(8 * M, 128)
    field, resid = call(
        final_kernel,
        "final",
        (f32(8 * M, 128), f32(8 * M, 128)),
        [VMEM, VMEM],
        [pltpu.VMEM((LEVELS * M, LEVELS * M), jnp.float32)],
    )(gram, basis)
    return field.reshape(right_side.shape), resid.reshape(right_side.shape)


def solution(mesh):
    placed = (
        P(None, "gx", "gy", "gz"),
        P(None, "gx", "gy", "gz"),
        P("gx", "gy", "gz"),
        P("gx", "gy", "gz"),
        P(),
        P(),
        P(),
    )
    return jax.shard_map(
        per_device,
        mesh=mesh,
        in_specs=placed,
        out_specs=(P(None, "gx", "gy", "gz"), P(None, "gx", "gy", "gz")),
        check_vma=False,
    )
```

```python
import functools

import jax
import jax.numpy as jnp
from jax import lax
from jax.experimental import pallas as pl
from jax.experimental.pallas import tpu as pltpu
from jax.sharding import PartitionSpec as P

SHIFT = 7.5
SCALE = 3.0
LEVELS = 5
M = 64
HALF = M // 2
NEXTRA = 5
SLOT = HALF + NEXTRA
GROUPS = 16
TG = HALF // GROUPS
NE = 2 * TG + 1
HI = lax.Precision.HIGHEST


def iota_row():
    return lax.broadcasted_iota(jnp.int32, (8, 128), 0)


def iota_lane():
    return lax.broadcasted_iota(jnp.int32, (8, 128), 1)


def roll_lane(tile, shift):
    shift = shift % 128
    return tile if shift == 0 else pltpu.roll(tile, shift, 1)


def roll_row(tile, shift):
    shift = shift % 8
    return tile if shift == 0 else pltpu.roll(tile, shift, 0)


def swap_shift(first, second, roll, shift, mask):
    first, second = roll(first, shift), roll(second, shift)
    return jnp.where(mask, second, first), jnp.where(mask, first, second)


def tile(ref, index):
    if isinstance(index, int):
        return ref[8 * index : 8 * index + 8, :]
    return ref[pl.ds(pl.multiple_of(index * 8, 8), 8), :]


def put(ref, index, value):
    if isinstance(index, int):
        ref[8 * index : 8 * index + 8, :] = value
    else:
        ref[pl.ds(pl.multiple_of(index * 8, 8), 8), :] = value


def group_mask(lane, q):
    at = (lane + (4 - 8 * q)) & 127
    return at < 8


def core():
    return lax.rem(lax.axis_index("gx"), 2)


def pack_kernel(right_hbm, vel_hbm, decay_hbm, class_hbm, table_hbm, send_ref, keep_ref, class_ref, table_ref, sems):
    mine = pl.multiple_of(core() * 8 * HALF, 8)
    other = pl.multiple_of((1 - core()) * 8 * HALF, 8)
    copies = [
        (class_hbm, class_ref),
        (table_hbm, table_ref),
        (vel_hbm, keep_ref.at[pl.ds(8 * HALF, 24), :]),
        (decay_hbm, keep_ref.at[pl.ds(8 * (HALF + 3), 8), :]),
        (right_hbm.at[pl.ds(mine, 8 * HALF), :], keep_ref.at[pl.ds(0, 8 * HALF), :]),
        (right_hbm.at[pl.ds(other, 8 * HALF), :], send_ref.at[pl.ds(0, 8 * HALF), :]),
    ]
    copies = [pltpu.make_async_copy(src, dst, sems.at[i]) for i, (src, dst) in enumerate(copies)]
    for copy in copies:
        copy.start()
    for copy in copies:
        copy.wait()
    classes = class_ref[...]
    conduct = jnp.zeros((8, 128), jnp.float32)
    for index in range(table_ref.shape[0]):
        conduct = jnp.where(classes == index, table_ref[index], conduct)
    put(keep_ref, HALF + 4, conduct)
    put(send_ref, HALF + 4, conduct)
    for e in range(4):
        put(send_ref, HALF + e, tile(keep_ref, HALF + e))


def zmsg_kernel(keep_ref, got_ref, main_ref, zmsg_ref):
    lane = iota_lane()
    mine, other = core() * SLOT, (1 - core()) * SLOT
    for i in range(SLOT):
        put(main_ref, mine + i, tile(keep_ref, i))
        put(main_ref, other + i, tile(got_ref, i))

    def packed(indices):
        total = jnp.zeros((8, 128), jnp.float32)
        for q, index in enumerate(indices):
            total = jnp.where(group_mask(lane, q), roll_lane(tile(main_ref, index), 8 * q), total)
        return total

    for p in range(2):
        for t in range(TG):
            put(zmsg_ref, TG * p + t, packed([SLOT * p + GROUPS * t + q for q in range(GROUPS)]))
    put(zmsg_ref, NE - 1, packed([SLOT * p + HALF + e for p in range(2) for e in range(NEXTRA)]))


YPAIRS = (2 * SLOT + NE + 1) // 2


def ymsg_kernel(main_ref, low_ref, high_ref, up_ref, down_ref, edge_ref):
    row, lane = iota_row(), iota_lane()
    edges = []
    for t in range(NE):
        edge = jnp.where((lane & 7) >= 4, tile(low_ref, t), tile(high_ref, t))
        put(edge_ref, t, edge)
        edges.append(edge)

    def source(index):
        if index < 2 * SLOT:
            return tile(main_ref, index)
        return edges[min(index - 2 * SLOT, NE - 1)]

    lower = row < 4
    for g in range(YPAIRS):
        first, second = source(2 * g), roll_row(source(2 * g + 1), 4)
        put(up_ref, g, jnp.where(lower, second, first))
        put(down_ref, g, jnp.where(lower, first, second))


A_SECOND = SLOT
A_EDGE = A_SECOND + HALF // 2 + 1
A_TILES = A_EDGE + 2 * NE
B_MY = HALF
B_EDGE = B_MY + HALF // 4
B_SECOND = B_EDGE + TG
B_TILES = B_SECOND + HALF


def xmsg_kernel(edge_ref, below_ref, above_ref, my_ref, ey_ref, to_left_ref, to_right_ref):
    row = iota_row()
    lower = row < 4
    keep_2 = (row < 2) | (row >= 6)
    for g in range(YPAIRS):
        below, above = tile(below_ref, g), tile(above_ref, g)
        pair = (jnp.where(lower, above, below), roll_row(jnp.where(lower, below, above), 4))
        for half in range(2):
            index = 2 * g + half
            if index < 2 * SLOT:
                put(my_ref, index, pair[half])
                p, i = divmod(index, SLOT)
                put((to_left_ref, to_right_ref)[p], i, pair[half])
                if i == SLOT - 1:
                    put((to_right_ref, to_left_ref)[p], A_SECOND + HALF // 2, pair[half])
            elif index < 2 * SLOT + NE:
                put(ey_ref, index - 2 * SLOT, pair[half])
                for ref in (to_left_ref, to_right_ref):
                    put(ref, A_EDGE + NE + index - 2 * SLOT, pair[half])
    for p, second in enumerate((to_right_ref, to_left_ref)):
        for i in range(HALF // 2):
            value = jnp.where(
                keep_2,
                tile(my_ref, SLOT * p + 2 * i),
                roll_row(tile(my_ref, SLOT * p + 2 * i + 1), 4),
            )
            put(second, A_SECOND + i, value)
    for t in range(NE):
        value = tile(edge_ref, t)
        put(to_left_ref, A_EDGE + t, value)
        put(to_right_ref, A_EDGE + t, value)


def part_places():
    row, lane = iota_row(), iota_lane()
    at_y, at_z = lax.axis_index("gy"), lax.axis_index("gz")
    y_main = at_y * 8 + row
    y_my = at_y * 8 + jnp.where(row < 4, row + 8, row - 8)
    z_main = at_z * 128 + lane
    z_edge = at_z * 128 + jnp.where(lane < 64, lane + 128, lane - 128)
    return ((y_main, z_main), (y_my, z_main), (y_main, z_edge), (y_my, z_edge))


def wells_kernel(sizes, cells_ref, rate_ref, wells_ref):
    size_x, size_y, size_z = sizes
    first_x = lax.axis_index("gx") - core() - 1
    for part, (y_at, z_at) in enumerate(part_places()):
        flats = [((first_x + s) * size_y + y_at) * size_z + z_at for s in range(4)]
        wells = [jnp.zeros((8, 128), jnp.float32)] * 4
        for w in range(cells_ref.shape[0]):
            for s in range(4):
                wells[s] = wells[s] + jnp.where(flats[s] == cells_ref[w], rate_ref[w], 0.0)
        for s in range(4):
            put(wells_ref, s * 4 + part, wells[s])


def plane_coefficients(sizes, wells_ref, conduct_ref, given_ref, coef_ref):
    row, lane = iota_row(), iota_lane()
    size_x, size_y, size_z = sizes
    first_x = lax.axis_index("gx") - core() - 1
    where = part_places()

    def shift_y(four, shift, mask):
        main, my = swap_shift(four[0], four[1], roll_row, shift, mask)
        edge, ey = swap_shift(four[2], four[3], roll_row, shift, mask)
        return [main, my, edge, ey]

    def shift_z(four, shift, mask):
        main, edge = swap_shift(four[0], four[2], roll_lane, shift, mask)
        my, ey = swap_shift(four[1], four[3], roll_lane, shift, mask)
        return [main, my, edge, ey]

    def plane(s, carry):
        center = [tile(conduct_ref, (s + 1) * 4 + part) for part in range(4)]
        before = [tile(conduct_ref, s * 4 + part) for part in range(4)]
        after = [tile(conduct_ref, (s + 2) * 4 + part) for part in range(4)]
        plus = [after, shift_y(center, -1, row == 7), shift_z(center, -1, lane == 127)]
        minus = [before, shift_y(center, 1, row == 0), shift_z(center, 1, lane == 0)]
        at_x = first_x + s
        x_inside = (at_x >= 0) & (at_x < size_x)
        for part, (y_at, z_at) in enumerate(where):
            inside = (y_at >= 0) & (y_at < size_y) & (z_at >= 0) & (z_at < size_z) & x_inside
            if part >= 2:
                inside = inside & ((lane < 4) | (lane >= 124))
            given = [tile(given_ref, (s * 4 + e) * 4 + part) for e in range(4)]
            diagonal = given[3] + tile(wells_ref, s * 4 + part)
            values = []
            for d in range(3):
                plus_face = 0.5 * (center[part] + plus[d][part])
                minus_face = 0.5 * (center[part] + minus[d][part])
                diagonal = diagonal + (given[d] + plus_face + minus_face)
                values += [(given[d] + plus_face) * (-1.0 / SCALE), minus_face * (-1.0 / SCALE)]
            for index, value in enumerate([(diagonal - SHIFT) * (1.0 / SCALE)] + values):
                value = jnp.where(inside, value, 0.0)
                if part >= 2:
                    for shift in (8, 16, 32, 64):
                        value = value + roll_lane(value, shift)
                put(coef_ref, (s * 7 + index) * 4 + part, value)
        return carry

    lax.fori_loop(0, 4, plane, 0)


def step(source, target, coef_ref, first, count, coef_shift, out_shift, with_my=True, with_em=True, with_ey=True):
    main_ref, my_ref, em_ref, ey_ref = source
    row, lane = iota_row(), iota_lane()
    row_0, row_7 = row == 0, row == 7
    lane_0, lane_127 = lane == 0, lane == 127

    def block(i, carry):
        s, t = first + lax.div(i, TG), lax.rem(i, TG)

        def apply(part, center, after, before, y_plus, y_minus, z_plus, z_minus):
            def coef(index):
                return tile(coef_ref, ((s + coef_shift) * 7 + index) * 4 + part)

            total = coef(0) * center + (coef(1) * after + coef(2) * before)
            total = total + (coef(3) * y_plus + coef(4) * y_minus)
            return total + (coef(5) * z_plus + coef(6) * z_minus)

        at_field, at_edge = s * HALF + t * GROUPS, s * TG + t
        out_field, out_edge = (s + out_shift) * HALF + t * GROUPS, (s + out_shift) * TG + t
        em = tile(em_ref, at_edge)
        ey = tile(ey_ref, at_edge) if with_em or with_my else None
        near_m = jnp.zeros((8, 128), jnp.float32)
        near_y = jnp.zeros((8, 128), jnp.float32)
        for q in range(GROUPS):
            f = at_field + q
            main, my = tile(main_ref, f), tile(my_ref, f)
            beside = roll_lane(em, -8 * q)
            z_plus = roll_lane(jnp.where(lane_0, beside, main), -1)
            z_minus = roll_lane(jnp.where(lane_127, beside, main), 1)
            y_plus, my_plus = swap_shift(main, my, roll_row, -1, row_7)
            y_minus, my_minus = swap_shift(main, my, roll_row, 1, row_0)
            after, before = tile(main_ref, f + HALF), tile(main_ref, f - HALF)
            put(target[0], out_field + q, apply(0, main, after, before, y_plus, y_minus, z_plus, z_minus))
            at = ((lane + (1 - 8 * q)) & 127) < 2
            if with_em:
                near_m = jnp.where(at, roll_lane(main, 8 * q), near_m)
            if with_ey:
                near_y = jnp.where(at, roll_lane(my, 8 * q), near_y)
            if with_my:
                beside = roll_lane(ey, -8 * q)
                z_plus = roll_lane(jnp.where(lane_0, beside, my), -1)
                z_minus = roll_lane(jnp.where(lane_127, beside, my), 1)
                after, before = tile(my_ref, f + HALF), tile(my_ref, f - HALF)
                put(target[1], out_field + q, apply(1, my, after, before, my_plus, my_minus, z_plus, z_minus))
        seven, zero = (lane & 7) == 7, (lane & 7) == 0
        if with_em:
            em_plus, ey_plus = swap_shift(em, ey, roll_row, -1, row_7)
            em_minus, ey_minus = swap_shift(em, ey, roll_row, 1, row_0)
            z_plus = jnp.where(seven, roll_lane(near_m, -1), roll_lane(em, -1))
            z_minus = jnp.where(zero, roll_lane(near_m, 1), roll_lane(em, 1))
            after, before = tile(em_ref, at_edge + TG), tile(em_ref, at_edge - TG)
            put(target[2], out_edge, apply(2, em, after, before, em_plus, em_minus, z_plus, z_minus))
        if with_ey:
            z_plus = jnp.where(seven, roll_lane(near_y, -1), roll_lane(ey, -1))
            z_minus = jnp.where(zero, roll_lane(near_y, 1), roll_lane(ey, 1))
            after, before = tile(ey_ref, at_edge + TG), tile(ey_ref, at_edge - TG)
            put(target[3], out_edge, apply(3, ey, after, before, ey_plus, ey_minus, z_plus, z_minus))
        return carry

    lax.fori_loop(0, count * TG, block, 0)


def copy_tiles(source, at, target, to, count):
    for i in range(count):
        put(target, to + i, tile(source, at + i))


def first_two_kernel(
    sizes,
    wells_ref,
    main_ref,
    edge_ref,
    my_ref,
    ey_ref,
    left_main_ref,
    right_main_ref,
    left_ref,
    right_ref,
    coef_ref,
    block_1_ref,
    block_2_ref,
    my_2_ref,
    em_2_ref,
    ey_2_ref,
    to_left_ref,
    to_right_ref,
    conduct_ref,
    given_ref,
    main_0,
    my_0,
    em_0,
    ey_0,
    main_1,
    my_1,
    em_1,
    ey_1,
):
    row = iota_row()
    for p in range(2):
        copy_tiles(main_ref, SLOT * p, main_0, HALF * (2 + p), HALF)
        copy_tiles(my_ref, SLOT * p, my_0, HALF * (2 + p), HALF)
        copy_tiles(edge_ref, TG * p, em_0, TG * (2 + p), TG)
        copy_tiles(ey_ref, TG * p, ey_0, TG * (2 + p), TG)
    extras = {2: (main_ref, HALF, my_ref, HALF, edge_ref, NE - 1, ey_ref, NE - 1, 0)}
    extras[3] = (main_ref, SLOT + HALF, my_ref, SLOT + HALF, edge_ref, NE - 1, ey_ref, NE - 1, NEXTRA)
    for whole, ref, adjacent, second, p in ((left_main_ref, left_ref, 1, 0, 1), (right_main_ref, right_ref, 4, 5, 0)):
        copy_tiles(whole, SLOT * p, main_0, HALF * adjacent, HALF)
        copy_tiles(whole, SLOT * (1 - p), main_0, HALF * second, HALF)
        copy_tiles(ref, 0, my_0, HALF * adjacent, HALF)
        for i in range(HALF // 2):
            value = tile(ref, A_SECOND + i)
            put(my_0, HALF * second + 2 * i, value)
            put(my_0, HALF * second + 2 * i + 1, roll_row(value, 4))
        for plane, at in ((adjacent, p), (second, 1 - p)):
            copy_tiles(ref, A_EDGE + TG * at, em_0, TG * plane, TG)
            copy_tiles(ref, A_EDGE + NE + TG * at, ey_0, TG * plane, TG)
        em_at, ey_at = A_EDGE + NE - 1, A_EDGE + 2 * NE - 1
        extras[adjacent] = (whole, SLOT * p + HALF, ref, HALF, ref, em_at, ref, ey_at, NEXTRA * p)
        for part, value in enumerate(
            (
                tile(whole, SLOT * (1 - p) + SLOT - 1),
                tile(ref, A_SECOND + HALF // 2),
                roll_lane(tile(ref, em_at), -8 * (NEXTRA * (1 - p) + 4)),
                roll_lane(tile(ref, ey_at), -8 * (NEXTRA * (1 - p) + 4)),
            )
        ):
            put(conduct_ref, 4 * second + part, value)
    for plane, (a, a_at, b, b_at, c, c_at, d, d_at, q) in extras.items():
        for e in range(NEXTRA):
            values = (
                tile(a, a_at + e),
                tile(b, b_at + e),
                roll_lane(tile(c, c_at), -8 * (q + e)),
                roll_lane(tile(d, d_at), -8 * (q + e)),
            )
            for part, value in enumerate(values):
                if e == NEXTRA - 1:
                    put(conduct_ref, 4 * plane + part, value)
                else:
                    put(given_ref, ((plane - 1) * 4 + e) * 4 + part, value)
    plane_coefficients(sizes, wells_ref, conduct_ref, given_ref, coef_ref)
    step((main_0, my_0, em_0, ey_0), (main_1, my_1, em_1, ey_1), coef_ref, 1, 4, -1, -1)
    copy_tiles(main_1, HALF, block_1_ref, 0, 2 * HALF)
    step((main_1, my_1, em_1, ey_1), (block_2_ref, my_2_ref, em_2_ref, ey_2_ref), coef_ref, 1, 2, 0, -1)
    for p, (adjacent, second) in enumerate(((to_left_ref, to_right_ref), (to_right_ref, to_left_ref))):
        for i in range(HALF):
            value = tile(block_2_ref, HALF * p + i)
            put(adjacent, i, value)
            put(second, B_SECOND + i, value)
        for i in range(HALF // 4):
            value = tile(my_2_ref, HALF * p + 4 * i)
            for k in range(1, 4):
                at_row = ((row + (1 - 2 * k)) & 7) < 2
                value = jnp.where(at_row, roll_row(tile(my_2_ref, HALF * p + 4 * i + k), 2 * k), value)
            put(adjacent, B_MY + i, value)
        copy_tiles(em_2_ref, TG * p, adjacent, B_EDGE, TG)


def last_two_kernel(
    coef_ref,
    block_1_ref,
    block_2_ref,
    my_2_ref,
    em_2_ref,
    ey_2_ref,
    left_ref,
    right_ref,
    keep_ref,
    send_ref,
    main_2,
    my_2,
    em_2,
    ey_2,
    main_3,
    my_3,
    em_3,
    main_4,
):
    copy_tiles(block_2_ref, 0, main_2, 2 * HALF, 2 * HALF)
    copy_tiles(my_2_ref, 0, my_2, 2 * HALF, 2 * HALF)
    copy_tiles(em_2_ref, 0, em_2, 2 * TG, 2 * TG)
    copy_tiles(ey_2_ref, 0, ey_2, 2 * TG, 2 * TG)
    for ref, adjacent, second in ((left_ref, 1, 0), (right_ref, 4, 5)):
        copy_tiles(ref, 0, main_2, HALF * adjacent, HALF)
        for i in range(HALF // 4):
            value = tile(ref, B_MY + i)
            for k in range(4):
                put(my_2, HALF * adjacent + 4 * i + k, roll_row(value, -2 * k))
        copy_tiles(ref, B_EDGE, em_2, TG * adjacent, TG)
        copy_tiles(ref, B_SECOND, main_2, HALF * second, HALF)
    source, target = (main_2, my_2, em_2, ey_2), (main_3, my_3, em_3, None)
    for plane in (1, 4):
        step(source, target, coef_ref, plane, 1, -1, -1, False, False, False)
    step(source, target, coef_ref, 2, 2, -1, -1, True, True, False)
    step((main_3, my_3, em_3, None), (main_4, None, None, None), coef_ref, 1, 2, 0, -1, False, False, False)
    mine, other = core() * HALF, (1 - core()) * HALF
    for level, (ref, base) in enumerate(((block_1_ref, 0), (block_2_ref, 0), (main_3, HALF), (main_4, 0))):
        for i in range(HALF):
            put(keep_ref, HALF * level + i, tile(ref, base + mine + i))
            put(send_ref, HALF * level + i, tile(ref, base + other + i))


PAIRS = (
    ((0, 0), (0, 1)),
    ((0, 2), (0, 3)),
    ((1, 1), (1, 2)),
    ((1, 3), (1, 4)),
    ((2, 2), (2, 3)),
    ((3, 3), (3, 4)),
    ((4, 4), (2, 4)),
    ((0, 4), None),
)


def two_parts(values):
    high = values.astype(jnp.bfloat16)
    return high, (values - high.astype(jnp.float32)).astype(jnp.bfloat16)


def three_products(first, second, dims):
    def dot(a, b):
        return lax.dot_general(a, b, (dims, ((), ())), preferred_element_type=jnp.float32)

    return dot(first[0], second[0]) + (dot(first[0], second[1]) + dot(first[1], second[0]))


def dot_tn(first, second):
    return lax.dot_general(first, second, (((0,), (0,)), ((), ())), precision=HI, preferred_element_type=jnp.float32)


def dot_nn(first, second):
    return lax.dot_general(first, second, (((1,), (0,)), ((), ())), precision=HI, preferred_element_type=jnp.float32)


def gram_kernel(block_0, keep_ref, got_ref, high_ref, low_ref, gram_ref, basis_ref):
    mine, other = core() * HALF, (1 - core()) * HALF
    for y in range(8):
        lanes = slice(128 * y, 128 * (y + 1))
        basis_ref[0:M, lanes] = block_0[pl.ds(y, M, stride=8), :]
        for level in range(1, LEVELS):
            at = pl.ds(8 * HALF * (level - 1) + y, HALF, stride=8)
            basis_ref[pl.ds(pl.multiple_of(M * level + mine, 8), HALF), lanes] = keep_ref[at, :]
            basis_ref[pl.ds(pl.multiple_of(M * level + other, 8), HALF), lanes] = got_ref[at, :]
    parts = two_parts(basis_ref[...])
    high_ref[...], low_ref[...] = parts
    full = three_products(parts, parts, ((1,), (1,)))
    for index, pair in enumerate(PAIRS):
        for half, at in enumerate(pair):
            if at is None:
                value = jnp.zeros((M, M), jnp.float32)
            else:
                value = full[M * at[0] : M * at[0] + M, M * at[1] : M * at[1] + M]
            gram_ref[M * index : M * (index + 1), M * half : M * (half + 1)] = value


def eliminate(matrix, wanted):
    both = jnp.concatenate([matrix, wanted], axis=1)
    tiles = [both[8 * i : 8 * i + 8, :] for i in range(M // 8)]
    rows = iota_row()

    def column(value, at):
        return jnp.broadcast_to(value[:, at : at + 1], (8, 128))

    for i in range(M // 8):
        columns = [[column(t, 8 * i + b) for b in range(8)] for t in tiles]
        row = [jnp.broadcast_to(tiles[i][a : a + 1, :], (8, 128)) for a in range(8)]
        small = [
            [jnp.broadcast_to(columns[i][b][a : a + 1, :], (8, 128)) for b in range(8)]
            for a in range(8)
        ]
        for p in range(8):
            inverse = 1.0 / small[p][p]
            for a in range(p + 1, 8):
                factor = small[a][p] * inverse
                row[a] = row[a] - factor * row[p]
                for b in range(p + 1, 8):
                    small[a][b] = small[a][b] - factor * small[p][b]
            row[p] = row[p] * inverse
            for b in range(p + 1, 8):
                small[p][b] = small[p][b] * inverse
        for p in range(7, 0, -1):
            for a in range(p):
                row[a] = row[a] - small[a][p] * row[p]
        for j in range(M // 8):
            if j == i:
                value = row[0]
                for b in range(1, 8):
                    value = jnp.where(rows == b, row[b], value)
            else:
                value = tiles[j]
                for b in range(8):
                    value = value - columns[j][b] * row[b]
            tiles[j] = value
    return jnp.concatenate(tiles, axis=0)[:, M:]


def apply_levels(blocks):
    out = [SHIFT * b for b in blocks] + [None]
    for j, b in enumerate(blocks):
        out[j + 1] = SCALE * b if out[j + 1] is None else out[j + 1] + SCALE * b
    return out


def pad_levels(blocks, count):
    return list(blocks) + [jnp.zeros((M, M), jnp.float32)] * (count - len(blocks))


def final_kernel(gram_ref, high_ref, low_ref, field_ref, resid_ref, full_ref):
    for index, pair in enumerate(PAIRS):
        for half, at in enumerate(pair):
            if at is None:
                continue
            value = gram_ref[M * index : M * (index + 1), M * half : M * (half + 1)]
            full_ref[M * at[0] : M * at[0] + M, M * at[1] : M * at[1] + M] = value
            if at[0] != at[1]:
                full_ref[M * at[1] : M * at[1] + M, M * at[0] : M * at[0] + M] = value.T
    eye = jnp.where(
        lax.broadcasted_iota(jnp.int32, (M, M), 0) == lax.broadcasted_iota(jnp.int32, (M, M), 1), 1.0, 0.0
    ).astype(jnp.float32)

    def gram(levels, blocks):
        count = M * levels
        return dot_nn(full_ref[0:count, 0 : M * len(blocks)], jnp.concatenate(blocks, axis=0))

    def minimal(half, second):
        levels = len(second)
        product = gram(levels, second)
        cross = sum(product[M * j : M * j + M] * b for j, b in enumerate(half))
        square = sum(product[M * j : M * j + M] * b for j, b in enumerate(second))
        def total(values):
            return jnp.sum(jnp.sum(values, axis=0, keepdims=True), axis=1, keepdims=True)

        return total(cross) / total(square), product[0:M]

    image_gram = SHIFT * full_ref[0:M, 0:M] + SCALE * full_ref[0:M, M : 2 * M]
    inverse = eliminate(dot_tn(image_gram, image_gram), image_gram.T)
    alpha = dot_nn(inverse, full_ref[0:M, 0:M])
    half = [eye - SHIFT * alpha, -SCALE * alpha]
    second = apply_levels(half)
    omega, second_gram = minimal(half, second)
    field = [alpha + omega * half[0], omega * half[1]]
    resid = [half[0] - omega * second[0], half[1] - omega * second[1], -omega * second[2]]
    beta = -dot_nn(inverse, second_gram)
    direct = [
        resid[0] + (1.0 - omega * SHIFT) * beta,
        resid[1] - (omega * SCALE) * beta,
        resid[2],
    ]
    image = apply_levels(direct)
    stacked = jnp.concatenate(
        [jnp.concatenate(image, axis=0), jnp.concatenate(pad_levels(resid, 4), axis=0)], axis=1
    )
    both = dot_nn(full_ref[0:M, 0 : 4 * M], stacked)
    image_gram, resid_gram = both[:, 0:M], both[:, M:]
    inverse = eliminate(dot_tn(image_gram, image_gram), image_gram.T)
    alpha = dot_nn(inverse, resid_gram)
    product = dot_nn(jnp.concatenate(image + direct, axis=0), alpha)
    half = [r - product[M * j : M * j + M] for j, r in enumerate(pad_levels(resid, 4))]
    second = apply_levels(half)
    omega, _ = minimal(half, second)
    field = pad_levels(field, 4)
    moved = [product[M * (4 + j) : M * (5 + j)] for j in range(3)] + [None]
    field = [
        f + omega * h + (0.0 if m is None else m) for f, h, m in zip(field, half, moved)
    ]
    field = pad_levels(field, 5)
    resid = [h - omega * s for h, s in zip(pad_levels(half, 5), second)]
    coefs = jnp.concatenate([jnp.concatenate(field, axis=0), jnp.concatenate(resid, axis=0)], axis=1)
    result = three_products(two_parts(coefs.T), (high_ref[...], low_ref[...]), ((1,), (0,)))
    for y in range(8):
        field_ref[pl.ds(y, M, stride=8), :] = result[0:M, 128 * y : 128 * (y + 1)]
        resid_ref[pl.ds(y, M, stride=8), :] = result[M:, 128 * y : 128 * (y + 1)]


VMEM = pl.BlockSpec(memory_space=pltpu.VMEM)
SMEM = pl.BlockSpec(memory_space=pltpu.SMEM)


def f32(*shape):
    return jax.ShapeDtypeStruct(shape, jnp.float32)


def call(kernel, name, outs, specs, scratch=()):
    return pl.pallas_call(
        kernel,
        name=name,
        out_shape=outs,
        in_specs=specs,
        out_specs=tuple(VMEM for _ in outs) if isinstance(outs, tuple) else VMEM,
        scratch_shapes=list(scratch),
        compiler_params=pltpu.CompilerParams(vmem_limit_bytes=32 * 1024 * 1024),
    )


def from_sides(axis, up, down, by=1):
    count = lax.axis_size(axis)
    lower = lax.ppermute(up, axis, [(i, i + by) for i in range(count - by)])
    upper = lax.ppermute(down, axis, [(i + by, i) for i in range(count - by)])
    return lower, upper


def spread(values, axes):
    count = lax.axis_size(axes)
    return lax.all_to_all(jnp.broadcast_to(values, (count, *values.shape)), axes, 0, 0)


def in_hbm(values):
    return pltpu.with_memory_space_constraint(values, pltpu.HBM)


def other_core(values):
    count = lax.axis_size("gx")
    return lax.ppermute(values, "gx", [(i, i ^ 1) for i in range(count)])


def tiles(count):
    return f32(8 * count, 128)


def scratch(*counts):
    return [pltpu.VMEM((8 * count, 128), jnp.float32) for count in counts]


def per_device(right_side, velocity, decay_rate, perm_class, conductivity, well_cells, well_rate):
    sizes = (lax.axis_size("gx"), 8 * lax.axis_size("gy"), 128 * lax.axis_size("gz"))
    block_0 = right_side.reshape(8 * M, 128)
    any_space = pl.BlockSpec(memory_space=pltpu.HBM)

    send, keep = call(
        pack_kernel,
        "pack",
        (tiles(SLOT), tiles(SLOT)),
        [any_space] * 5,
        [
            pltpu.VMEM((8, 128), jnp.int32),
            pltpu.SMEM(conductivity.shape, jnp.float32),
            pltpu.SemaphoreType.DMA((6,)),
        ],
    )(
        in_hbm(block_0),
        in_hbm(velocity.reshape(24, 128)),
        in_hbm(decay_rate.reshape(8, 128)),
        in_hbm(perm_class.reshape(8, 128)),
        in_hbm(conductivity),
    )
    got = other_core(send)
    wells = call(functools.partial(wells_kernel, sizes), "wells", tiles(16), [SMEM, SMEM])(well_cells, well_rate)
    main, zmsg = call(zmsg_kernel, "zmsg", (tiles(2 * SLOT), tiles(NE)), [VMEM] * 2)(keep, got)
    left_main, right_main = from_sides("gx", main, main, 2)
    low, high = from_sides("gz", zmsg, zmsg)
    up, down, edge = call(ymsg_kernel, "ymsg", (tiles(YPAIRS), tiles(YPAIRS), tiles(NE)), [VMEM] * 3)(
        main, low, high
    )
    below, above = from_sides("gy", up, down)
    my, ey, to_left, to_right = call(
        xmsg_kernel, "xmsg", (tiles(2 * SLOT), tiles(NE), tiles(A_TILES), tiles(A_TILES)), [VMEM] * 3
    )(edge, below, above)
    left, right = from_sides("gx", to_right, to_left, 2)
    coef, block_1, block_2, my, em, ey, to_left, to_right = call(
        functools.partial(first_two_kernel, sizes),
        "first_two",
        (
            tiles(4 * 28),
            tiles(M),
            tiles(M),
            tiles(M),
            tiles(2 * TG),
            tiles(2 * TG),
            tiles(B_TILES),
            tiles(B_TILES),
        ),
        [VMEM] * 9,
        scratch(24, 64, 6 * HALF, 6 * HALF, 6 * TG, 6 * TG, 4 * HALF, 4 * HALF, 4 * TG, 4 * TG),
    )(wells, main, edge, my, ey, left_main, right_main, left, right)
    left, right = from_sides("gx", to_right, to_left, 2)
    keep, send = call(
        last_two_kernel,
        "last_two",
        (tiles(4 * HALF), tiles(4 * HALF)),
        [VMEM] * 8,
        scratch(6 * HALF, 6 * HALF, 6 * TG, 6 * TG, 4 * HALF, 4 * HALF, 4 * TG, 2 * HALF),
    )(coef, block_1, block_2, my, em, ey, left, right)
    got = other_core(send)
    part = jax.ShapeDtypeStruct((LEVELS * M, 1024), jnp.bfloat16)
    high, low, gram = call(
        gram_kernel,
        "gram",
        (part, part, f32(8 * M, 128)),
        [VMEM] * 3,
        [pltpu.VMEM((LEVELS * M, 1024), jnp.float32)],
    )(block_0, keep, got)

    plane = ("gz", "gy")
    count = lax.axis_size(plane)
    gram = lax.all_to_all(gram.reshape(count, -1, 128), plane, 0, 0)
    gram = jnp.sum(gram, axis=0)
    gram = jnp.sum(spread(gram, "gx"), axis=0)
    gram = spread(gram, plane).reshape(8 * M, 128)
    field, resid = call(
        final_kernel,
        "final",
        (f32(8 * M, 128), f32(8 * M, 128)),
        [VMEM] * 3,
        [pltpu.VMEM((LEVELS * M, LEVELS * M), jnp.float32)],
    )(gram, high, low)
    return field.reshape(right_side.shape), resid.reshape(right_side.shape)


def solution(mesh):
    placed = (
        P(None, "gx", "gy", "gz"),
        P(None, "gx", "gy", "gz"),
        P("gx", "gy", "gz"),
        P("gx", "gy", "gz"),
        P(),
        P(),
        P(),
    )
    return jax.shard_map(
        per_device,
        mesh=mesh,
        in_specs=placed,
        out_specs=(P(None, "gx", "gy", "gz"), P(None, "gx", "gy", "gz")),
        check_vma=False,
    )
```

```python
import functools

import jax
import jax.numpy as jnp
from jax import lax
from jax.experimental import pallas as pl
from jax.experimental.pallas import tpu as pltpu
from jax.sharding import PartitionSpec as P

SHIFT = 7.5
SCALE = 3.0
LEVELS = 5
M = 64
HALF = M // 2
NEXTRA = 5
SLOT = HALF + NEXTRA
GROUPS = 16
TG = HALF // GROUPS
NE = 2 * TG + 1
HI = lax.Precision.HIGHEST


def iota_row():
    return lax.broadcasted_iota(jnp.int32, (8, 128), 0)


def iota_lane():
    return lax.broadcasted_iota(jnp.int32, (8, 128), 1)


def roll_lane(tile, shift):
    shift = shift % 128
    return tile if shift == 0 else pltpu.roll(tile, shift, 1)


def roll_row(tile, shift):
    shift = shift % 8
    return tile if shift == 0 else pltpu.roll(tile, shift, 0)


def swap_shift(first, second, roll, shift, mask):
    first, second = roll(first, shift), roll(second, shift)
    return jnp.where(mask, second, first), jnp.where(mask, first, second)


def tile(ref, index):
    if isinstance(index, int):
        return ref[8 * index : 8 * index + 8, :]
    return ref[pl.ds(pl.multiple_of(index * 8, 8), 8), :]


def put(ref, index, value):
    if isinstance(index, int):
        ref[8 * index : 8 * index + 8, :] = value
    else:
        ref[pl.ds(pl.multiple_of(index * 8, 8), 8), :] = value


def group_mask(lane, q):
    at = (lane + (4 - 8 * q)) & 127
    return at < 8


def core():
    return lax.rem(lax.axis_index("gx"), 2)


def pack_kernel(right_hbm, vel_hbm, decay_hbm, class_hbm, table_hbm, send_ref, keep_ref, class_ref, table_ref, sems):
    mine = pl.multiple_of(core() * 8 * HALF, 8)
    other = pl.multiple_of((1 - core()) * 8 * HALF, 8)
    copies = [
        (class_hbm, class_ref),
        (table_hbm, table_ref),
        (vel_hbm, keep_ref.at[pl.ds(8 * HALF, 24), :]),
        (decay_hbm, keep_ref.at[pl.ds(8 * (HALF + 3), 8), :]),
        (right_hbm.at[pl.ds(mine, 8 * HALF), :], keep_ref.at[pl.ds(0, 8 * HALF), :]),
        (right_hbm.at[pl.ds(other, 8 * HALF), :], send_ref.at[pl.ds(0, 8 * HALF), :]),
    ]
    copies = [pltpu.make_async_copy(src, dst, sems.at[i]) for i, (src, dst) in enumerate(copies)]
    for copy in copies:
        copy.start()
    for copy in copies:
        copy.wait()
    classes = class_ref[...]
    conduct = jnp.zeros((8, 128), jnp.float32)
    for index in range(table_ref.shape[0]):
        conduct = jnp.where(classes == index, table_ref[index], conduct)
    put(keep_ref, HALF + 4, conduct)
    put(send_ref, HALF + 4, conduct)
    for e in range(4):
        put(send_ref, HALF + e, tile(keep_ref, HALF + e))


def zmsg_kernel(keep_ref, got_ref, main_ref, zmsg_ref):
    lane = iota_lane()
    mine, other = core() * SLOT, (1 - core()) * SLOT
    for i in range(SLOT):
        put(main_ref, mine + i, tile(keep_ref, i))
        put(main_ref, other + i, tile(got_ref, i))

    def packed(indices):
        total = jnp.zeros((8, 128), jnp.float32)
        for q, index in enumerate(indices):
            total = jnp.where(group_mask(lane, q), roll_lane(tile(main_ref, index), 8 * q), total)
        return total

    for p in range(2):
        for t in range(TG):
            put(zmsg_ref, TG * p + t, packed([SLOT * p + GROUPS * t + q for q in range(GROUPS)]))
    put(zmsg_ref, NE - 1, packed([SLOT * p + HALF + e for p in range(2) for e in range(NEXTRA)]))


YPAIRS = (2 * SLOT + NE + 1) // 2


def ymsg_kernel(main_ref, low_ref, high_ref, up_ref, down_ref, edge_ref):
    row, lane = iota_row(), iota_lane()
    edges = []
    for t in range(NE):
        edge = jnp.where((lane & 7) >= 4, tile(low_ref, t), tile(high_ref, t))
        put(edge_ref, t, edge)
        edges.append(edge)

    def source(index):
        if index < 2 * SLOT:
            return tile(main_ref, index)
        return edges[min(index - 2 * SLOT, NE - 1)]

    lower = row < 4
    for g in range(YPAIRS):
        first, second = source(2 * g), roll_row(source(2 * g + 1), 4)
        put(up_ref, g, jnp.where(lower, second, first))
        put(down_ref, g, jnp.where(lower, first, second))


A_SECOND = SLOT
A_EDGE = A_SECOND + HALF // 2 + 1
A_TILES = A_EDGE + 2 * NE
B_MY = HALF
B_EDGE = B_MY + HALF // 4
B_SECOND = B_EDGE + TG
B_TILES = B_SECOND + HALF


def xmsg_kernel(edge_ref, below_ref, above_ref, my_ref, ey_ref, to_left_ref, to_right_ref):
    row = iota_row()
    lower = row < 4
    keep_2 = (row < 2) | (row >= 6)
    for g in range(YPAIRS):
        below, above = tile(below_ref, g), tile(above_ref, g)
        pair = (jnp.where(lower, above, below), roll_row(jnp.where(lower, below, above), 4))
        for half in range(2):
            index = 2 * g + half
            if index < 2 * SLOT:
                put(my_ref, index, pair[half])
                p, i = divmod(index, SLOT)
                put((to_left_ref, to_right_ref)[p], i, pair[half])
                if i == SLOT - 1:
                    put((to_right_ref, to_left_ref)[p], A_SECOND + HALF // 2, pair[half])
            elif index < 2 * SLOT + NE:
                put(ey_ref, index - 2 * SLOT, pair[half])
                for ref in (to_left_ref, to_right_ref):
                    put(ref, A_EDGE + NE + index - 2 * SLOT, pair[half])
    for p, second in enumerate((to_right_ref, to_left_ref)):
        for i in range(HALF // 2):
            value = jnp.where(
                keep_2,
                tile(my_ref, SLOT * p + 2 * i),
                roll_row(tile(my_ref, SLOT * p + 2 * i + 1), 4),
            )
            put(second, A_SECOND + i, value)
    for t in range(NE):
        value = tile(edge_ref, t)
        put(to_left_ref, A_EDGE + t, value)
        put(to_right_ref, A_EDGE + t, value)


def part_places():
    row, lane = iota_row(), iota_lane()
    at_y, at_z = lax.axis_index("gy"), lax.axis_index("gz")
    y_main = at_y * 8 + row
    y_my = at_y * 8 + jnp.where(row < 4, row + 8, row - 8)
    z_main = at_z * 128 + lane
    z_edge = at_z * 128 + jnp.where(lane < 64, lane + 128, lane - 128)
    return ((y_main, z_main), (y_my, z_main), (y_main, z_edge), (y_my, z_edge))


def wells_kernel(sizes, cells_ref, rate_ref, wells_ref):
    size_x, size_y, size_z = sizes
    first_x = lax.axis_index("gx") - core() - 1
    for part, (y_at, z_at) in enumerate(part_places()):
        flats = [((first_x + s) * size_y + y_at) * size_z + z_at for s in range(4)]
        wells = [jnp.zeros((8, 128), jnp.float32)] * 4
        for w in range(cells_ref.shape[0]):
            for s in range(4):
                wells[s] = wells[s] + jnp.where(flats[s] == cells_ref[w], rate_ref[w], 0.0)
        for s in range(4):
            put(wells_ref, s * 4 + part, wells[s])


def plane_coefficients(sizes, wells_ref, conduct_ref, given_ref, coef_ref):
    row, lane = iota_row(), iota_lane()
    size_x, size_y, size_z = sizes
    first_x = lax.axis_index("gx") - core() - 1
    where = part_places()

    def shift_y(four, shift, mask):
        main, my = swap_shift(four[0], four[1], roll_row, shift, mask)
        edge, ey = swap_shift(four[2], four[3], roll_row, shift, mask)
        return [main, my, edge, ey]

    def shift_z(four, shift, mask):
        main, edge = swap_shift(four[0], four[2], roll_lane, shift, mask)
        my, ey = swap_shift(four[1], four[3], roll_lane, shift, mask)
        return [main, my, edge, ey]

    def plane(s, carry):
        center = [tile(conduct_ref, (s + 1) * 4 + part) for part in range(4)]
        before = [tile(conduct_ref, s * 4 + part) for part in range(4)]
        after = [tile(conduct_ref, (s + 2) * 4 + part) for part in range(4)]
        plus = [after, shift_y(center, -1, row == 7), shift_z(center, -1, lane == 127)]
        minus = [before, shift_y(center, 1, row == 0), shift_z(center, 1, lane == 0)]
        at_x = first_x + s
        x_inside = (at_x >= 0) & (at_x < size_x)
        for part, (y_at, z_at) in enumerate(where):
            inside = (y_at >= 0) & (y_at < size_y) & (z_at >= 0) & (z_at < size_z) & x_inside
            if part >= 2:
                inside = inside & ((lane < 4) | (lane >= 124))
            given = [tile(given_ref, (s * 4 + e) * 4 + part) for e in range(4)]
            diagonal = given[3] + tile(wells_ref, s * 4 + part)
            values = []
            for d in range(3):
                plus_face = 0.5 * (center[part] + plus[d][part])
                minus_face = 0.5 * (center[part] + minus[d][part])
                diagonal = diagonal + (given[d] + plus_face + minus_face)
                values += [(given[d] + plus_face) * (-1.0 / SCALE), minus_face * (-1.0 / SCALE)]
            for index, value in enumerate([(diagonal - SHIFT) * (1.0 / SCALE)] + values):
                value = jnp.where(inside, value, 0.0)
                if part >= 2:
                    for shift in (8, 16, 32, 64):
                        value = value + roll_lane(value, shift)
                put(coef_ref, (s * 7 + index) * 4 + part, value)
        return carry

    lax.fori_loop(0, 4, plane, 0, unroll=True)


def step(source, target, coef_ref, first, count, coef_shift, out_shift, with_my=True, with_em=True, with_ey=True):
    main_ref, my_ref, em_ref, ey_ref = source
    row, lane = iota_row(), iota_lane()
    row_0, row_7 = row == 0, row == 7
    lane_0, lane_127 = lane == 0, lane == 127

    def block(i, carry):
        s, t = first + lax.div(i, TG), lax.rem(i, TG)

        def apply(part, center, after, before, y_plus, y_minus, z_plus, z_minus):
            def coef(index):
                return tile(coef_ref, ((s + coef_shift) * 7 + index) * 4 + part)

            total = coef(0) * center + (coef(1) * after + coef(2) * before)
            total = total + (coef(3) * y_plus + coef(4) * y_minus)
            return total + (coef(5) * z_plus + coef(6) * z_minus)

        at_field, at_edge = s * HALF + t * GROUPS, s * TG + t
        out_field, out_edge = (s + out_shift) * HALF + t * GROUPS, (s + out_shift) * TG + t
        em = tile(em_ref, at_edge)
        ey = tile(ey_ref, at_edge) if with_em or with_my else None
        near_m = jnp.zeros((8, 128), jnp.float32)
        near_y = jnp.zeros((8, 128), jnp.float32)
        for q in range(GROUPS):
            f = at_field + q
            main, my = tile(main_ref, f), tile(my_ref, f)
            beside = roll_lane(em, -8 * q)
            z_plus = roll_lane(jnp.where(lane_0, beside, main), -1)
            z_minus = roll_lane(jnp.where(lane_127, beside, main), 1)
            y_plus, my_plus = swap_shift(main, my, roll_row, -1, row_7)
            y_minus, my_minus = swap_shift(main, my, roll_row, 1, row_0)
            after, before = tile(main_ref, f + HALF), tile(main_ref, f - HALF)
            put(target[0], out_field + q, apply(0, main, after, before, y_plus, y_minus, z_plus, z_minus))
            at = ((lane + (1 - 8 * q)) & 127) < 2
            if with_em:
                near_m = jnp.where(at, roll_lane(main, 8 * q), near_m)
            if with_ey:
                near_y = jnp.where(at, roll_lane(my, 8 * q), near_y)
            if with_my:
                beside = roll_lane(ey, -8 * q)
                z_plus = roll_lane(jnp.where(lane_0, beside, my), -1)
                z_minus = roll_lane(jnp.where(lane_127, beside, my), 1)
                after, before = tile(my_ref, f + HALF), tile(my_ref, f - HALF)
                put(target[1], out_field + q, apply(1, my, after, before, my_plus, my_minus, z_plus, z_minus))
        seven, zero = (lane & 7) == 7, (lane & 7) == 0
        if with_em:
            em_plus, ey_plus = swap_shift(em, ey, roll_row, -1, row_7)
            em_minus, ey_minus = swap_shift(em, ey, roll_row, 1, row_0)
            z_plus = jnp.where(seven, roll_lane(near_m, -1), roll_lane(em, -1))
            z_minus = jnp.where(zero, roll_lane(near_m, 1), roll_lane(em, 1))
            after, before = tile(em_ref, at_edge + TG), tile(em_ref, at_edge - TG)
            put(target[2], out_edge, apply(2, em, after, before, em_plus, em_minus, z_plus, z_minus))
        if with_ey:
            z_plus = jnp.where(seven, roll_lane(near_y, -1), roll_lane(ey, -1))
            z_minus = jnp.where(zero, roll_lane(near_y, 1), roll_lane(ey, 1))
            after, before = tile(ey_ref, at_edge + TG), tile(ey_ref, at_edge - TG)
            put(target[3], out_edge, apply(3, ey, after, before, ey_plus, ey_minus, z_plus, z_minus))
        return carry

    lax.fori_loop(0, count * TG, block, 0)


def copy_tiles(source, at, target, to, count):
    for i in range(count):
        put(target, to + i, tile(source, at + i))


def first_two_kernel(
    sizes,
    wells_ref,
    main_ref,
    edge_ref,
    my_ref,
    ey_ref,
    left_main_ref,
    right_main_ref,
    left_ref,
    right_ref,
    coef_ref,
    block_1_ref,
    block_2_ref,
    my_2_ref,
    em_2_ref,
    ey_2_ref,
    to_left_ref,
    to_right_ref,
    conduct_ref,
    given_ref,
    main_0,
    my_0,
    em_0,
    ey_0,
    main_1,
    my_1,
    em_1,
    ey_1,
):
    row = iota_row()
    for p in range(2):
        copy_tiles(main_ref, SLOT * p, main_0, HALF * (2 + p), HALF)
        copy_tiles(my_ref, SLOT * p, my_0, HALF * (2 + p), HALF)
        copy_tiles(edge_ref, TG * p, em_0, TG * (2 + p), TG)
        copy_tiles(ey_ref, TG * p, ey_0, TG * (2 + p), TG)
    extras = {2: (main_ref, HALF, my_ref, HALF, edge_ref, NE - 1, ey_ref, NE - 1, 0)}
    extras[3] = (main_ref, SLOT + HALF, my_ref, SLOT + HALF, edge_ref, NE - 1, ey_ref, NE - 1, NEXTRA)
    for whole, ref, adjacent, second, p in ((left_main_ref, left_ref, 1, 0, 1), (right_main_ref, right_ref, 4, 5, 0)):
        copy_tiles(whole, SLOT * p, main_0, HALF * adjacent, HALF)
        copy_tiles(whole, SLOT * (1 - p), main_0, HALF * second, HALF)
        copy_tiles(ref, 0, my_0, HALF * adjacent, HALF)
        for i in range(HALF // 2):
            value = tile(ref, A_SECOND + i)
            put(my_0, HALF * second + 2 * i, value)
            put(my_0, HALF * second + 2 * i + 1, roll_row(value, 4))
        for plane, at in ((adjacent, p), (second, 1 - p)):
            copy_tiles(ref, A_EDGE + TG * at, em_0, TG * plane, TG)
            copy_tiles(ref, A_EDGE + NE + TG * at, ey_0, TG * plane, TG)
        em_at, ey_at = A_EDGE + NE - 1, A_EDGE + 2 * NE - 1
        extras[adjacent] = (whole, SLOT * p + HALF, ref, HALF, ref, em_at, ref, ey_at, NEXTRA * p)
        for part, value in enumerate(
            (
                tile(whole, SLOT * (1 - p) + SLOT - 1),
                tile(ref, A_SECOND + HALF // 2),
                roll_lane(tile(ref, em_at), -8 * (NEXTRA * (1 - p) + 4)),
                roll_lane(tile(ref, ey_at), -8 * (NEXTRA * (1 - p) + 4)),
            )
        ):
            put(conduct_ref, 4 * second + part, value)
    for plane, (a, a_at, b, b_at, c, c_at, d, d_at, q) in extras.items():
        for e in range(NEXTRA):
            values = (
                tile(a, a_at + e),
                tile(b, b_at + e),
                roll_lane(tile(c, c_at), -8 * (q + e)),
                roll_lane(tile(d, d_at), -8 * (q + e)),
            )
            for part, value in enumerate(values):
                if e == NEXTRA - 1:
                    put(conduct_ref, 4 * plane + part, value)
                else:
                    put(given_ref, ((plane - 1) * 4 + e) * 4 + part, value)
    plane_coefficients(sizes, wells_ref, conduct_ref, given_ref, coef_ref)
    step((main_0, my_0, em_0, ey_0), (main_1, my_1, em_1, ey_1), coef_ref, 1, 4, -1, -1)
    copy_tiles(main_1, HALF, block_1_ref, 0, 2 * HALF)
    step((main_1, my_1, em_1, ey_1), (block_2_ref, my_2_ref, em_2_ref, ey_2_ref), coef_ref, 1, 2, 0, -1)
    for p, (adjacent, second) in enumerate(((to_left_ref, to_right_ref), (to_right_ref, to_left_ref))):
        for i in range(HALF):
            value = tile(block_2_ref, HALF * p + i)
            put(adjacent, i, value)
            put(second, B_SECOND + i, value)
        for i in range(HALF // 4):
            value = tile(my_2_ref, HALF * p + 4 * i)
            for k in range(1, 4):
                at_row = ((row + (1 - 2 * k)) & 7) < 2
                value = jnp.where(at_row, roll_row(tile(my_2_ref, HALF * p + 4 * i + k), 2 * k), value)
            put(adjacent, B_MY + i, value)
        copy_tiles(em_2_ref, TG * p, adjacent, B_EDGE, TG)


def last_two_kernel(
    coef_ref,
    block_1_ref,
    block_2_ref,
    my_2_ref,
    em_2_ref,
    ey_2_ref,
    left_ref,
    right_ref,
    keep_ref,
    send_ref,
    main_2,
    my_2,
    em_2,
    ey_2,
    main_3,
    my_3,
    em_3,
    main_4,
):
    copy_tiles(block_2_ref, 0, main_2, 2 * HALF, 2 * HALF)
    copy_tiles(my_2_ref, 0, my_2, 2 * HALF, 2 * HALF)
    copy_tiles(em_2_ref, 0, em_2, 2 * TG, 2 * TG)
    copy_tiles(ey_2_ref, 0, ey_2, 2 * TG, 2 * TG)
    for ref, adjacent, second in ((left_ref, 1, 0), (right_ref, 4, 5)):
        copy_tiles(ref, 0, main_2, HALF * adjacent, HALF)
        for i in range(HALF // 4):
            value = tile(ref, B_MY + i)
            for k in range(4):
                put(my_2, HALF * adjacent + 4 * i + k, roll_row(value, -2 * k))
        copy_tiles(ref, B_EDGE, em_2, TG * adjacent, TG)
        copy_tiles(ref, B_SECOND, main_2, HALF * second, HALF)
    source, target = (main_2, my_2, em_2, ey_2), (main_3, my_3, em_3, None)
    for plane in (1, 4):
        step(source, target, coef_ref, plane, 1, -1, -1, False, False, False)
    step(source, target, coef_ref, 2, 2, -1, -1, True, True, False)
    step((main_3, my_3, em_3, None), (main_4, None, None, None), coef_ref, 1, 2, 0, -1, False, False, False)
    mine, other = core() * HALF, (1 - core()) * HALF
    for level, (ref, base) in enumerate(((block_1_ref, 0), (block_2_ref, 0), (main_3, HALF), (main_4, 0))):
        for i in range(HALF):
            put(keep_ref, HALF * level + i, tile(ref, base + mine + i))
            put(send_ref, HALF * level + i, tile(ref, base + other + i))


PAIRS = (
    ((0, 0), (0, 1)),
    ((0, 2), (0, 3)),
    ((1, 1), (1, 2)),
    ((1, 3), (1, 4)),
    ((2, 2), (2, 3)),
    ((3, 3), (3, 4)),
    ((4, 4), (2, 4)),
    ((0, 4), None),
)


def two_parts(values):
    high = values.astype(jnp.bfloat16)
    return high, (values - high.astype(jnp.float32)).astype(jnp.bfloat16)


def three_products(first, second, dims):
    def dot(a, b):
        return lax.dot_general(a, b, (dims, ((), ())), preferred_element_type=jnp.float32)

    return dot(first[0], second[0]) + (dot(first[0], second[1]) + dot(first[1], second[0]))


def dot_tn(first, second):
    return lax.dot_general(first, second, (((0,), (0,)), ((), ())), precision=HI, preferred_element_type=jnp.float32)


def dot_nn(first, second):
    return lax.dot_general(first, second, (((1,), (0,)), ((), ())), precision=HI, preferred_element_type=jnp.float32)


def gram_kernel(block_0, keep_ref, got_ref, high_ref, low_ref, gram_ref, basis_ref):
    mine, other = core() * HALF, (1 - core()) * HALF
    for y in range(8):
        lanes = slice(128 * y, 128 * (y + 1))
        basis_ref[0:M, lanes] = block_0[pl.ds(y, M, stride=8), :]
        for level in range(1, LEVELS):
            at = pl.ds(8 * HALF * (level - 1) + y, HALF, stride=8)
            basis_ref[pl.ds(pl.multiple_of(M * level + mine, 8), HALF), lanes] = keep_ref[at, :]
            basis_ref[pl.ds(pl.multiple_of(M * level + other, 8), HALF), lanes] = got_ref[at, :]
    parts = two_parts(basis_ref[...])
    high_ref[...], low_ref[...] = parts
    full = three_products(parts, parts, ((1,), (1,)))
    for index, pair in enumerate(PAIRS):
        for half, at in enumerate(pair):
            if at is None:
                value = jnp.zeros((M, M), jnp.float32)
            else:
                value = full[M * at[0] : M * at[0] + M, M * at[1] : M * at[1] + M]
            gram_ref[M * index : M * (index + 1), M * half : M * (half + 1)] = value


def eliminate(matrix, wanted):
    both = jnp.concatenate([matrix, wanted], axis=1)
    tiles = [both[8 * i : 8 * i + 8, :] for i in range(M // 8)]
    rows = iota_row()

    def column(value, at):
        return jnp.broadcast_to(value[:, at : at + 1], (8, 128))

    def block(_, tiles):
        tiles = list(tiles)
        columns = [column(tiles[0], b) for b in range(8)]
        row = [jnp.broadcast_to(tiles[0][a : a + 1, :], (8, 128)) for a in range(8)]
        small = [[jnp.broadcast_to(columns[b][a : a + 1, :], (8, 128)) for b in range(8)] for a in range(8)]
        for p in range(8):
            inverse = 1.0 / small[p][p]
            for a in range(p + 1, 8):
                factor = small[p][a] * inverse
                row[a] = row[a] - factor * row[p]
                for b in range(a, 8):
                    small[a][b] = small[a][b] - factor * small[p][b]
            row[p] = row[p] * inverse
            for b in range(p + 1, 8):
                small[p][b] = small[p][b] * inverse
        for p in range(7, 0, -1):
            for a in range(p):
                row[a] = row[a] - small[a][p] * row[p]
        for j in range(1, M // 8):
            value = tiles[j]
            for b in range(8):
                value = value - column(tiles[j], b) * row[b]
            tiles[j] = value
        value = row[0]
        for b in range(1, 8):
            value = jnp.where(rows == b, row[b], value)
        tiles[0] = value
        return tuple(roll_lane(t, -8) for t in tiles[1:] + tiles[:1])

    tiles = lax.fori_loop(0, M // 8, block, tuple(tiles), unroll=1)
    return jnp.concatenate(tiles, axis=0)[:, :M]


def apply_levels(blocks):
    out = [SHIFT * b for b in blocks] + [None]
    for j, b in enumerate(blocks):
        out[j + 1] = SCALE * b if out[j + 1] is None else out[j + 1] + SCALE * b
    return out


def pad_levels(blocks, count):
    return list(blocks) + [jnp.zeros((M, M), jnp.float32)] * (count - len(blocks))


def final_kernel(gram_ref, high_ref, low_ref, field_ref, resid_ref, full_ref):
    for index, pair in enumerate(PAIRS):
        for half, at in enumerate(pair):
            if at is None:
                continue
            value = gram_ref[M * index : M * (index + 1), M * half : M * (half + 1)]
            full_ref[M * at[0] : M * at[0] + M, M * at[1] : M * at[1] + M] = value
            if at[0] != at[1]:
                full_ref[M * at[1] : M * at[1] + M, M * at[0] : M * at[0] + M] = value.T
    eye = jnp.where(
        lax.broadcasted_iota(jnp.int32, (M, M), 0) == lax.broadcasted_iota(jnp.int32, (M, M), 1), 1.0, 0.0
    ).astype(jnp.float32)

    def gram(levels, blocks):
        count = M * levels
        return dot_nn(full_ref[0:count, 0 : M * len(blocks)], jnp.concatenate(blocks, axis=0))

    def minimal(half, second):
        levels = len(second)
        product = gram(levels, second)
        cross = sum(product[M * j : M * j + M] * b for j, b in enumerate(half))
        square = sum(product[M * j : M * j + M] * b for j, b in enumerate(second))
        def total(values):
            return jnp.sum(jnp.sum(values, axis=0, keepdims=True), axis=1, keepdims=True)

        return total(cross) / total(square), product[0:M]

    image_gram = SHIFT * full_ref[0:M, 0:M] + SCALE * full_ref[0:M, M : 2 * M]
    inverse = eliminate(dot_tn(image_gram, image_gram), image_gram.T)
    alpha = dot_nn(inverse, full_ref[0:M, 0:M])
    half = [eye - SHIFT * alpha, -SCALE * alpha]
    second = apply_levels(half)
    omega, second_gram = minimal(half, second)
    field = [alpha + omega * half[0], omega * half[1]]
    resid = [half[0] - omega * second[0], half[1] - omega * second[1], -omega * second[2]]
    beta = -dot_nn(inverse, second_gram)
    direct = [
        resid[0] + (1.0 - omega * SHIFT) * beta,
        resid[1] - (omega * SCALE) * beta,
        resid[2],
    ]
    image = apply_levels(direct)
    stacked = jnp.concatenate(
        [jnp.concatenate(image, axis=0), jnp.concatenate(pad_levels(resid, 4), axis=0)], axis=1
    )
    both = dot_nn(full_ref[0:M, 0 : 4 * M], stacked)
    image_gram, resid_gram = both[:, 0:M], both[:, M:]
    inverse = eliminate(dot_tn(image_gram, image_gram), image_gram.T)
    alpha = dot_nn(inverse, resid_gram)
    product = dot_nn(jnp.concatenate(image + direct, axis=0), alpha)
    half = [r - product[M * j : M * j + M] for j, r in enumerate(pad_levels(resid, 4))]
    second = apply_levels(half)
    omega, _ = minimal(half, second)
    field = pad_levels(field, 4)
    moved = [product[M * (4 + j) : M * (5 + j)] for j in range(3)] + [None]
    field = [
        f + omega * h + (0.0 if m is None else m) for f, h, m in zip(field, half, moved)
    ]
    field = pad_levels(field, 5)
    resid = [h - omega * s for h, s in zip(pad_levels(half, 5), second)]
    coefs = jnp.concatenate([jnp.concatenate(field, axis=0), jnp.concatenate(resid, axis=0)], axis=1)
    result = three_products(two_parts(coefs.T), (high_ref[...], low_ref[...]), ((1,), (0,)))
    for y in range(8):
        field_ref[pl.ds(y, M, stride=8), :] = result[0:M, 128 * y : 128 * (y + 1)]
        resid_ref[pl.ds(y, M, stride=8), :] = result[M:, 128 * y : 128 * (y + 1)]


VMEM = pl.BlockSpec(memory_space=pltpu.VMEM)
SMEM = pl.BlockSpec(memory_space=pltpu.SMEM)


def f32(*shape):
    return jax.ShapeDtypeStruct(shape, jnp.float32)


def call(kernel, name, outs, specs, scratch=()):
    return pl.pallas_call(
        kernel,
        name=name,
        out_shape=outs,
        in_specs=specs,
        out_specs=tuple(VMEM for _ in outs) if isinstance(outs, tuple) else VMEM,
        scratch_shapes=list(scratch),
        compiler_params=pltpu.CompilerParams(vmem_limit_bytes=32 * 1024 * 1024),
    )


def from_sides(axis, up, down, by=1):
    count = lax.axis_size(axis)
    lower = lax.ppermute(up, axis, [(i, i + by) for i in range(count - by)])
    upper = lax.ppermute(down, axis, [(i + by, i) for i in range(count - by)])
    return lower, upper


def spread(values, axes):
    count = lax.axis_size(axes)
    return lax.all_to_all(jnp.broadcast_to(values, (count, *values.shape)), axes, 0, 0)


def in_hbm(values):
    return pltpu.with_memory_space_constraint(values, pltpu.HBM)


def other_core(values):
    count = lax.axis_size("gx")
    return lax.ppermute(values, "gx", [(i, i ^ 1) for i in range(count)])


def tiles(count):
    return f32(8 * count, 128)


def scratch(*counts):
    return [pltpu.VMEM((8 * count, 128), jnp.float32) for count in counts]


def per_device(right_side, velocity, decay_rate, perm_class, conductivity, well_cells, well_rate):
    sizes = (lax.axis_size("gx"), 8 * lax.axis_size("gy"), 128 * lax.axis_size("gz"))
    block_0 = right_side.reshape(8 * M, 128)
    any_space = pl.BlockSpec(memory_space=pltpu.HBM)

    send, keep = call(
        pack_kernel,
        "pack",
        (tiles(SLOT), tiles(SLOT)),
        [any_space] * 5,
        [
            pltpu.VMEM((8, 128), jnp.int32),
            pltpu.SMEM(conductivity.shape, jnp.float32),
            pltpu.SemaphoreType.DMA((6,)),
        ],
    )(
        in_hbm(block_0),
        in_hbm(velocity.reshape(24, 128)),
        in_hbm(decay_rate.reshape(8, 128)),
        in_hbm(perm_class.reshape(8, 128)),
        in_hbm(conductivity),
    )
    got = other_core(send)
    wells = call(functools.partial(wells_kernel, sizes), "wells", tiles(16), [SMEM, SMEM])(well_cells, well_rate)
    main, zmsg = call(zmsg_kernel, "zmsg", (tiles(2 * SLOT), tiles(NE)), [VMEM] * 2)(keep, got)
    left_main, right_main = from_sides("gx", main, main, 2)
    low, high = from_sides("gz", zmsg, zmsg)
    up, down, edge = call(ymsg_kernel, "ymsg", (tiles(YPAIRS), tiles(YPAIRS), tiles(NE)), [VMEM] * 3)(
        main, low, high
    )
    below, above = from_sides("gy", up, down)
    my, ey, to_left, to_right = call(
        xmsg_kernel, "xmsg", (tiles(2 * SLOT), tiles(NE), tiles(A_TILES), tiles(A_TILES)), [VMEM] * 3
    )(edge, below, above)
    left, right = from_sides("gx", to_right, to_left, 2)
    coef, block_1, block_2, my, em, ey, to_left, to_right = call(
        functools.partial(first_two_kernel, sizes),
        "first_two",
        (
            tiles(4 * 28),
            tiles(M),
            tiles(M),
            tiles(M),
            tiles(2 * TG),
            tiles(2 * TG),
            tiles(B_TILES),
            tiles(B_TILES),
        ),
        [VMEM] * 9,
        scratch(24, 64, 6 * HALF, 6 * HALF, 6 * TG, 6 * TG, 4 * HALF, 4 * HALF, 4 * TG, 4 * TG),
    )(wells, main, edge, my, ey, left_main, right_main, left, right)
    left, right = from_sides("gx", to_right, to_left, 2)
    keep, send = call(
        last_two_kernel,
        "last_two",
        (tiles(4 * HALF), tiles(4 * HALF)),
        [VMEM] * 8,
        scratch(6 * HALF, 6 * HALF, 6 * TG, 6 * TG, 4 * HALF, 4 * HALF, 4 * TG, 2 * HALF),
    )(coef, block_1, block_2, my, em, ey, left, right)
    got = other_core(send)
    part = jax.ShapeDtypeStruct((LEVELS * M, 1024), jnp.bfloat16)
    high, low, gram = call(
        gram_kernel,
        "gram",
        (part, part, f32(8 * M, 128)),
        [VMEM] * 3,
        [pltpu.VMEM((LEVELS * M, 1024), jnp.float32)],
    )(block_0, keep, got)

    plane = ("gz", "gy")
    count = lax.axis_size(plane)
    gram = lax.all_to_all(gram.reshape(count, -1, 128), plane, 0, 0)
    gram = jnp.sum(gram, axis=0)
    gram = jnp.sum(spread(gram, "gx"), axis=0)
    gram = spread(gram, plane).reshape(8 * M, 128)
    field, resid = call(
        final_kernel,
        "final",
        (f32(8 * M, 128), f32(8 * M, 128)),
        [VMEM] * 3,
        [pltpu.VMEM((LEVELS * M, LEVELS * M), jnp.float32)],
    )(gram, high, low)
    return field.reshape(right_side.shape), resid.reshape(right_side.shape)


def solution(mesh):
    placed = (
        P(None, "gx", "gy", "gz"),
        P(None, "gx", "gy", "gz"),
        P("gx", "gy", "gz"),
        P("gx", "gy", "gz"),
        P(),
        P(),
        P(),
    )
    return jax.shard_map(
        per_device,
        mesh=mesh,
        in_specs=placed,
        out_specs=(P(None, "gx", "gy", "gz"), P(None, "gx", "gy", "gz")),
        check_vma=False,
    )
```

```python
import functools

import jax
import jax.numpy as jnp
from jax import lax
from jax.experimental import pallas as pl
from jax.experimental.pallas import tpu as pltpu
from jax.sharding import PartitionSpec as P

SHIFT = 7.5
SCALE = 3.0
LEVELS = 5
M = 64
HALF = M // 2
NEXTRA = 5
SLOT = HALF + NEXTRA
GROUPS = 16
TG = HALF // GROUPS
NE = 2 * TG + 1
HI = lax.Precision.HIGHEST


def iota_row():
    return lax.broadcasted_iota(jnp.int32, (8, 128), 0)


def iota_lane():
    return lax.broadcasted_iota(jnp.int32, (8, 128), 1)


def roll_lane(tile, shift):
    shift = shift % 128
    return tile if shift == 0 else pltpu.roll(tile, shift, 1)


def roll_row(tile, shift):
    shift = shift % 8
    return tile if shift == 0 else pltpu.roll(tile, shift, 0)


def swap_shift(first, second, roll, shift, mask):
    first, second = roll(first, shift), roll(second, shift)
    return jnp.where(mask, second, first), jnp.where(mask, first, second)


def tile(ref, index):
    if isinstance(index, int):
        return ref[8 * index : 8 * index + 8, :]
    return ref[pl.ds(pl.multiple_of(index * 8, 8), 8), :]


def put(ref, index, value):
    if isinstance(index, int):
        ref[8 * index : 8 * index + 8, :] = value
    else:
        ref[pl.ds(pl.multiple_of(index * 8, 8), 8), :] = value


def group_mask(lane, q):
    at = (lane + (4 - 8 * q)) & 127
    return at < 8


def core():
    return lax.rem(lax.axis_index("gx"), 2)


def pack_kernel(right_hbm, vel_hbm, decay_hbm, class_hbm, table_hbm, send_ref, keep_ref, class_ref, table_ref, sems):
    mine = pl.multiple_of(core() * 8 * HALF, 8)
    other = pl.multiple_of((1 - core()) * 8 * HALF, 8)
    copies = [
        (class_hbm, class_ref),
        (table_hbm, table_ref),
        (vel_hbm, keep_ref.at[pl.ds(8 * HALF, 24), :]),
        (decay_hbm, keep_ref.at[pl.ds(8 * (HALF + 3), 8), :]),
        (right_hbm.at[pl.ds(mine, 8 * HALF), :], keep_ref.at[pl.ds(0, 8 * HALF), :]),
        (right_hbm.at[pl.ds(other, 8 * HALF), :], send_ref.at[pl.ds(0, 8 * HALF), :]),
    ]
    copies = [pltpu.make_async_copy(src, dst, sems.at[i]) for i, (src, dst) in enumerate(copies)]
    for copy in copies:
        copy.start()
    for copy in copies:
        copy.wait()
    classes = class_ref[...]
    conduct = jnp.zeros((8, 128), jnp.float32)
    for index in range(table_ref.shape[0]):
        conduct = jnp.where(classes == index, table_ref[index], conduct)
    put(keep_ref, HALF + 4, conduct)
    put(send_ref, HALF + 4, conduct)
    for e in range(4):
        put(send_ref, HALF + e, tile(keep_ref, HALF + e))


def zmsg_kernel(keep_ref, got_ref, main_ref, zmsg_ref):
    lane = iota_lane()
    mine, other = core() * SLOT, (1 - core()) * SLOT
    for i in range(SLOT):
        put(main_ref, mine + i, tile(keep_ref, i))
        put(main_ref, other + i, tile(got_ref, i))

    def packed(indices):
        total = jnp.zeros((8, 128), jnp.float32)
        for q, index in enumerate(indices):
            total = jnp.where(group_mask(lane, q), roll_lane(tile(main_ref, index), 8 * q), total)
        return total

    for p in range(2):
        for t in range(TG):
            put(zmsg_ref, TG * p + t, packed([SLOT * p + GROUPS * t + q for q in range(GROUPS)]))
    put(zmsg_ref, NE - 1, packed([SLOT * p + HALF + e for p in range(2) for e in range(NEXTRA)]))


YPAIRS = (2 * SLOT + NE + 1) // 2


def ymsg_kernel(main_ref, low_ref, high_ref, up_ref, down_ref, edge_ref):
    row, lane = iota_row(), iota_lane()
    edges = []
    for t in range(NE):
        edge = jnp.where((lane & 7) >= 4, tile(low_ref, t), tile(high_ref, t))
        put(edge_ref, t, edge)
        edges.append(edge)

    def source(index):
        if index < 2 * SLOT:
            return tile(main_ref, index)
        return edges[min(index - 2 * SLOT, NE - 1)]

    lower = row < 4
    for g in range(YPAIRS):
        first, second = source(2 * g), roll_row(source(2 * g + 1), 4)
        put(up_ref, g, jnp.where(lower, second, first))
        put(down_ref, g, jnp.where(lower, first, second))


A_SECOND = SLOT
A_EDGE = A_SECOND + HALF // 2 + 1
A_TILES = A_EDGE + 2 * NE
B_MY = HALF
B_EDGE = B_MY + HALF // 4
B_SECOND = B_EDGE + TG
B_TILES = B_SECOND + HALF


def xmsg_kernel(edge_ref, below_ref, above_ref, my_ref, ey_ref, to_left_ref, to_right_ref):
    row = iota_row()
    lower = row < 4
    keep_2 = (row < 2) | (row >= 6)
    for g in range(YPAIRS):
        below, above = tile(below_ref, g), tile(above_ref, g)
        pair = (jnp.where(lower, above, below), roll_row(jnp.where(lower, below, above), 4))
        for half in range(2):
            index = 2 * g + half
            if index < 2 * SLOT:
                put(my_ref, index, pair[half])
                p, i = divmod(index, SLOT)
                put((to_left_ref, to_right_ref)[p], i, pair[half])
                if i == SLOT - 1:
                    put((to_right_ref, to_left_ref)[p], A_SECOND + HALF // 2, pair[half])
            elif index < 2 * SLOT + NE:
                put(ey_ref, index - 2 * SLOT, pair[half])
                for ref in (to_left_ref, to_right_ref):
                    put(ref, A_EDGE + NE + index - 2 * SLOT, pair[half])
    for p, second in enumerate((to_right_ref, to_left_ref)):
        for i in range(HALF // 2):
            value = jnp.where(
                keep_2,
                tile(my_ref, SLOT * p + 2 * i),
                roll_row(tile(my_ref, SLOT * p + 2 * i + 1), 4),
            )
            put(second, A_SECOND + i, value)
    for t in range(NE):
        value = tile(edge_ref, t)
        put(to_left_ref, A_EDGE + t, value)
        put(to_right_ref, A_EDGE + t, value)


def part_places():
    row, lane = iota_row(), iota_lane()
    at_y, at_z = lax.axis_index("gy"), lax.axis_index("gz")
    y_main = at_y * 8 + row
    y_my = at_y * 8 + jnp.where(row < 4, row + 8, row - 8)
    z_main = at_z * 128 + lane
    z_edge = at_z * 128 + jnp.where(lane < 64, lane + 128, lane - 128)
    return ((y_main, z_main), (y_my, z_main), (y_main, z_edge), (y_my, z_edge))


def wells_kernel(sizes, cells_ref, rate_ref, wells_ref):
    size_x, size_y, size_z = sizes
    first_x = lax.axis_index("gx") - core() - 1
    for part, (y_at, z_at) in enumerate(part_places()):
        flats = [((first_x + s) * size_y + y_at) * size_z + z_at for s in range(4)]
        wells = [jnp.zeros((8, 128), jnp.float32)] * 4
        for w in range(cells_ref.shape[0]):
            for s in range(4):
                wells[s] = wells[s] + jnp.where(flats[s] == cells_ref[w], rate_ref[w], 0.0)
        for s in range(4):
            put(wells_ref, s * 4 + part, wells[s])


def plane_coefficients(sizes, wells_ref, conduct_ref, given_ref, coef_ref):
    row, lane = iota_row(), iota_lane()
    size_x, size_y, size_z = sizes
    first_x = lax.axis_index("gx") - core() - 1
    where = part_places()

    def shift_y(four, shift, mask):
        main, my = swap_shift(four[0], four[1], roll_row, shift, mask)
        edge, ey = swap_shift(four[2], four[3], roll_row, shift, mask)
        return [main, my, edge, ey]

    def shift_z(four, shift, mask):
        main, edge = swap_shift(four[0], four[2], roll_lane, shift, mask)
        my, ey = swap_shift(four[1], four[3], roll_lane, shift, mask)
        return [main, my, edge, ey]

    def plane(s, carry):
        center = [tile(conduct_ref, (s + 1) * 4 + part) for part in range(4)]
        before = [tile(conduct_ref, s * 4 + part) for part in range(4)]
        after = [tile(conduct_ref, (s + 2) * 4 + part) for part in range(4)]
        plus = [after, shift_y(center, -1, row == 7), shift_z(center, -1, lane == 127)]
        minus = [before, shift_y(center, 1, row == 0), shift_z(center, 1, lane == 0)]
        at_x = first_x + s
        x_inside = (at_x >= 0) & (at_x < size_x)
        for part, (y_at, z_at) in enumerate(where):
            inside = (y_at >= 0) & (y_at < size_y) & (z_at >= 0) & (z_at < size_z) & x_inside
            if part >= 2:
                inside = inside & ((lane < 4) | (lane >= 124))
            given = [tile(given_ref, (s * 4 + e) * 4 + part) for e in range(4)]
            diagonal = given[3] + tile(wells_ref, s * 4 + part)
            values = []
            for d in range(3):
                plus_face = 0.5 * (center[part] + plus[d][part])
                minus_face = 0.5 * (center[part] + minus[d][part])
                diagonal = diagonal + (given[d] + plus_face + minus_face)
                values += [(given[d] + plus_face) * (-1.0 / SCALE), minus_face * (-1.0 / SCALE)]
            for index, value in enumerate([(diagonal - SHIFT) * (1.0 / SCALE)] + values):
                value = jnp.where(inside, value, 0.0)
                if part >= 2:
                    for shift in (8, 16, 32, 64):
                        value = value + roll_lane(value, shift)
                put(coef_ref, (s * 7 + index) * 4 + part, value)
        return carry

    lax.fori_loop(0, 4, plane, 0, unroll=True)


def step(source, target, coef_ref, first, count, coef_shift, out_shift, with_my=True, with_em=True, with_ey=True):
    main_ref, my_ref, em_ref, ey_ref = source
    row, lane = iota_row(), iota_lane()
    row_0, row_7 = row == 0, row == 7
    lane_0, lane_127 = lane == 0, lane == 127

    def block(i, carry):
        s, t = first + lax.div(i, TG), lax.rem(i, TG)

        def apply(part, center, after, before, y_plus, y_minus, z_plus, z_minus):
            def coef(index):
                return tile(coef_ref, ((s + coef_shift) * 7 + index) * 4 + part)

            total = coef(0) * center + (coef(1) * after + coef(2) * before)
            total = total + (coef(3) * y_plus + coef(4) * y_minus)
            return total + (coef(5) * z_plus + coef(6) * z_minus)

        at_field, at_edge = s * HALF + t * GROUPS, s * TG + t
        out_field, out_edge = (s + out_shift) * HALF + t * GROUPS, (s + out_shift) * TG + t
        em = tile(em_ref, at_edge)
        ey = tile(ey_ref, at_edge) if with_em or with_my else None
        near_m = jnp.zeros((8, 128), jnp.float32)
        near_y = jnp.zeros((8, 128), jnp.float32)
        for q in range(GROUPS):
            f = at_field + q
            main, my = tile(main_ref, f), tile(my_ref, f)
            beside = roll_lane(em, -8 * q)
            z_plus = roll_lane(jnp.where(lane_0, beside, main), -1)
            z_minus = roll_lane(jnp.where(lane_127, beside, main), 1)
            y_plus, my_plus = swap_shift(main, my, roll_row, -1, row_7)
            y_minus, my_minus = swap_shift(main, my, roll_row, 1, row_0)
            after, before = tile(main_ref, f + HALF), tile(main_ref, f - HALF)
            put(target[0], out_field + q, apply(0, main, after, before, y_plus, y_minus, z_plus, z_minus))
            at = ((lane + (1 - 8 * q)) & 127) < 2
            if with_em:
                near_m = jnp.where(at, roll_lane(main, 8 * q), near_m)
            if with_ey:
                near_y = jnp.where(at, roll_lane(my, 8 * q), near_y)
            if with_my:
                beside = roll_lane(ey, -8 * q)
                z_plus = roll_lane(jnp.where(lane_0, beside, my), -1)
                z_minus = roll_lane(jnp.where(lane_127, beside, my), 1)
                after, before = tile(my_ref, f + HALF), tile(my_ref, f - HALF)
                put(target[1], out_field + q, apply(1, my, after, before, my_plus, my_minus, z_plus, z_minus))
        seven, zero = (lane & 7) == 7, (lane & 7) == 0
        if with_em:
            em_plus, ey_plus = swap_shift(em, ey, roll_row, -1, row_7)
            em_minus, ey_minus = swap_shift(em, ey, roll_row, 1, row_0)
            z_plus = jnp.where(seven, roll_lane(near_m, -1), roll_lane(em, -1))
            z_minus = jnp.where(zero, roll_lane(near_m, 1), roll_lane(em, 1))
            after, before = tile(em_ref, at_edge + TG), tile(em_ref, at_edge - TG)
            put(target[2], out_edge, apply(2, em, after, before, em_plus, em_minus, z_plus, z_minus))
        if with_ey:
            z_plus = jnp.where(seven, roll_lane(near_y, -1), roll_lane(ey, -1))
            z_minus = jnp.where(zero, roll_lane(near_y, 1), roll_lane(ey, 1))
            after, before = tile(ey_ref, at_edge + TG), tile(ey_ref, at_edge - TG)
            put(target[3], out_edge, apply(3, ey, after, before, ey_plus, ey_minus, z_plus, z_minus))
        return carry

    lax.fori_loop(0, count * TG, block, 0)


def copy_tiles(source, at, target, to, count):
    for i in range(count):
        put(target, to + i, tile(source, at + i))


def first_two_kernel(
    sizes,
    wells_ref,
    main_ref,
    edge_ref,
    my_ref,
    ey_ref,
    left_main_ref,
    right_main_ref,
    left_ref,
    right_ref,
    coef_ref,
    keep_ref,
    send_ref,
    block_2_ref,
    my_2_ref,
    em_2_ref,
    ey_2_ref,
    to_left_ref,
    to_right_ref,
    conduct_ref,
    given_ref,
    main_0,
    my_0,
    em_0,
    ey_0,
    main_1,
    my_1,
    em_1,
    ey_1,
):
    row = iota_row()
    for p in range(2):
        copy_tiles(main_ref, SLOT * p, main_0, HALF * (2 + p), HALF)
        copy_tiles(my_ref, SLOT * p, my_0, HALF * (2 + p), HALF)
        copy_tiles(edge_ref, TG * p, em_0, TG * (2 + p), TG)
        copy_tiles(ey_ref, TG * p, ey_0, TG * (2 + p), TG)
    extras = {2: (main_ref, HALF, my_ref, HALF, edge_ref, NE - 1, ey_ref, NE - 1, 0)}
    extras[3] = (main_ref, SLOT + HALF, my_ref, SLOT + HALF, edge_ref, NE - 1, ey_ref, NE - 1, NEXTRA)
    for whole, ref, adjacent, second, p in ((left_main_ref, left_ref, 1, 0, 1), (right_main_ref, right_ref, 4, 5, 0)):
        copy_tiles(whole, SLOT * p, main_0, HALF * adjacent, HALF)
        copy_tiles(whole, SLOT * (1 - p), main_0, HALF * second, HALF)
        copy_tiles(ref, 0, my_0, HALF * adjacent, HALF)
        for i in range(HALF // 2):
            value = tile(ref, A_SECOND + i)
            put(my_0, HALF * second + 2 * i, value)
            put(my_0, HALF * second + 2 * i + 1, roll_row(value, 4))
        for plane, at in ((adjacent, p), (second, 1 - p)):
            copy_tiles(ref, A_EDGE + TG * at, em_0, TG * plane, TG)
            copy_tiles(ref, A_EDGE + NE + TG * at, ey_0, TG * plane, TG)
        em_at, ey_at = A_EDGE + NE - 1, A_EDGE + 2 * NE - 1
        extras[adjacent] = (whole, SLOT * p + HALF, ref, HALF, ref, em_at, ref, ey_at, NEXTRA * p)
        for part, value in enumerate(
            (
                tile(whole, SLOT * (1 - p) + SLOT - 1),
                tile(ref, A_SECOND + HALF // 2),
                roll_lane(tile(ref, em_at), -8 * (NEXTRA * (1 - p) + 4)),
                roll_lane(tile(ref, ey_at), -8 * (NEXTRA * (1 - p) + 4)),
            )
        ):
            put(conduct_ref, 4 * second + part, value)
    for plane, (a, a_at, b, b_at, c, c_at, d, d_at, q) in extras.items():
        for e in range(NEXTRA):
            values = (
                tile(a, a_at + e),
                tile(b, b_at + e),
                roll_lane(tile(c, c_at), -8 * (q + e)),
                roll_lane(tile(d, d_at), -8 * (q + e)),
            )
            for part, value in enumerate(values):
                if e == NEXTRA - 1:
                    put(conduct_ref, 4 * plane + part, value)
                else:
                    put(given_ref, ((plane - 1) * 4 + e) * 4 + part, value)
    plane_coefficients(sizes, wells_ref, conduct_ref, given_ref, coef_ref)
    step((main_0, my_0, em_0, ey_0), (main_1, my_1, em_1, ey_1), coef_ref, 1, 4, -1, -1)
    step((main_1, my_1, em_1, ey_1), (block_2_ref, my_2_ref, em_2_ref, ey_2_ref), coef_ref, 1, 2, 0, -1)
    for p, (adjacent, second) in enumerate(((to_left_ref, to_right_ref), (to_right_ref, to_left_ref))):
        for i in range(HALF):
            value = tile(block_2_ref, HALF * p + i)
            put(adjacent, i, value)
            put(second, B_SECOND + i, value)
        for i in range(HALF // 4):
            value = tile(my_2_ref, HALF * p + 4 * i)
            for k in range(1, 4):
                at_row = ((row + (1 - 2 * k)) & 7) < 2
                value = jnp.where(at_row, roll_row(tile(my_2_ref, HALF * p + 4 * i + k), 2 * k), value)
            put(adjacent, B_MY + i, value)
        copy_tiles(em_2_ref, TG * p, adjacent, B_EDGE, TG)
    by_plane(((main_1, HALF), (block_2_ref, 0)), keep_ref, send_ref)


def by_plane(levels, keep_ref, send_ref):
    mine, other = core() * HALF, (1 - core()) * HALF
    for level, (ref, base) in enumerate(levels):
        for i in range(HALF):
            put(keep_ref, HALF * level + i, tile(ref, base + mine + i))
            put(send_ref, HALF * level + i, tile(ref, base + other + i))


def last_two_kernel(
    coef_ref,
    block_2_ref,
    my_2_ref,
    em_2_ref,
    ey_2_ref,
    left_ref,
    right_ref,
    _,
    keep_ref,
    send_ref,
    main_2,
    my_2,
    em_2,
    ey_2,
    main_3,
    my_3,
    em_3,
    main_4,
):
    copy_tiles(block_2_ref, 0, main_2, 2 * HALF, 2 * HALF)
    copy_tiles(my_2_ref, 0, my_2, 2 * HALF, 2 * HALF)
    copy_tiles(em_2_ref, 0, em_2, 2 * TG, 2 * TG)
    copy_tiles(ey_2_ref, 0, ey_2, 2 * TG, 2 * TG)
    for ref, adjacent, second in ((left_ref, 1, 0), (right_ref, 4, 5)):
        copy_tiles(ref, 0, main_2, HALF * adjacent, HALF)
        for i in range(HALF // 4):
            value = tile(ref, B_MY + i)
            for k in range(4):
                put(my_2, HALF * adjacent + 4 * i + k, roll_row(value, -2 * k))
        copy_tiles(ref, B_EDGE, em_2, TG * adjacent, TG)
        copy_tiles(ref, B_SECOND, main_2, HALF * second, HALF)
    source, target = (main_2, my_2, em_2, ey_2), (main_3, my_3, em_3, None)
    for plane in (1, 4):
        step(source, target, coef_ref, plane, 1, -1, -1, False, False, False)
    step(source, target, coef_ref, 2, 2, -1, -1, True, True, False)
    step((main_3, my_3, em_3, None), (main_4, None, None, None), coef_ref, 1, 2, 0, -1, False, False, False)
    by_plane(((main_3, HALF), (main_4, 0)), keep_ref, send_ref)


PAIRS = (
    ((0, 0), (0, 1)),
    ((0, 2), (0, 3)),
    ((1, 1), (1, 2)),
    ((1, 3), (1, 4)),
    ((2, 2), (2, 3)),
    ((3, 3), (3, 4)),
    ((4, 4), (2, 4)),
    ((0, 4), None),
)


def two_parts(values):
    high = values.astype(jnp.bfloat16)
    return high, (values - high.astype(jnp.float32)).astype(jnp.bfloat16)


def three_products(first, second, dims):
    def dot(a, b):
        return lax.dot_general(a, b, (dims, ((), ())), preferred_element_type=jnp.float32)

    return dot(first[0], second[0]) + (dot(first[0], second[1]) + dot(first[1], second[0]))


def dot_tn(first, second):
    return lax.dot_general(first, second, (((0,), (0,)), ((), ())), precision=HI, preferred_element_type=jnp.float32)


def dot_nn(first, second):
    return lax.dot_general(first, second, (((1,), (0,)), ((), ())), precision=HI, preferred_element_type=jnp.float32)


def fill_levels(keep_ref, got_ref, basis_ref, base):
    mine, other = core() * HALF, (1 - core()) * HALF
    for y in range(8):
        lanes = slice(128 * y, 128 * (y + 1))
        for level in range(2):
            at = pl.ds(8 * HALF * level + y, HALF, stride=8)
            rows = base + M * level
            basis_ref[pl.ds(pl.multiple_of(rows + mine, 8), HALF), lanes] = keep_ref[at, :]
            basis_ref[pl.ds(pl.multiple_of(rows + other, 8), HALF), lanes] = got_ref[at, :]


def early_gram_kernel(block_0, keep_ref, got_ref, high_ref, low_ref, full_ref, basis_ref):
    for y in range(8):
        basis_ref[0:M, 128 * y : 128 * (y + 1)] = block_0[pl.ds(y, M, stride=8), :]
    fill_levels(keep_ref, got_ref, basis_ref, M)
    parts = two_parts(basis_ref[...])
    high_ref[...], low_ref[...] = parts
    full_ref[...] = three_products(parts, parts, ((1,), (1,)))


def gram_kernel(keep_ref, got_ref, early_high, early_low, early_full, high_ref, low_ref, gram_ref, basis_ref):
    fill_levels(keep_ref, got_ref, basis_ref, 0)
    parts = two_parts(basis_ref[...])
    high_ref[...], low_ref[...] = parts
    among = three_products(parts, parts, ((1,), (1,)))
    across = three_products((early_high[...], early_low[...]), parts, ((1,), (1,)))
    for index, pair in enumerate(PAIRS):
        for half, at in enumerate(pair):
            if at is None:
                value = jnp.zeros((M, M), jnp.float32)
            else:
                first, second = (slice(M * k, M * k + M) for k in at)
                if at[1] < 3:
                    value = early_full[first, second]
                else:
                    source, shift = (among, 3 * M) if at[0] >= 3 else (across, 0)
                    value = source[first.start - shift : first.stop - shift, second.start - 3 * M : second.stop - 3 * M]
            gram_ref[M * index : M * (index + 1), M * half : M * (half + 1)] = value


def eliminate(matrix, wanted):
    both = jnp.concatenate([matrix, wanted], axis=1)
    tiles = [both[8 * i : 8 * i + 8, :] for i in range(M // 8)]
    rows = iota_row()

    def column(value, at):
        return jnp.broadcast_to(value[:, at : at + 1], (8, 128))

    def block(_, tiles):
        tiles = list(tiles)
        columns = [column(tiles[0], b) for b in range(8)]
        row = [jnp.broadcast_to(tiles[0][a : a + 1, :], (8, 128)) for a in range(8)]
        small = [[jnp.broadcast_to(columns[b][a : a + 1, :], (8, 128)) for b in range(8)] for a in range(8)]
        for p in range(8):
            inverse = 1.0 / small[p][p]
            for a in range(p + 1, 8):
                factor = small[p][a] * inverse
                row[a] = row[a] - factor * row[p]
                for b in range(a, 8):
                    small[a][b] = small[a][b] - factor * small[p][b]
            row[p] = row[p] * inverse
            for b in range(p + 1, 8):
                small[p][b] = small[p][b] * inverse
        for p in range(7, 0, -1):
            for a in range(p):
                row[a] = row[a] - small[a][p] * row[p]
        for j in range(1, M // 8):
            value = tiles[j]
            for b in range(8):
                value = value - column(tiles[j], b) * row[b]
            tiles[j] = value
        value = row[0]
        for b in range(1, 8):
            value = jnp.where(rows == b, row[b], value)
        tiles[0] = value
        return tuple(roll_lane(t, -8) for t in tiles[1:] + tiles[:1])

    tiles = lax.fori_loop(0, M // 8, block, tuple(tiles), unroll=1)
    return jnp.concatenate(tiles, axis=0)[:, :M]


def apply_levels(blocks):
    out = [SHIFT * b for b in blocks] + [None]
    for j, b in enumerate(blocks):
        out[j + 1] = SCALE * b if out[j + 1] is None else out[j + 1] + SCALE * b
    return out


def pad_levels(blocks, count):
    return list(blocks) + [jnp.zeros((M, M), jnp.float32)] * (count - len(blocks))


def final_kernel(gram_ref, early_high, early_low, high_ref, low_ref, field_ref, resid_ref, full_ref):
    for index, pair in enumerate(PAIRS):
        for half, at in enumerate(pair):
            if at is None:
                continue
            value = gram_ref[M * index : M * (index + 1), M * half : M * (half + 1)]
            full_ref[M * at[0] : M * at[0] + M, M * at[1] : M * at[1] + M] = value
            if at[0] != at[1]:
                full_ref[M * at[1] : M * at[1] + M, M * at[0] : M * at[0] + M] = value.T
    eye = jnp.where(
        lax.broadcasted_iota(jnp.int32, (M, M), 0) == lax.broadcasted_iota(jnp.int32, (M, M), 1), 1.0, 0.0
    ).astype(jnp.float32)

    def gram(levels, blocks):
        count = M * levels
        return dot_nn(full_ref[0:count, 0 : M * len(blocks)], jnp.concatenate(blocks, axis=0))

    def minimal(half, second):
        levels = len(second)
        product = gram(levels, second)
        cross = sum(product[M * j : M * j + M] * b for j, b in enumerate(half))
        square = sum(product[M * j : M * j + M] * b for j, b in enumerate(second))
        def total(values):
            return jnp.sum(jnp.sum(values, axis=0, keepdims=True), axis=1, keepdims=True)

        return total(cross) / total(square), product[0:M]

    image_gram = SHIFT * full_ref[0:M, 0:M] + SCALE * full_ref[0:M, M : 2 * M]
    inverse = eliminate(dot_tn(image_gram, image_gram), image_gram.T)
    alpha = dot_nn(inverse, full_ref[0:M, 0:M])
    half = [eye - SHIFT * alpha, -SCALE * alpha]
    second = apply_levels(half)
    omega, second_gram = minimal(half, second)
    field = [alpha + omega * half[0], omega * half[1]]
    resid = [half[0] - omega * second[0], half[1] - omega * second[1], -omega * second[2]]
    beta = -dot_nn(inverse, second_gram)
    direct = [
        resid[0] + (1.0 - omega * SHIFT) * beta,
        resid[1] - (omega * SCALE) * beta,
        resid[2],
    ]
    image = apply_levels(direct)
    stacked = jnp.concatenate(
        [jnp.concatenate(image, axis=0), jnp.concatenate(pad_levels(resid, 4), axis=0)], axis=1
    )
    both = dot_nn(full_ref[0:M, 0 : 4 * M], stacked)
    image_gram, resid_gram = both[:, 0:M], both[:, M:]
    inverse = eliminate(dot_tn(image_gram, image_gram), image_gram.T)
    alpha = dot_nn(inverse, resid_gram)
    product = dot_nn(jnp.concatenate(image + direct, axis=0), alpha)
    half = [r - product[M * j : M * j + M] for j, r in enumerate(pad_levels(resid, 4))]
    second = apply_levels(half)
    omega, _ = minimal(half, second)
    field = pad_levels(field, 4)
    moved = [product[M * (4 + j) : M * (5 + j)] for j in range(3)] + [None]
    field = [
        f + omega * h + (0.0 if m is None else m) for f, h, m in zip(field, half, moved)
    ]
    field = pad_levels(field, 5)
    resid = [h - omega * s for h, s in zip(pad_levels(half, 5), second)]
    coefs = jnp.concatenate([jnp.concatenate(field, axis=0), jnp.concatenate(resid, axis=0)], axis=1)
    coefs = coefs.T
    result = three_products(two_parts(coefs[:, 0 : 3 * M]), (early_high[...], early_low[...]), ((1,), (0,)))
    result = result + three_products(two_parts(coefs[:, 3 * M :]), (high_ref[...], low_ref[...]), ((1,), (0,)))
    for y in range(8):
        field_ref[pl.ds(y, M, stride=8), :] = result[0:M, 128 * y : 128 * (y + 1)]
        resid_ref[pl.ds(y, M, stride=8), :] = result[M:, 128 * y : 128 * (y + 1)]


VMEM = pl.BlockSpec(memory_space=pltpu.VMEM)
SMEM = pl.BlockSpec(memory_space=pltpu.SMEM)


def f32(*shape):
    return jax.ShapeDtypeStruct(shape, jnp.float32)


def call(kernel, name, outs, specs, scratch=()):
    return pl.pallas_call(
        kernel,
        name=name,
        out_shape=outs,
        in_specs=specs,
        out_specs=tuple(VMEM for _ in outs) if isinstance(outs, tuple) else VMEM,
        scratch_shapes=list(scratch),
        compiler_params=pltpu.CompilerParams(vmem_limit_bytes=32 * 1024 * 1024),
    )


def from_sides(axis, up, down, by=1):
    count = lax.axis_size(axis)
    lower = lax.ppermute(up, axis, [(i, i + by) for i in range(count - by)])
    upper = lax.ppermute(down, axis, [(i + by, i) for i in range(count - by)])
    return lower, upper


def spread(values, axes):
    count = lax.axis_size(axes)
    return lax.all_to_all(jnp.broadcast_to(values, (count, *values.shape)), axes, 0, 0)


def in_hbm(values):
    return pltpu.with_memory_space_constraint(values, pltpu.HBM)


def other_core(values):
    count = lax.axis_size("gx")
    return lax.ppermute(values, "gx", [(i, i ^ 1) for i in range(count)])


def tiles(count):
    return f32(8 * count, 128)


def scratch(*counts):
    return [pltpu.VMEM((8 * count, 128), jnp.float32) for count in counts]


def per_device(right_side, velocity, decay_rate, perm_class, conductivity, well_cells, well_rate):
    sizes = (lax.axis_size("gx"), 8 * lax.axis_size("gy"), 128 * lax.axis_size("gz"))
    block_0 = right_side.reshape(8 * M, 128)
    any_space = pl.BlockSpec(memory_space=pltpu.HBM)

    send, keep = call(
        pack_kernel,
        "pack",
        (tiles(SLOT), tiles(SLOT)),
        [any_space] * 5,
        [
            pltpu.VMEM((8, 128), jnp.int32),
            pltpu.SMEM(conductivity.shape, jnp.float32),
            pltpu.SemaphoreType.DMA((6,)),
        ],
    )(
        in_hbm(block_0),
        in_hbm(velocity.reshape(24, 128)),
        in_hbm(decay_rate.reshape(8, 128)),
        in_hbm(perm_class.reshape(8, 128)),
        in_hbm(conductivity),
    )
    got = other_core(send)
    wells = call(functools.partial(wells_kernel, sizes), "wells", tiles(16), [SMEM, SMEM])(well_cells, well_rate)
    main, zmsg = call(zmsg_kernel, "zmsg", (tiles(2 * SLOT), tiles(NE)), [VMEM] * 2)(keep, got)
    left_main, right_main = from_sides("gx", main, main, 2)
    low, high = from_sides("gz", zmsg, zmsg)
    up, down, edge = call(ymsg_kernel, "ymsg", (tiles(YPAIRS), tiles(YPAIRS), tiles(NE)), [VMEM] * 3)(
        main, low, high
    )
    below, above = from_sides("gy", up, down)
    my, ey, to_left, to_right = call(
        xmsg_kernel, "xmsg", (tiles(2 * SLOT), tiles(NE), tiles(A_TILES), tiles(A_TILES)), [VMEM] * 3
    )(edge, below, above)
    left, right = from_sides("gx", to_right, to_left, 2)
    coef, keep, send, block_2, my, em, ey, to_left, to_right = call(
        functools.partial(first_two_kernel, sizes),
        "first_two",
        (
            tiles(4 * 28),
            tiles(2 * HALF),
            tiles(2 * HALF),
            tiles(M),
            tiles(M),
            tiles(2 * TG),
            tiles(2 * TG),
            tiles(B_TILES),
            tiles(B_TILES),
        ),
        [VMEM] * 9,
        scratch(24, 64, 6 * HALF, 6 * HALF, 6 * TG, 6 * TG, 4 * HALF, 4 * HALF, 4 * TG, 4 * TG),
    )(wells, main, edge, my, ey, left_main, right_main, left, right)
    left, right = from_sides("gx", to_right, to_left, 2)
    got = other_core(send)

    def rows(levels):
        return jax.ShapeDtypeStruct((levels * M, 1024), jnp.bfloat16)

    early_high, early_low, early_full = call(
        early_gram_kernel,
        "early_gram",
        (rows(3), rows(3), f32(3 * M, 3 * M)),
        [VMEM] * 3,
        [pltpu.VMEM((3 * M, 1024), jnp.float32)],
    )(block_0, keep, got)
    keep, send = call(
        last_two_kernel,
        "last_two",
        (tiles(2 * HALF), tiles(2 * HALF)),
        [VMEM] * 7 + [pl.BlockSpec(memory_space=pl.ANY)],
        scratch(6 * HALF, 6 * HALF, 6 * TG, 6 * TG, 4 * HALF, 4 * HALF, 4 * TG, 2 * HALF),
    )(coef, block_2, my, em, ey, left, right, early_full)
    got = other_core(send)
    high, low, gram = call(
        gram_kernel,
        "gram",
        (rows(2), rows(2), f32(8 * M, 128)),
        [VMEM] * 5,
        [pltpu.VMEM((2 * M, 1024), jnp.float32)],
    )(keep, got, early_high, early_low, early_full)

    plane = ("gz", "gy")
    count = lax.axis_size(plane)
    gram = lax.all_to_all(gram.reshape(count, -1, 128), plane, 0, 0)
    gram = jnp.sum(gram, axis=0)
    gram = jnp.sum(spread(gram, "gx"), axis=0)
    gram = spread(gram, plane).reshape(8 * M, 128)
    field, resid = call(
        final_kernel,
        "final",
        (f32(8 * M, 128), f32(8 * M, 128)),
        [VMEM] * 5,
        [pltpu.VMEM((LEVELS * M, LEVELS * M), jnp.float32)],
    )(gram, early_high, early_low, high, low)
    return field.reshape(right_side.shape), resid.reshape(right_side.shape)


def solution(mesh):
    placed = (
        P(None, "gx", "gy", "gz"),
        P(None, "gx", "gy", "gz"),
        P("gx", "gy", "gz"),
        P("gx", "gy", "gz"),
        P(),
        P(),
        P(),
    )
    return jax.shard_map(
        per_device,
        mesh=mesh,
        in_specs=placed,
        out_specs=(P(None, "gx", "gy", "gz"), P(None, "gx", "gy", "gz")),
        check_vma=False,
    )
```

```python
import functools

import jax
import jax.numpy as jnp
from jax import lax
from jax.experimental import pallas as pl
from jax.experimental.pallas import tpu as pltpu
from jax.sharding import PartitionSpec as P

SHIFT = 7.5
SCALE = 3.0
LEVELS = 5
M = 64
HALF = M // 2
NEXTRA = 5
SLOT = HALF + NEXTRA
GROUPS = 16
TG = HALF // GROUPS
NE = 2 * TG + 1
HI = lax.Precision.HIGHEST


def iota_row():
    return lax.broadcasted_iota(jnp.int32, (8, 128), 0)


def iota_lane():
    return lax.broadcasted_iota(jnp.int32, (8, 128), 1)


def roll_lane(tile, shift):
    shift = shift % 128
    return tile if shift == 0 else pltpu.roll(tile, shift, 1)


def roll_row(tile, shift):
    shift = shift % 8
    return tile if shift == 0 else pltpu.roll(tile, shift, 0)


def swap_shift(first, second, roll, shift, mask):
    first, second = roll(first, shift), roll(second, shift)
    return jnp.where(mask, second, first), jnp.where(mask, first, second)


def tile(ref, index):
    if isinstance(index, int):
        return ref[8 * index : 8 * index + 8, :]
    return ref[pl.ds(pl.multiple_of(index * 8, 8), 8), :]


def put(ref, index, value):
    if isinstance(index, int):
        ref[8 * index : 8 * index + 8, :] = value
    else:
        ref[pl.ds(pl.multiple_of(index * 8, 8), 8), :] = value


def group_mask(lane, q):
    at = (lane + (4 - 8 * q)) & 127
    return at < 8


def core():
    return lax.rem(lax.axis_index("gx"), 2)


def pack_kernel(right_hbm, vel_hbm, decay_hbm, class_hbm, table_hbm, send_ref, keep_ref, class_ref, table_ref, sems):
    mine = pl.multiple_of(core() * 8 * HALF, 8)
    other = pl.multiple_of((1 - core()) * 8 * HALF, 8)
    copies = [
        (class_hbm, class_ref),
        (table_hbm, table_ref),
        (vel_hbm, keep_ref.at[pl.ds(8 * HALF, 24), :]),
        (decay_hbm, keep_ref.at[pl.ds(8 * (HALF + 3), 8), :]),
        (right_hbm.at[pl.ds(mine, 8 * HALF), :], keep_ref.at[pl.ds(0, 8 * HALF), :]),
        (right_hbm.at[pl.ds(other, 8 * HALF), :], send_ref.at[pl.ds(0, 8 * HALF), :]),
    ]
    copies = [pltpu.make_async_copy(src, dst, sems.at[i]) for i, (src, dst) in enumerate(copies)]
    for copy in copies:
        copy.start()
    for copy in copies:
        copy.wait()
    classes = class_ref[...]
    conduct = jnp.zeros((8, 128), jnp.float32)
    for index in range(table_ref.shape[0]):
        conduct = jnp.where(classes == index, table_ref[index], conduct)
    put(keep_ref, HALF + 4, conduct)
    put(send_ref, HALF + 4, conduct)
    for e in range(4):
        put(send_ref, HALF + e, tile(keep_ref, HALF + e))


EARLY_TILES = SLOT + HALF + 1


def zmsg_kernel(keep_ref, got_ref, main_ref, zmsg_ref, to_left_ref, to_right_ref):
    lane = iota_lane()
    mine, other = core() * SLOT, (1 - core()) * SLOT
    for i in range(SLOT):
        put(main_ref, mine + i, tile(keep_ref, i))
        put(main_ref, other + i, tile(got_ref, i))

    def packed(indices):
        total = jnp.zeros((8, 128), jnp.float32)
        for q, index in enumerate(indices):
            total = jnp.where(group_mask(lane, q), roll_lane(tile(main_ref, index), 8 * q), total)
        return total

    for p in range(2):
        for t in range(TG):
            put(zmsg_ref, TG * p + t, packed([SLOT * p + GROUPS * t + q for q in range(GROUPS)]))
    put(zmsg_ref, NE - 1, packed([SLOT * p + HALF + e for p in range(2) for e in range(NEXTRA)]))
    for p, (adjacent, second) in enumerate(((to_left_ref, to_right_ref), (to_right_ref, to_left_ref))):
        for i in range(SLOT):
            value = tile(main_ref, SLOT * p + i)
            put(adjacent, i, value)
            if i < HALF or i == SLOT - 1:
                put(second, SLOT + min(i, HALF), value)


YPAIRS = (2 * SLOT + NE + 1) // 2


def ymsg_kernel(main_ref, low_ref, high_ref, up_ref, down_ref, edge_ref):
    row, lane = iota_row(), iota_lane()
    edges = []
    for t in range(NE):
        edge = jnp.where((lane & 7) >= 4, tile(low_ref, t), tile(high_ref, t))
        put(edge_ref, t, edge)
        edges.append(edge)

    def source(index):
        if index < 2 * SLOT:
            return tile(main_ref, index)
        return edges[min(index - 2 * SLOT, NE - 1)]

    lower = row < 4
    for g in range(YPAIRS):
        first, second = source(2 * g), roll_row(source(2 * g + 1), 4)
        put(up_ref, g, jnp.where(lower, second, first))
        put(down_ref, g, jnp.where(lower, first, second))


A_EXTRA = HALF // 4 * 3
A_SECOND = A_EXTRA + NEXTRA
A_EDGE = A_SECOND + HALF // 2 + 1
A_TILES = A_EDGE + 2 * NE
B_MY = HALF
B_EDGE = B_MY + HALF // 4
B_SECOND = B_EDGE + TG
B_TILES = B_SECOND + HALF


def xmsg_kernel(edge_ref, below_ref, above_ref, my_ref, ey_ref, to_left_ref, to_right_ref):
    row = iota_row()
    lower = row < 4
    keep_2 = (row < 2) | (row >= 6)
    for g in range(YPAIRS):
        below, above = tile(below_ref, g), tile(above_ref, g)
        pair = (jnp.where(lower, above, below), roll_row(jnp.where(lower, below, above), 4))
        for half in range(2):
            index = 2 * g + half
            if index < 2 * SLOT:
                put(my_ref, index, pair[half])
                p, i = divmod(index, SLOT)
                if i >= HALF:
                    put((to_left_ref, to_right_ref)[p], A_EXTRA + i - HALF, pair[half])
                if i == SLOT - 1:
                    put((to_right_ref, to_left_ref)[p], A_SECOND + HALF // 2, pair[half])
            elif index < 2 * SLOT + NE:
                put(ey_ref, index - 2 * SLOT, pair[half])
                for ref in (to_left_ref, to_right_ref):
                    put(ref, A_EDGE + NE + index - 2 * SLOT, pair[half])
    free = (row == 3) | (row == 4)
    for p, (adjacent, second) in enumerate(((to_left_ref, to_right_ref), (to_right_ref, to_left_ref))):
        for i in range(HALF // 4):
            first = SLOT * p + 4 * i
            fourth = tile(my_ref, first + 3)
            moved = (
                roll_row(fourth, 3),
                jnp.where(row < 4, roll_row(fourth, 1), roll_row(fourth, -1)),
                roll_row(fourth, -3),
            )
            for k in range(3):
                put(adjacent, 3 * i + k, jnp.where(free, moved[k], tile(my_ref, first + k)))
        for i in range(HALF // 2):
            value = jnp.where(
                keep_2,
                tile(my_ref, SLOT * p + 2 * i),
                roll_row(tile(my_ref, SLOT * p + 2 * i + 1), 4),
            )
            put(second, A_SECOND + i, value)
    for t in range(NE):
        value = tile(edge_ref, t)
        put(to_left_ref, A_EDGE + t, value)
        put(to_right_ref, A_EDGE + t, value)


def part_places():
    row, lane = iota_row(), iota_lane()
    at_y, at_z = lax.axis_index("gy"), lax.axis_index("gz")
    y_main = at_y * 8 + row
    y_my = at_y * 8 + jnp.where(row < 4, row + 8, row - 8)
    z_main = at_z * 128 + lane
    z_edge = at_z * 128 + jnp.where(lane < 64, lane + 128, lane - 128)
    return ((y_main, z_main), (y_my, z_main), (y_main, z_edge), (y_my, z_edge))


def wells_kernel(sizes, cells_ref, rate_ref, wells_ref):
    size_x, size_y, size_z = sizes
    first_x = lax.axis_index("gx") - core() - 1
    for part, (y_at, z_at) in enumerate(part_places()):
        flats = [((first_x + s) * size_y + y_at) * size_z + z_at for s in range(4)]
        wells = [jnp.zeros((8, 128), jnp.float32)] * 4
        for w in range(cells_ref.shape[0]):
            for s in range(4):
                wells[s] = wells[s] + jnp.where(flats[s] == cells_ref[w], rate_ref[w], 0.0)
        for s in range(4):
            put(wells_ref, s * 4 + part, wells[s])


def plane_coefficients(sizes, wells_ref, conduct_ref, given_ref, coef_ref):
    row, lane = iota_row(), iota_lane()
    size_x, size_y, size_z = sizes
    first_x = lax.axis_index("gx") - core() - 1
    where = part_places()

    def shift_y(four, shift, mask):
        main, my = swap_shift(four[0], four[1], roll_row, shift, mask)
        edge, ey = swap_shift(four[2], four[3], roll_row, shift, mask)
        return [main, my, edge, ey]

    def shift_z(four, shift, mask):
        main, edge = swap_shift(four[0], four[2], roll_lane, shift, mask)
        my, ey = swap_shift(four[1], four[3], roll_lane, shift, mask)
        return [main, my, edge, ey]

    def plane(s, carry):
        center = [tile(conduct_ref, (s + 1) * 4 + part) for part in range(4)]
        before = [tile(conduct_ref, s * 4 + part) for part in range(4)]
        after = [tile(conduct_ref, (s + 2) * 4 + part) for part in range(4)]
        plus = [after, shift_y(center, -1, row == 7), shift_z(center, -1, lane == 127)]
        minus = [before, shift_y(center, 1, row == 0), shift_z(center, 1, lane == 0)]
        at_x = first_x + s
        x_inside = (at_x >= 0) & (at_x < size_x)
        for part, (y_at, z_at) in enumerate(where):
            inside = (y_at >= 0) & (y_at < size_y) & (z_at >= 0) & (z_at < size_z) & x_inside
            if part >= 2:
                inside = inside & ((lane < 4) | (lane >= 124))
            given = [tile(given_ref, (s * 4 + e) * 4 + part) for e in range(4)]
            diagonal = given[3] + tile(wells_ref, s * 4 + part)
            values = []
            for d in range(3):
                plus_face = 0.5 * (center[part] + plus[d][part])
                minus_face = 0.5 * (center[part] + minus[d][part])
                diagonal = diagonal + (given[d] + plus_face + minus_face)
                values += [(given[d] + plus_face) * (-1.0 / SCALE), minus_face * (-1.0 / SCALE)]
            for index, value in enumerate([(diagonal - SHIFT) * (1.0 / SCALE)] + values):
                value = jnp.where(inside, value, 0.0)
                if part >= 2:
                    for shift in (8, 16, 32, 64):
                        value = value + roll_lane(value, shift)
                put(coef_ref, (s * 7 + index) * 4 + part, value)
        return carry

    lax.fori_loop(0, 4, plane, 0, unroll=True)


def step(source, target, coef_ref, first, count, coef_shift, out_shift, with_my=True, with_em=True, with_ey=True):
    main_ref, my_ref, em_ref, ey_ref = source
    row, lane = iota_row(), iota_lane()
    row_0, row_7 = row == 0, row == 7
    lane_0, lane_127 = lane == 0, lane == 127

    def block(i, carry):
        s, t = first + lax.div(i, TG), lax.rem(i, TG)

        def apply(part, center, after, before, y_plus, y_minus, z_plus, z_minus):
            def coef(index):
                return tile(coef_ref, ((s + coef_shift) * 7 + index) * 4 + part)

            total = coef(0) * center + (coef(1) * after + coef(2) * before)
            total = total + (coef(3) * y_plus + coef(4) * y_minus)
            return total + (coef(5) * z_plus + coef(6) * z_minus)

        at_field, at_edge = s * HALF + t * GROUPS, s * TG + t
        out_field, out_edge = (s + out_shift) * HALF + t * GROUPS, (s + out_shift) * TG + t
        em = tile(em_ref, at_edge)
        ey = tile(ey_ref, at_edge) if with_em or with_my else None
        near_m = jnp.zeros((8, 128), jnp.float32)
        near_y = jnp.zeros((8, 128), jnp.float32)
        for q in range(GROUPS):
            f = at_field + q
            main, my = tile(main_ref, f), tile(my_ref, f)
            beside = roll_lane(em, -8 * q)
            z_plus = roll_lane(jnp.where(lane_0, beside, main), -1)
            z_minus = roll_lane(jnp.where(lane_127, beside, main), 1)
            y_plus, my_plus = swap_shift(main, my, roll_row, -1, row_7)
            y_minus, my_minus = swap_shift(main, my, roll_row, 1, row_0)
            after, before = tile(main_ref, f + HALF), tile(main_ref, f - HALF)
            put(target[0], out_field + q, apply(0, main, after, before, y_plus, y_minus, z_plus, z_minus))
            at = ((lane + (1 - 8 * q)) & 127) < 2
            if with_em:
                near_m = jnp.where(at, roll_lane(main, 8 * q), near_m)
            if with_ey:
                near_y = jnp.where(at, roll_lane(my, 8 * q), near_y)
            if with_my:
                beside = roll_lane(ey, -8 * q)
                z_plus = roll_lane(jnp.where(lane_0, beside, my), -1)
                z_minus = roll_lane(jnp.where(lane_127, beside, my), 1)
                after, before = tile(my_ref, f + HALF), tile(my_ref, f - HALF)
                put(target[1], out_field + q, apply(1, my, after, before, my_plus, my_minus, z_plus, z_minus))
        seven, zero = (lane & 7) == 7, (lane & 7) == 0
        if with_em:
            em_plus, ey_plus = swap_shift(em, ey, roll_row, -1, row_7)
            em_minus, ey_minus = swap_shift(em, ey, roll_row, 1, row_0)
            z_plus = jnp.where(seven, roll_lane(near_m, -1), roll_lane(em, -1))
            z_minus = jnp.where(zero, roll_lane(near_m, 1), roll_lane(em, 1))
            after, before = tile(em_ref, at_edge + TG), tile(em_ref, at_edge - TG)
            put(target[2], out_edge, apply(2, em, after, before, em_plus, em_minus, z_plus, z_minus))
        if with_ey:
            z_plus = jnp.where(seven, roll_lane(near_y, -1), roll_lane(ey, -1))
            z_minus = jnp.where(zero, roll_lane(near_y, 1), roll_lane(ey, 1))
            after, before = tile(ey_ref, at_edge + TG), tile(ey_ref, at_edge - TG)
            put(target[3], out_edge, apply(3, ey, after, before, ey_plus, ey_minus, z_plus, z_minus))
        return carry

    lax.fori_loop(0, count * TG, block, 0)


def copy_tiles(source, at, target, to, count):
    for i in range(count):
        put(target, to + i, tile(source, at + i))


def first_two_kernel(
    sizes,
    wells_ref,
    main_ref,
    edge_ref,
    my_ref,
    ey_ref,
    left_main_ref,
    right_main_ref,
    left_ref,
    right_ref,
    coef_ref,
    keep_ref,
    send_ref,
    block_2_ref,
    my_2_ref,
    em_2_ref,
    ey_2_ref,
    to_left_ref,
    to_right_ref,
    conduct_ref,
    given_ref,
    main_0,
    my_0,
    em_0,
    ey_0,
    main_1,
    my_1,
    em_1,
    ey_1,
):
    row = iota_row()
    for p in range(2):
        copy_tiles(main_ref, SLOT * p, main_0, HALF * (2 + p), HALF)
        copy_tiles(my_ref, SLOT * p, my_0, HALF * (2 + p), HALF)
        copy_tiles(edge_ref, TG * p, em_0, TG * (2 + p), TG)
        copy_tiles(ey_ref, TG * p, ey_0, TG * (2 + p), TG)
    extras = {2: (main_ref, HALF, my_ref, HALF, edge_ref, NE - 1, ey_ref, NE - 1, 0)}
    extras[3] = (main_ref, SLOT + HALF, my_ref, SLOT + HALF, edge_ref, NE - 1, ey_ref, NE - 1, NEXTRA)
    for whole, ref, adjacent, second, p in ((left_main_ref, left_ref, 1, 0, 1), (right_main_ref, right_ref, 4, 5, 0)):
        copy_tiles(whole, 0, main_0, HALF * adjacent, HALF)
        copy_tiles(whole, SLOT, main_0, HALF * second, HALF)
        for i in range(HALF // 4):
            three = [tile(ref, 3 * i + k) for k in range(3)]
            for k in range(3):
                put(my_0, HALF * adjacent + 4 * i + k, three[k])
            fourth = jnp.where(row < 6, roll_row(three[1], 1), roll_row(three[2], 3))
            fourth = jnp.where(row < 4, roll_row(three[1], -1), fourth)
            fourth = jnp.where(row < 2, roll_row(three[0], -3), fourth)
            put(my_0, HALF * adjacent + 4 * i + 3, fourth)
        for i in range(HALF // 2):
            value = tile(ref, A_SECOND + i)
            put(my_0, HALF * second + 2 * i, value)
            put(my_0, HALF * second + 2 * i + 1, roll_row(value, 4))
        for plane, at in ((adjacent, p), (second, 1 - p)):
            copy_tiles(ref, A_EDGE + TG * at, em_0, TG * plane, TG)
            copy_tiles(ref, A_EDGE + NE + TG * at, ey_0, TG * plane, TG)
        em_at, ey_at = A_EDGE + NE - 1, A_EDGE + 2 * NE - 1
        extras[adjacent] = (whole, HALF, ref, A_EXTRA, ref, em_at, ref, ey_at, NEXTRA * p)
        for part, value in enumerate(
            (
                tile(whole, SLOT + HALF),
                tile(ref, A_SECOND + HALF // 2),
                roll_lane(tile(ref, em_at), -8 * (NEXTRA * (1 - p) + 4)),
                roll_lane(tile(ref, ey_at), -8 * (NEXTRA * (1 - p) + 4)),
            )
        ):
            put(conduct_ref, 4 * second + part, value)
    for plane, (a, a_at, b, b_at, c, c_at, d, d_at, q) in extras.items():
        for e in range(NEXTRA):
            values = (
                tile(a, a_at + e),
                tile(b, b_at + e),
                roll_lane(tile(c, c_at), -8 * (q + e)),
                roll_lane(tile(d, d_at), -8 * (q + e)),
            )
            for part, value in enumerate(values):
                if e == NEXTRA - 1:
                    put(conduct_ref, 4 * plane + part, value)
                else:
                    put(given_ref, ((plane - 1) * 4 + e) * 4 + part, value)
    plane_coefficients(sizes, wells_ref, conduct_ref, given_ref, coef_ref)
    step((main_0, my_0, em_0, ey_0), (main_1, my_1, em_1, ey_1), coef_ref, 1, 4, -1, -1)
    step((main_1, my_1, em_1, ey_1), (block_2_ref, my_2_ref, em_2_ref, ey_2_ref), coef_ref, 1, 2, 0, -1)
    for p, (adjacent, second) in enumerate(((to_left_ref, to_right_ref), (to_right_ref, to_left_ref))):
        for i in range(HALF):
            value = tile(block_2_ref, HALF * p + i)
            put(adjacent, i, value)
            put(second, B_SECOND + i, value)
        for i in range(HALF // 4):
            value = tile(my_2_ref, HALF * p + 4 * i)
            for k in range(1, 4):
                at_row = ((row + (1 - 2 * k)) & 7) < 2
                value = jnp.where(at_row, roll_row(tile(my_2_ref, HALF * p + 4 * i + k), 2 * k), value)
            put(adjacent, B_MY + i, value)
        copy_tiles(em_2_ref, TG * p, adjacent, B_EDGE, TG)
    by_plane(((main_1, HALF), (block_2_ref, 0)), keep_ref, send_ref)


def by_plane(levels, keep_ref, send_ref):
    mine, other = core() * HALF, (1 - core()) * HALF
    for level, (ref, base) in enumerate(levels):
        for i in range(HALF):
            put(keep_ref, HALF * level + i, tile(ref, base + mine + i))
            put(send_ref, HALF * level + i, tile(ref, base + other + i))


def last_two_kernel(
    coef_ref,
    block_2_ref,
    my_2_ref,
    em_2_ref,
    ey_2_ref,
    left_ref,
    right_ref,
    _,
    keep_ref,
    send_ref,
    main_2,
    my_2,
    em_2,
    ey_2,
    main_3,
    my_3,
    em_3,
    main_4,
):
    copy_tiles(block_2_ref, 0, main_2, 2 * HALF, 2 * HALF)
    copy_tiles(my_2_ref, 0, my_2, 2 * HALF, 2 * HALF)
    copy_tiles(em_2_ref, 0, em_2, 2 * TG, 2 * TG)
    copy_tiles(ey_2_ref, 0, ey_2, 2 * TG, 2 * TG)
    for ref, adjacent, second in ((left_ref, 1, 0), (right_ref, 4, 5)):
        copy_tiles(ref, 0, main_2, HALF * adjacent, HALF)
        for i in range(HALF // 4):
            value = tile(ref, B_MY + i)
            for k in range(4):
                put(my_2, HALF * adjacent + 4 * i + k, roll_row(value, -2 * k))
        copy_tiles(ref, B_EDGE, em_2, TG * adjacent, TG)
        copy_tiles(ref, B_SECOND, main_2, HALF * second, HALF)
    source, target = (main_2, my_2, em_2, ey_2), (main_3, my_3, em_3, None)
    for plane in (1, 4):
        step(source, target, coef_ref, plane, 1, -1, -1, False, False, False)
    step(source, target, coef_ref, 2, 2, -1, -1, True, True, False)
    step((main_3, my_3, em_3, None), (main_4, None, None, None), coef_ref, 1, 2, 0, -1, False, False, False)
    by_plane(((main_3, HALF), (main_4, 0)), keep_ref, send_ref)


PAIRS = (
    ((0, 0), (0, 1)),
    ((0, 2), (0, 3)),
    ((1, 1), (1, 2)),
    ((1, 3), (1, 4)),
    ((2, 2), (2, 3)),
    ((3, 3), (3, 4)),
    ((4, 4), (2, 4)),
    ((0, 4), None),
)


def two_parts(values):
    high = values.astype(jnp.bfloat16)
    return high, (values - high.astype(jnp.float32)).astype(jnp.bfloat16)


def three_products(first, second, dims):
    def dot(a, b):
        return lax.dot_general(a, b, (dims, ((), ())), preferred_element_type=jnp.float32)

    return dot(first[0], second[0]) + (dot(first[0], second[1]) + dot(first[1], second[0]))


def dot_tn(first, second):
    return lax.dot_general(first, second, (((0,), (0,)), ((), ())), precision=HI, preferred_element_type=jnp.float32)


def dot_nn(first, second):
    return lax.dot_general(first, second, (((1,), (0,)), ((), ())), precision=HI, preferred_element_type=jnp.float32)


def fill_levels(keep_ref, got_ref, basis_ref, base):
    mine, other = core() * HALF, (1 - core()) * HALF
    for y in range(8):
        lanes = slice(128 * y, 128 * (y + 1))
        for level in range(2):
            at = pl.ds(8 * HALF * level + y, HALF, stride=8)
            rows = base + M * level
            basis_ref[pl.ds(pl.multiple_of(rows + mine, 8), HALF), lanes] = keep_ref[at, :]
            basis_ref[pl.ds(pl.multiple_of(rows + other, 8), HALF), lanes] = got_ref[at, :]


def early_gram_kernel(block_0, keep_ref, got_ref, high_ref, low_ref, full_ref, basis_ref):
    for y in range(8):
        basis_ref[0:M, 128 * y : 128 * (y + 1)] = block_0[pl.ds(y, M, stride=8), :]
    fill_levels(keep_ref, got_ref, basis_ref, M)
    parts = two_parts(basis_ref[...])
    high_ref[...], low_ref[...] = parts
    full_ref[...] = three_products(parts, parts, ((1,), (1,)))


def gram_kernel(keep_ref, got_ref, early_high, early_low, early_full, high_ref, low_ref, gram_ref, basis_ref):
    fill_levels(keep_ref, got_ref, basis_ref, 0)
    parts = two_parts(basis_ref[...])
    high_ref[...], low_ref[...] = parts
    among = three_products(parts, parts, ((1,), (1,)))
    across = three_products((early_high[...], early_low[...]), parts, ((1,), (1,)))
    for index, pair in enumerate(PAIRS):
        for half, at in enumerate(pair):
            if at is None:
                value = jnp.zeros((M, M), jnp.float32)
            else:
                first, second = (slice(M * k, M * k + M) for k in at)
                if at[1] < 3:
                    value = early_full[first, second]
                else:
                    source, shift = (among, 3 * M) if at[0] >= 3 else (across, 0)
                    value = source[first.start - shift : first.stop - shift, second.start - 3 * M : second.stop - 3 * M]
            gram_ref[M * index : M * (index + 1), M * half : M * (half + 1)] = value


def eliminate(matrix, wanted):
    both = jnp.concatenate([matrix, wanted], axis=1)
    tiles = [both[8 * i : 8 * i + 8, :] for i in range(M // 8)]
    rows = iota_row()

    def column(value, at):
        return jnp.broadcast_to(value[:, at : at + 1], (8, 128))

    def block(_, tiles):
        tiles = list(tiles)
        columns = [column(tiles[0], b) for b in range(8)]
        row = [jnp.broadcast_to(tiles[0][a : a + 1, :], (8, 128)) for a in range(8)]
        small = [[jnp.broadcast_to(columns[b][a : a + 1, :], (8, 128)) for b in range(8)] for a in range(8)]
        for p in range(8):
            inverse = 1.0 / small[p][p]
            for a in range(p + 1, 8):
                factor = small[p][a] * inverse
                row[a] = row[a] - factor * row[p]
                for b in range(a, 8):
                    small[a][b] = small[a][b] - factor * small[p][b]
            row[p] = row[p] * inverse
            for b in range(p + 1, 8):
                small[p][b] = small[p][b] * inverse
        for p in range(7, 0, -1):
            for a in range(p):
                row[a] = row[a] - small[a][p] * row[p]
        for j in range(1, M // 8):
            value = tiles[j]
            for b in range(8):
                value = value - column(tiles[j], b) * row[b]
            tiles[j] = value
        value = row[0]
        for b in range(1, 8):
            value = jnp.where(rows == b, row[b], value)
        tiles[0] = value
        return tuple(roll_lane(t, -8) for t in tiles[1:] + tiles[:1])

    tiles = lax.fori_loop(0, M // 8, block, tuple(tiles), unroll=1)
    return jnp.concatenate(tiles, axis=0)[:, :M]


def apply_levels(blocks):
    out = [SHIFT * b for b in blocks] + [None]
    for j, b in enumerate(blocks):
        out[j + 1] = SCALE * b if out[j + 1] is None else out[j + 1] + SCALE * b
    return out


def pad_levels(blocks, count):
    return list(blocks) + [jnp.zeros((M, M), jnp.float32)] * (count - len(blocks))


def final_kernel(gram_ref, early_high, early_low, high_ref, low_ref, field_ref, resid_ref, full_ref):
    for index, pair in enumerate(PAIRS):
        for half, at in enumerate(pair):
            if at is None:
                continue
            value = gram_ref[M * index : M * (index + 1), M * half : M * (half + 1)]
            full_ref[M * at[0] : M * at[0] + M, M * at[1] : M * at[1] + M] = value
            if at[0] != at[1]:
                full_ref[M * at[1] : M * at[1] + M, M * at[0] : M * at[0] + M] = value.T
    eye = jnp.where(
        lax.broadcasted_iota(jnp.int32, (M, M), 0) == lax.broadcasted_iota(jnp.int32, (M, M), 1), 1.0, 0.0
    ).astype(jnp.float32)

    def gram(levels, blocks):
        count = M * levels
        return dot_nn(full_ref[0:count, 0 : M * len(blocks)], jnp.concatenate(blocks, axis=0))

    def minimal(half, second):
        levels = len(second)
        product = gram(levels, second)
        cross = sum(product[M * j : M * j + M] * b for j, b in enumerate(half))
        square = sum(product[M * j : M * j + M] * b for j, b in enumerate(second))
        def total(values):
            return jnp.sum(jnp.sum(values, axis=0, keepdims=True), axis=1, keepdims=True)

        return total(cross) / total(square), product[0:M]

    image_gram = SHIFT * full_ref[0:M, 0:M] + SCALE * full_ref[0:M, M : 2 * M]
    inverse = eliminate(dot_tn(image_gram, image_gram), image_gram.T)
    alpha = dot_nn(inverse, full_ref[0:M, 0:M])
    half = [eye - SHIFT * alpha, -SCALE * alpha]
    second = apply_levels(half)
    omega, second_gram = minimal(half, second)
    field = [alpha + omega * half[0], omega * half[1]]
    resid = [half[0] - omega * second[0], half[1] - omega * second[1], -omega * second[2]]
    beta = -dot_nn(inverse, second_gram)
    direct = [
        resid[0] + (1.0 - omega * SHIFT) * beta,
        resid[1] - (omega * SCALE) * beta,
        resid[2],
    ]
    image = apply_levels(direct)
    stacked = jnp.concatenate(
        [jnp.concatenate(image, axis=0), jnp.concatenate(pad_levels(resid, 4), axis=0)], axis=1
    )
    both = dot_nn(full_ref[0:M, 0 : 4 * M], stacked)
    image_gram, resid_gram = both[:, 0:M], both[:, M:]
    inverse = eliminate(dot_tn(image_gram, image_gram), image_gram.T)
    alpha = dot_nn(inverse, resid_gram)
    product = dot_nn(jnp.concatenate(image + direct, axis=0), alpha)
    half = [r - product[M * j : M * j + M] for j, r in enumerate(pad_levels(resid, 4))]
    second = apply_levels(half)
    omega, _ = minimal(half, second)
    field = pad_levels(field, 4)
    moved = [product[M * (4 + j) : M * (5 + j)] for j in range(3)] + [None]
    field = [
        f + omega * h + (0.0 if m is None else m) for f, h, m in zip(field, half, moved)
    ]
    field = pad_levels(field, 5)
    resid = [h - omega * s for h, s in zip(pad_levels(half, 5), second)]
    coefs = jnp.concatenate([jnp.concatenate(field, axis=0), jnp.concatenate(resid, axis=0)], axis=1)
    coefs = coefs.T
    result = three_products(two_parts(coefs[:, 0 : 3 * M]), (early_high[...], early_low[...]), ((1,), (0,)))
    result = result + three_products(two_parts(coefs[:, 3 * M :]), (high_ref[...], low_ref[...]), ((1,), (0,)))
    for y in range(8):
        field_ref[pl.ds(y, M, stride=8), :] = result[0:M, 128 * y : 128 * (y + 1)]
        resid_ref[pl.ds(y, M, stride=8), :] = result[M:, 128 * y : 128 * (y + 1)]


VMEM = pl.BlockSpec(memory_space=pltpu.VMEM)
SMEM = pl.BlockSpec(memory_space=pltpu.SMEM)


def f32(*shape):
    return jax.ShapeDtypeStruct(shape, jnp.float32)


def call(kernel, name, outs, specs, scratch=()):
    return pl.pallas_call(
        kernel,
        name=name,
        out_shape=outs,
        in_specs=specs,
        out_specs=tuple(VMEM for _ in outs) if isinstance(outs, tuple) else VMEM,
        scratch_shapes=list(scratch),
        compiler_params=pltpu.CompilerParams(vmem_limit_bytes=32 * 1024 * 1024),
    )


def from_sides(axis, up, down, by=1):
    count = lax.axis_size(axis)
    lower = lax.ppermute(up, axis, [(i, i + by) for i in range(count - by)])
    upper = lax.ppermute(down, axis, [(i + by, i) for i in range(count - by)])
    return lower, upper


def spread(values, axes):
    count = lax.axis_size(axes)
    return lax.all_to_all(jnp.broadcast_to(values, (count, *values.shape)), axes, 0, 0)


def in_hbm(values):
    return pltpu.with_memory_space_constraint(values, pltpu.HBM)


def other_core(values):
    count = lax.axis_size("gx")
    return lax.ppermute(values, "gx", [(i, i ^ 1) for i in range(count)])


def tiles(count):
    return f32(8 * count, 128)


def scratch(*counts):
    return [pltpu.VMEM((8 * count, 128), jnp.float32) for count in counts]


def per_device(right_side, velocity, decay_rate, perm_class, conductivity, well_cells, well_rate):
    sizes = (lax.axis_size("gx"), 8 * lax.axis_size("gy"), 128 * lax.axis_size("gz"))
    block_0 = right_side.reshape(8 * M, 128)
    any_space = pl.BlockSpec(memory_space=pltpu.HBM)

    send, keep = call(
        pack_kernel,
        "pack",
        (tiles(SLOT), tiles(SLOT)),
        [any_space] * 5,
        [
            pltpu.VMEM((8, 128), jnp.int32),
            pltpu.SMEM(conductivity.shape, jnp.float32),
            pltpu.SemaphoreType.DMA((6,)),
        ],
    )(
        in_hbm(block_0),
        in_hbm(velocity.reshape(24, 128)),
        in_hbm(decay_rate.reshape(8, 128)),
        in_hbm(perm_class.reshape(8, 128)),
        in_hbm(conductivity),
    )
    got = other_core(send)
    wells = call(functools.partial(wells_kernel, sizes), "wells", tiles(16), [SMEM, SMEM])(well_cells, well_rate)
    main, zmsg, to_left, to_right = call(
        zmsg_kernel, "zmsg", (tiles(2 * SLOT), tiles(NE), tiles(EARLY_TILES), tiles(EARLY_TILES)), [VMEM] * 2
    )(keep, got)
    left_main, right_main = from_sides("gx", to_right, to_left, 2)
    low, high = from_sides("gz", zmsg, zmsg)
    up, down, edge = call(ymsg_kernel, "ymsg", (tiles(YPAIRS), tiles(YPAIRS), tiles(NE)), [VMEM] * 3)(
        main, low, high
    )
    below, above = from_sides("gy", up, down)
    my, ey, to_left, to_right = call(
        xmsg_kernel, "xmsg", (tiles(2 * SLOT), tiles(NE), tiles(A_TILES), tiles(A_TILES)), [VMEM] * 3
    )(edge, below, above)
    left, right = from_sides("gx", to_right, to_left, 2)
    coef, keep, send, block_2, my, em, ey, to_left, to_right = call(
        functools.partial(first_two_kernel, sizes),
        "first_two",
        (
            tiles(4 * 28),
            tiles(2 * HALF),
            tiles(2 * HALF),
            tiles(M),
            tiles(M),
            tiles(2 * TG),
            tiles(2 * TG),
            tiles(B_TILES),
            tiles(B_TILES),
        ),
        [VMEM] * 9,
        scratch(24, 64, 6 * HALF, 6 * HALF, 6 * TG, 6 * TG, 4 * HALF, 4 * HALF, 4 * TG, 4 * TG),
    )(wells, main, edge, my, ey, left_main, right_main, left, right)
    left, right = from_sides("gx", to_right, to_left, 2)
    got = other_core(send)

    def rows(levels):
        return jax.ShapeDtypeStruct((levels * M, 1024), jnp.bfloat16)

    early_high, early_low, early_full = call(
        early_gram_kernel,
        "early_gram",
        (rows(3), rows(3), f32(3 * M, 3 * M)),
        [VMEM] * 3,
        [pltpu.VMEM((3 * M, 1024), jnp.float32)],
    )(block_0, keep, got)
    keep, send = call(
        last_two_kernel,
        "last_two",
        (tiles(2 * HALF), tiles(2 * HALF)),
        [VMEM] * 7 + [pl.BlockSpec(memory_space=pl.ANY)],
        scratch(6 * HALF, 6 * HALF, 6 * TG, 6 * TG, 4 * HALF, 4 * HALF, 4 * TG, 2 * HALF),
    )(coef, block_2, my, em, ey, left, right, early_full)
    got = other_core(send)
    high, low, gram = call(
        gram_kernel,
        "gram",
        (rows(2), rows(2), f32(8 * M, 128)),
        [VMEM] * 5,
        [pltpu.VMEM((2 * M, 1024), jnp.float32)],
    )(keep, got, early_high, early_low, early_full)

    plane = ("gz", "gy")
    count = lax.axis_size(plane)
    gram = lax.all_to_all(gram.reshape(count, -1, 128), plane, 0, 0)
    gram = jnp.sum(gram, axis=0)
    gram = jnp.sum(spread(gram, "gx"), axis=0)
    gram = spread(gram, plane).reshape(8 * M, 128)
    field, resid = call(
        final_kernel,
        "final",
        (f32(8 * M, 128), f32(8 * M, 128)),
        [VMEM] * 5,
        [pltpu.VMEM((LEVELS * M, LEVELS * M), jnp.float32)],
    )(gram, early_high, early_low, high, low)
    return field.reshape(right_side.shape), resid.reshape(right_side.shape)


def solution(mesh):
    placed = (
        P(None, "gx", "gy", "gz"),
        P(None, "gx", "gy", "gz"),
        P("gx", "gy", "gz"),
        P("gx", "gy", "gz"),
        P(),
        P(),
        P(),
    )
    return jax.shard_map(
        per_device,
        mesh=mesh,
        in_specs=placed,
        out_specs=(P(None, "gx", "gy", "gz"), P(None, "gx", "gy", "gz")),
        check_vma=False,
    )
```

```python
import functools

import jax
import jax.numpy as jnp
from jax import lax
from jax.experimental import pallas as pl
from jax.experimental.pallas import tpu as pltpu
from jax.sharding import PartitionSpec as P

SHIFT = 7.5
SCALE = 3.0
LEVELS = 5
M = 64
HALF = M // 2
NEXTRA = 5
SLOT = HALF + NEXTRA
GROUPS = 16
TG = HALF // GROUPS
NE = 2 * TG + 1
HI = lax.Precision.HIGHEST


def iota_row():
    return lax.broadcasted_iota(jnp.int32, (8, 128), 0)


def iota_lane():
    return lax.broadcasted_iota(jnp.int32, (8, 128), 1)


def roll_lane(tile, shift):
    shift = shift % 128
    return tile if shift == 0 else pltpu.roll(tile, shift, 1)


def roll_row(tile, shift):
    shift = shift % 8
    return tile if shift == 0 else pltpu.roll(tile, shift, 0)


def swap_shift(first, second, roll, shift, mask):
    first, second = roll(first, shift), roll(second, shift)
    return jnp.where(mask, second, first), jnp.where(mask, first, second)


def tile(ref, index):
    if isinstance(index, int):
        return ref[8 * index : 8 * index + 8, :]
    return ref[pl.ds(pl.multiple_of(index * 8, 8), 8), :]


def put(ref, index, value):
    if isinstance(index, int):
        ref[8 * index : 8 * index + 8, :] = value
    else:
        ref[pl.ds(pl.multiple_of(index * 8, 8), 8), :] = value


def group_mask(lane, q):
    at = (lane + (4 - 8 * q)) & 127
    return at < 8


def core():
    return lax.rem(lax.axis_index("gx"), 2)


def pack_kernel(right_hbm, vel_hbm, decay_hbm, class_hbm, table_hbm, send_ref, keep_ref, class_ref, table_ref, sems):
    mine = pl.multiple_of(core() * 8 * HALF, 8)
    other = pl.multiple_of((1 - core()) * 8 * HALF, 8)
    copies = [
        (class_hbm, class_ref),
        (table_hbm, table_ref),
        (vel_hbm, keep_ref.at[pl.ds(8 * HALF, 24), :]),
        (decay_hbm, keep_ref.at[pl.ds(8 * (HALF + 3), 8), :]),
        (right_hbm.at[pl.ds(mine, 8 * HALF), :], keep_ref.at[pl.ds(0, 8 * HALF), :]),
        (right_hbm.at[pl.ds(other, 8 * HALF), :], send_ref.at[pl.ds(0, 8 * HALF), :]),
    ]
    copies = [pltpu.make_async_copy(src, dst, sems.at[i]) for i, (src, dst) in enumerate(copies)]
    for copy in copies:
        copy.start()
    for copy in copies:
        copy.wait()
    classes = class_ref[...]
    conduct = jnp.zeros((8, 128), jnp.float32)
    for index in range(table_ref.shape[0]):
        conduct = jnp.where(classes == index, table_ref[index], conduct)
    put(keep_ref, HALF + 4, conduct)
    put(send_ref, HALF + 4, conduct)
    for e in range(4):
        put(send_ref, HALF + e, tile(keep_ref, HALF + e))


EARLY_TILES = SLOT + HALF + 1


def zmsg_kernel(keep_ref, got_ref, main_ref, zmsg_ref, to_left_ref, to_right_ref):
    lane = iota_lane()
    mine, other = core() * SLOT, (1 - core()) * SLOT
    for i in range(SLOT):
        put(main_ref, mine + i, tile(keep_ref, i))
        put(main_ref, other + i, tile(got_ref, i))

    def packed(indices):
        total = jnp.zeros((8, 128), jnp.float32)
        for q, index in enumerate(indices):
            total = jnp.where(group_mask(lane, q), roll_lane(tile(main_ref, index), 8 * q), total)
        return total

    for p in range(2):
        for t in range(TG):
            put(zmsg_ref, TG * p + t, packed([SLOT * p + GROUPS * t + q for q in range(GROUPS)]))
    put(zmsg_ref, NE - 1, packed([SLOT * p + HALF + e for p in range(2) for e in range(NEXTRA)]))
    for p, (adjacent, second) in enumerate(((to_left_ref, to_right_ref), (to_right_ref, to_left_ref))):
        for i in range(SLOT):
            value = tile(main_ref, SLOT * p + i)
            put(adjacent, i, value)
            if i < HALF or i == SLOT - 1:
                put(second, SLOT + min(i, HALF), value)


YPAIRS = (2 * SLOT + NE + 1) // 2


def ymsg_kernel(main_ref, low_ref, high_ref, up_ref, down_ref, edge_ref):
    row, lane = iota_row(), iota_lane()
    edges = []
    for t in range(NE):
        edge = jnp.where((lane & 7) >= 4, tile(low_ref, t), tile(high_ref, t))
        put(edge_ref, t, edge)
        edges.append(edge)

    def source(index):
        if index < 2 * SLOT:
            return tile(main_ref, index)
        return edges[min(index - 2 * SLOT, NE - 1)]

    lower = row < 4
    for g in range(YPAIRS):
        first, second = source(2 * g), roll_row(source(2 * g + 1), 4)
        put(up_ref, g, jnp.where(lower, second, first))
        put(down_ref, g, jnp.where(lower, first, second))


A_EXTRA = HALF // 4 * 3
A_SECOND = A_EXTRA + NEXTRA
A_EDGE = A_SECOND + HALF // 2 + 1
A_TILES = A_EDGE + 2 * NE
B_MY = HALF
B_EDGE = B_MY + HALF // 4
B_SECOND = B_EDGE + TG
B_TILES = B_SECOND + HALF


def xmsg_kernel(edge_ref, below_ref, above_ref, my_ref, ey_ref, to_left_ref, to_right_ref):
    row = iota_row()
    lower = row < 4
    keep_2 = (row < 2) | (row >= 6)
    for g in range(YPAIRS):
        below, above = tile(below_ref, g), tile(above_ref, g)
        pair = (jnp.where(lower, above, below), roll_row(jnp.where(lower, below, above), 4))
        for half in range(2):
            index = 2 * g + half
            if index < 2 * SLOT:
                put(my_ref, index, pair[half])
                p, i = divmod(index, SLOT)
                if i >= HALF:
                    put((to_left_ref, to_right_ref)[p], A_EXTRA + i - HALF, pair[half])
                if i == SLOT - 1:
                    put((to_right_ref, to_left_ref)[p], A_SECOND + HALF // 2, pair[half])
            elif index < 2 * SLOT + NE:
                put(ey_ref, index - 2 * SLOT, pair[half])
                for ref in (to_left_ref, to_right_ref):
                    put(ref, A_EDGE + NE + index - 2 * SLOT, pair[half])
    free = (row == 3) | (row == 4)
    for p, (adjacent, second) in enumerate(((to_left_ref, to_right_ref), (to_right_ref, to_left_ref))):
        for i in range(HALF // 4):
            first = SLOT * p + 4 * i
            fourth = tile(my_ref, first + 3)
            moved = (
                roll_row(fourth, 3),
                jnp.where(row < 4, roll_row(fourth, 1), roll_row(fourth, -1)),
                roll_row(fourth, -3),
            )
            for k in range(3):
                put(adjacent, 3 * i + k, jnp.where(free, moved[k], tile(my_ref, first + k)))
        for i in range(HALF // 2):
            value = jnp.where(
                keep_2,
                tile(my_ref, SLOT * p + 2 * i),
                roll_row(tile(my_ref, SLOT * p + 2 * i + 1), 4),
            )
            put(second, A_SECOND + i, value)
    for t in range(NE):
        value = tile(edge_ref, t)
        put(to_left_ref, A_EDGE + t, value)
        put(to_right_ref, A_EDGE + t, value)


def part_places():
    row, lane = iota_row(), iota_lane()
    at_y, at_z = lax.axis_index("gy"), lax.axis_index("gz")
    y_main = at_y * 8 + row
    y_my = at_y * 8 + jnp.where(row < 4, row + 8, row - 8)
    z_main = at_z * 128 + lane
    z_edge = at_z * 128 + jnp.where(lane < 64, lane + 128, lane - 128)
    return ((y_main, z_main), (y_my, z_main), (y_main, z_edge), (y_my, z_edge))


def wells_kernel(sizes, cells_ref, rate_ref, wells_ref):
    size_x, size_y, size_z = sizes
    first_x = lax.axis_index("gx") - core() - 1
    for part, (y_at, z_at) in enumerate(part_places()):
        flats = [((first_x + s) * size_y + y_at) * size_z + z_at for s in range(4)]
        wells = [jnp.zeros((8, 128), jnp.float32)] * 4
        for w in range(cells_ref.shape[0]):
            for s in range(4):
                wells[s] = wells[s] + jnp.where(flats[s] == cells_ref[w], rate_ref[w], 0.0)
        for s in range(4):
            put(wells_ref, s * 4 + part, wells[s])


def plane_coefficients(sizes, wells_ref, conduct_ref, given_ref, coef_ref):
    row, lane = iota_row(), iota_lane()
    size_x, size_y, size_z = sizes
    first_x = lax.axis_index("gx") - core() - 1
    where = part_places()

    def shift_y(four, shift, mask):
        main, my = swap_shift(four[0], four[1], roll_row, shift, mask)
        edge, ey = swap_shift(four[2], four[3], roll_row, shift, mask)
        return [main, my, edge, ey]

    def shift_z(four, shift, mask):
        main, edge = swap_shift(four[0], four[2], roll_lane, shift, mask)
        my, ey = swap_shift(four[1], four[3], roll_lane, shift, mask)
        return [main, my, edge, ey]

    def plane(s, carry):
        center = [tile(conduct_ref, (s + 1) * 4 + part) for part in range(4)]
        before = [tile(conduct_ref, s * 4 + part) for part in range(4)]
        after = [tile(conduct_ref, (s + 2) * 4 + part) for part in range(4)]
        plus = [after, shift_y(center, -1, row == 7), shift_z(center, -1, lane == 127)]
        minus = [before, shift_y(center, 1, row == 0), shift_z(center, 1, lane == 0)]
        at_x = first_x + s
        x_inside = (at_x >= 0) & (at_x < size_x)
        for part, (y_at, z_at) in enumerate(where):
            inside = (y_at >= 0) & (y_at < size_y) & (z_at >= 0) & (z_at < size_z) & x_inside
            if part >= 2:
                inside = inside & ((lane < 4) | (lane >= 124))
            given = [tile(given_ref, (s * 4 + e) * 4 + part) for e in range(4)]
            diagonal = given[3] + tile(wells_ref, s * 4 + part)
            values = []
            for d in range(3):
                plus_face = 0.5 * (center[part] + plus[d][part])
                minus_face = 0.5 * (center[part] + minus[d][part])
                diagonal = diagonal + (given[d] + plus_face + minus_face)
                values += [(given[d] + plus_face) * (-1.0 / SCALE), minus_face * (-1.0 / SCALE)]
            for index, value in enumerate([(diagonal - SHIFT) * (1.0 / SCALE)] + values):
                value = jnp.where(inside, value, 0.0)
                if part >= 2:
                    for shift in (8, 16, 32, 64):
                        value = value + roll_lane(value, shift)
                put(coef_ref, (s * 7 + index) * 4 + part, value)
        return carry

    lax.fori_loop(0, 4, plane, 0, unroll=True)


def step(source, target, coef_ref, first, count, coef_shift, out_shift, with_my=True, with_em=True, with_ey=True):
    main_ref, my_ref, em_ref, ey_ref = source
    row, lane = iota_row(), iota_lane()
    row_0, row_7 = row == 0, row == 7
    lane_0, lane_127 = lane == 0, lane == 127

    def block(i, carry):
        s, t = first + lax.div(i, TG), lax.rem(i, TG)

        def apply(part, center, after, before, y_plus, y_minus, z_plus, z_minus):
            def coef(index):
                return tile(coef_ref, ((s + coef_shift) * 7 + index) * 4 + part)

            total = coef(0) * center + (coef(1) * after + coef(2) * before)
            total = total + (coef(3) * y_plus + coef(4) * y_minus)
            return total + (coef(5) * z_plus + coef(6) * z_minus)

        at_field, at_edge = s * HALF + t * GROUPS, s * TG + t
        out_field, out_edge = (s + out_shift) * HALF + t * GROUPS, (s + out_shift) * TG + t
        em = tile(em_ref, at_edge)
        ey = tile(ey_ref, at_edge) if with_em or with_my else None
        near_m = jnp.zeros((8, 128), jnp.float32)
        near_y = jnp.zeros((8, 128), jnp.float32)
        for q in range(GROUPS):
            f = at_field + q
            main, my = tile(main_ref, f), tile(my_ref, f)
            beside = roll_lane(em, -8 * q)
            z_plus = roll_lane(jnp.where(lane_0, beside, main), -1)
            z_minus = roll_lane(jnp.where(lane_127, beside, main), 1)
            y_plus, my_plus = swap_shift(main, my, roll_row, -1, row_7)
            y_minus, my_minus = swap_shift(main, my, roll_row, 1, row_0)
            after, before = tile(main_ref, f + HALF), tile(main_ref, f - HALF)
            put(target[0], out_field + q, apply(0, main, after, before, y_plus, y_minus, z_plus, z_minus))
            at = ((lane + (1 - 8 * q)) & 127) < 2
            if with_em:
                near_m = jnp.where(at, roll_lane(main, 8 * q), near_m)
            if with_ey:
                near_y = jnp.where(at, roll_lane(my, 8 * q), near_y)
            if with_my:
                beside = roll_lane(ey, -8 * q)
                z_plus = roll_lane(jnp.where(lane_0, beside, my), -1)
                z_minus = roll_lane(jnp.where(lane_127, beside, my), 1)
                after, before = tile(my_ref, f + HALF), tile(my_ref, f - HALF)
                put(target[1], out_field + q, apply(1, my, after, before, my_plus, my_minus, z_plus, z_minus))
        seven, zero = (lane & 7) == 7, (lane & 7) == 0
        if with_em:
            em_plus, ey_plus = swap_shift(em, ey, roll_row, -1, row_7)
            em_minus, ey_minus = swap_shift(em, ey, roll_row, 1, row_0)
            z_plus = jnp.where(seven, roll_lane(near_m, -1), roll_lane(em, -1))
            z_minus = jnp.where(zero, roll_lane(near_m, 1), roll_lane(em, 1))
            after, before = tile(em_ref, at_edge + TG), tile(em_ref, at_edge - TG)
            put(target[2], out_edge, apply(2, em, after, before, em_plus, em_minus, z_plus, z_minus))
        if with_ey:
            z_plus = jnp.where(seven, roll_lane(near_y, -1), roll_lane(ey, -1))
            z_minus = jnp.where(zero, roll_lane(near_y, 1), roll_lane(ey, 1))
            after, before = tile(ey_ref, at_edge + TG), tile(ey_ref, at_edge - TG)
            put(target[3], out_edge, apply(3, ey, after, before, ey_plus, ey_minus, z_plus, z_minus))
        return carry

    lax.fori_loop(0, count * TG, block, 0)


def copy_tiles(source, at, target, to, count):
    for i in range(count):
        put(target, to + i, tile(source, at + i))


def first_two_kernel(
    sizes,
    wells_ref,
    main_ref,
    edge_ref,
    my_ref,
    ey_ref,
    right_main_ref,
    left_main_ref,
    left_ref,
    right_ref,
    coef_ref,
    keep_ref,
    send_ref,
    block_2_ref,
    my_2_ref,
    em_2_ref,
    ey_2_ref,
    to_left_ref,
    to_right_ref,
    conduct_ref,
    given_ref,
    main_0,
    my_0,
    em_0,
    ey_0,
    main_1,
    my_1,
    em_1,
    ey_1,
):
    row = iota_row()
    for p in range(2):
        copy_tiles(main_ref, SLOT * p, main_0, HALF * (2 + p), HALF)
        copy_tiles(my_ref, SLOT * p, my_0, HALF * (2 + p), HALF)
        copy_tiles(edge_ref, TG * p, em_0, TG * (2 + p), TG)
        copy_tiles(ey_ref, TG * p, ey_0, TG * (2 + p), TG)
    extras = {2: (main_ref, HALF, my_ref, HALF, edge_ref, NE - 1, ey_ref, NE - 1, 0)}
    extras[3] = (main_ref, SLOT + HALF, my_ref, SLOT + HALF, edge_ref, NE - 1, ey_ref, NE - 1, NEXTRA)
    for whole, ref, adjacent, second, p in ((left_main_ref, left_ref, 1, 0, 1), (right_main_ref, right_ref, 4, 5, 0)):
        copy_tiles(whole, 0, main_0, HALF * adjacent, HALF)
        copy_tiles(whole, SLOT, main_0, HALF * second, HALF)
        for i in range(HALF // 4):
            three = [tile(ref, 3 * i + k) for k in range(3)]
            for k in range(3):
                put(my_0, HALF * adjacent + 4 * i + k, three[k])
            fourth = jnp.where(row < 6, roll_row(three[1], 1), roll_row(three[2], 3))
            fourth = jnp.where(row < 4, roll_row(three[1], -1), fourth)
            fourth = jnp.where(row < 2, roll_row(three[0], -3), fourth)
            put(my_0, HALF * adjacent + 4 * i + 3, fourth)
        for i in range(HALF // 2):
            value = tile(ref, A_SECOND + i)
            put(my_0, HALF * second + 2 * i, value)
            put(my_0, HALF * second + 2 * i + 1, roll_row(value, 4))
        for plane, at in ((adjacent, p), (second, 1 - p)):
            copy_tiles(ref, A_EDGE + TG * at, em_0, TG * plane, TG)
            copy_tiles(ref, A_EDGE + NE + TG * at, ey_0, TG * plane, TG)
        em_at, ey_at = A_EDGE + NE - 1, A_EDGE + 2 * NE - 1
        extras[adjacent] = (whole, HALF, ref, A_EXTRA, ref, em_at, ref, ey_at, NEXTRA * p)
        for part, value in enumerate(
            (
                tile(whole, SLOT + HALF),
                tile(ref, A_SECOND + HALF // 2),
                roll_lane(tile(ref, em_at), -8 * (NEXTRA * (1 - p) + 4)),
                roll_lane(tile(ref, ey_at), -8 * (NEXTRA * (1 - p) + 4)),
            )
        ):
            put(conduct_ref, 4 * second + part, value)
    for plane, (a, a_at, b, b_at, c, c_at, d, d_at, q) in extras.items():
        for e in range(NEXTRA):
            values = (
                tile(a, a_at + e),
                tile(b, b_at + e),
                roll_lane(tile(c, c_at), -8 * (q + e)),
                roll_lane(tile(d, d_at), -8 * (q + e)),
            )
            for part, value in enumerate(values):
                if e == NEXTRA - 1:
                    put(conduct_ref, 4 * plane + part, value)
                else:
                    put(given_ref, ((plane - 1) * 4 + e) * 4 + part, value)
    plane_coefficients(sizes, wells_ref, conduct_ref, given_ref, coef_ref)
    step((main_0, my_0, em_0, ey_0), (main_1, my_1, em_1, ey_1), coef_ref, 1, 4, -1, -1)
    step((main_1, my_1, em_1, ey_1), (block_2_ref, my_2_ref, em_2_ref, ey_2_ref), coef_ref, 1, 2, 0, -1)
    for p, (adjacent, second) in enumerate(((to_left_ref, to_right_ref), (to_right_ref, to_left_ref))):
        for i in range(HALF):
            value = tile(block_2_ref, HALF * p + i)
            put(adjacent, i, value)
            put(second, B_SECOND + i, value)
        for i in range(HALF // 4):
            value = tile(my_2_ref, HALF * p + 4 * i)
            for k in range(1, 4):
                at_row = ((row + (1 - 2 * k)) & 7) < 2
                value = jnp.where(at_row, roll_row(tile(my_2_ref, HALF * p + 4 * i + k), 2 * k), value)
            put(adjacent, B_MY + i, value)
        copy_tiles(em_2_ref, TG * p, adjacent, B_EDGE, TG)
    by_plane(((main_1, HALF), (block_2_ref, 0)), keep_ref, send_ref)


def by_plane(levels, keep_ref, send_ref):
    mine, other = core() * HALF, (1 - core()) * HALF
    for level, (ref, base) in enumerate(levels):
        for i in range(HALF):
            put(keep_ref, HALF * level + i, tile(ref, base + mine + i))
            put(send_ref, HALF * level + i, tile(ref, base + other + i))


def last_two_kernel(
    coef_ref,
    block_2_ref,
    my_2_ref,
    em_2_ref,
    ey_2_ref,
    left_ref,
    right_ref,
    _,
    keep_ref,
    send_ref,
    main_2,
    my_2,
    em_2,
    ey_2,
    main_3,
    my_3,
    em_3,
    main_4,
):
    copy_tiles(block_2_ref, 0, main_2, 2 * HALF, 2 * HALF)
    copy_tiles(my_2_ref, 0, my_2, 2 * HALF, 2 * HALF)
    copy_tiles(em_2_ref, 0, em_2, 2 * TG, 2 * TG)
    copy_tiles(ey_2_ref, 0, ey_2, 2 * TG, 2 * TG)
    for ref, adjacent, second in ((left_ref, 1, 0), (right_ref, 4, 5)):
        copy_tiles(ref, 0, main_2, HALF * adjacent, HALF)
        for i in range(HALF // 4):
            value = tile(ref, B_MY + i)
            for k in range(4):
                put(my_2, HALF * adjacent + 4 * i + k, roll_row(value, -2 * k))
        copy_tiles(ref, B_EDGE, em_2, TG * adjacent, TG)
        copy_tiles(ref, B_SECOND, main_2, HALF * second, HALF)
    source, target = (main_2, my_2, em_2, ey_2), (main_3, my_3, em_3, None)
    for plane in (1, 4):
        step(source, target, coef_ref, plane, 1, -1, -1, False, False, False)
    step(source, target, coef_ref, 2, 2, -1, -1, True, True, False)
    step((main_3, my_3, em_3, None), (main_4, None, None, None), coef_ref, 1, 2, 0, -1, False, False, False)
    by_plane(((main_3, HALF), (main_4, 0)), keep_ref, send_ref)


PAIRS = (
    ((0, 0), (0, 1)),
    ((0, 2), (0, 3)),
    ((1, 1), (1, 2)),
    ((1, 3), (1, 4)),
    ((2, 2), (2, 3)),
    ((3, 3), (3, 4)),
    ((4, 4), (2, 4)),
    ((0, 4), None),
)


def two_parts(values):
    high = values.astype(jnp.bfloat16)
    return high, (values - high.astype(jnp.float32)).astype(jnp.bfloat16)


def three_products(first, second, dims):
    def dot(a, b):
        return lax.dot_general(a, b, (dims, ((), ())), preferred_element_type=jnp.float32)

    return dot(first[0], second[0]) + (dot(first[0], second[1]) + dot(first[1], second[0]))


def dot_tn(first, second):
    return lax.dot_general(first, second, (((0,), (0,)), ((), ())), precision=HI, preferred_element_type=jnp.float32)


def dot_nn(first, second):
    return lax.dot_general(first, second, (((1,), (0,)), ((), ())), precision=HI, preferred_element_type=jnp.float32)


def fill_levels(keep_ref, got_ref, basis_ref, base):
    mine, other = core() * HALF, (1 - core()) * HALF
    for y in range(8):
        lanes = slice(128 * y, 128 * (y + 1))
        for level in range(2):
            at = pl.ds(8 * HALF * level + y, HALF, stride=8)
            rows = base + M * level
            basis_ref[pl.ds(pl.multiple_of(rows + mine, 8), HALF), lanes] = keep_ref[at, :]
            basis_ref[pl.ds(pl.multiple_of(rows + other, 8), HALF), lanes] = got_ref[at, :]


def early_gram_kernel(block_0, keep_ref, got_ref, high_ref, low_ref, full_ref, basis_ref):
    for y in range(8):
        basis_ref[0:M, 128 * y : 128 * (y + 1)] = block_0[pl.ds(y, M, stride=8), :]
    fill_levels(keep_ref, got_ref, basis_ref, M)
    parts = two_parts(basis_ref[...])
    high_ref[...], low_ref[...] = parts
    full_ref[...] = three_products(parts, parts, ((1,), (1,)))


def gram_kernel(keep_ref, got_ref, early_high, early_low, early_full, high_ref, low_ref, gram_ref, basis_ref):
    fill_levels(keep_ref, got_ref, basis_ref, 0)
    parts = two_parts(basis_ref[...])
    high_ref[...], low_ref[...] = parts
    among = three_products(parts, parts, ((1,), (1,)))
    across = three_products((early_high[...], early_low[...]), parts, ((1,), (1,)))
    for index, pair in enumerate(PAIRS):
        for half, at in enumerate(pair):
            if at is None:
                value = jnp.zeros((M, M), jnp.float32)
            else:
                first, second = (slice(M * k, M * k + M) for k in at)
                if at[1] < 3:
                    value = early_full[first, second]
                else:
                    source, shift = (among, 3 * M) if at[0] >= 3 else (across, 0)
                    value = source[first.start - shift : first.stop - shift, second.start - 3 * M : second.stop - 3 * M]
            gram_ref[M * index : M * (index + 1), M * half : M * (half + 1)] = value


def eliminate(matrix, wanted):
    both = jnp.concatenate([matrix, wanted], axis=1)
    tiles = [both[8 * i : 8 * i + 8, :] for i in range(M // 8)]
    rows = iota_row()

    def column(value, at):
        return jnp.broadcast_to(value[:, at : at + 1], (8, 128))

    def block(_, tiles):
        tiles = list(tiles)
        columns = [column(tiles[0], b) for b in range(8)]
        row = [jnp.broadcast_to(tiles[0][a : a + 1, :], (8, 128)) for a in range(8)]
        small = [[jnp.broadcast_to(columns[b][a : a + 1, :], (8, 128)) for b in range(8)] for a in range(8)]
        for p in range(8):
            inverse = 1.0 / small[p][p]
            for a in range(p + 1, 8):
                factor = small[p][a] * inverse
                row[a] = row[a] - factor * row[p]
                for b in range(a, 8):
                    small[a][b] = small[a][b] - factor * small[p][b]
            row[p] = row[p] * inverse
            for b in range(p + 1, 8):
                small[p][b] = small[p][b] * inverse
        for p in range(7, 0, -1):
            for a in range(p):
                row[a] = row[a] - small[a][p] * row[p]
        for j in range(1, M // 8):
            value = tiles[j]
            for b in range(8):
                value = value - column(tiles[j], b) * row[b]
            tiles[j] = value
        value = row[0]
        for b in range(1, 8):
            value = jnp.where(rows == b, row[b], value)
        tiles[0] = value
        return tuple(roll_lane(t, -8) for t in tiles[1:] + tiles[:1])

    tiles = lax.fori_loop(0, M // 8, block, tuple(tiles), unroll=1)
    return jnp.concatenate(tiles, axis=0)[:, :M]


def apply_levels(blocks):
    out = [SHIFT * b for b in blocks] + [None]
    for j, b in enumerate(blocks):
        out[j + 1] = SCALE * b if out[j + 1] is None else out[j + 1] + SCALE * b
    return out


def pad_levels(blocks, count):
    return list(blocks) + [jnp.zeros((M, M), jnp.float32)] * (count - len(blocks))


def final_kernel(gram_ref, early_high, early_low, high_ref, low_ref, field_ref, resid_ref, full_ref):
    for index, pair in enumerate(PAIRS):
        for half, at in enumerate(pair):
            if at is None:
                continue
            value = gram_ref[M * index : M * (index + 1), M * half : M * (half + 1)]
            full_ref[M * at[0] : M * at[0] + M, M * at[1] : M * at[1] + M] = value
            if at[0] != at[1]:
                full_ref[M * at[1] : M * at[1] + M, M * at[0] : M * at[0] + M] = value.T
    eye = jnp.where(
        lax.broadcasted_iota(jnp.int32, (M, M), 0) == lax.broadcasted_iota(jnp.int32, (M, M), 1), 1.0, 0.0
    ).astype(jnp.float32)

    def gram(levels, blocks):
        count = M * levels
        return dot_nn(full_ref[0:count, 0 : M * len(blocks)], jnp.concatenate(blocks, axis=0))

    def minimal(half, second):
        levels = len(second)
        product = gram(levels, second)
        cross = sum(product[M * j : M * j + M] * b for j, b in enumerate(half))
        square = sum(product[M * j : M * j + M] * b for j, b in enumerate(second))
        def total(values):
            return jnp.sum(jnp.sum(values, axis=0, keepdims=True), axis=1, keepdims=True)

        return total(cross) / total(square), product[0:M]

    image_gram = SHIFT * full_ref[0:M, 0:M] + SCALE * full_ref[0:M, M : 2 * M]
    inverse = eliminate(dot_tn(image_gram, image_gram), image_gram.T)
    alpha = dot_nn(inverse, full_ref[0:M, 0:M])
    half = [eye - SHIFT * alpha, -SCALE * alpha]
    second = apply_levels(half)
    omega, second_gram = minimal(half, second)
    field = [alpha + omega * half[0], omega * half[1]]
    resid = [half[0] - omega * second[0], half[1] - omega * second[1], -omega * second[2]]
    beta = -dot_nn(inverse, second_gram)
    direct = [
        resid[0] + (1.0 - omega * SHIFT) * beta,
        resid[1] - (omega * SCALE) * beta,
        resid[2],
    ]
    image = apply_levels(direct)
    stacked = jnp.concatenate(
        [jnp.concatenate(image, axis=0), jnp.concatenate(pad_levels(resid, 4), axis=0)], axis=1
    )
    both = dot_nn(full_ref[0:M, 0 : 4 * M], stacked)
    image_gram, resid_gram = both[:, 0:M], both[:, M:]
    inverse = eliminate(dot_tn(image_gram, image_gram), image_gram.T)
    alpha = dot_nn(inverse, resid_gram)
    product = dot_nn(jnp.concatenate(image + direct, axis=0), alpha)
    half = [r - product[M * j : M * j + M] for j, r in enumerate(pad_levels(resid, 4))]
    second = apply_levels(half)
    omega, _ = minimal(half, second)
    field = pad_levels(field, 4)
    moved = [product[M * (4 + j) : M * (5 + j)] for j in range(3)] + [None]
    field = [
        f + omega * h + (0.0 if m is None else m) for f, h, m in zip(field, half, moved)
    ]
    field = pad_levels(field, 5)
    resid = [h - omega * s for h, s in zip(pad_levels(half, 5), second)]
    coefs = jnp.concatenate([jnp.concatenate(field, axis=0), jnp.concatenate(resid, axis=0)], axis=1)
    coefs = coefs.T
    result = three_products(two_parts(coefs[:, 0 : 3 * M]), (early_high[...], early_low[...]), ((1,), (0,)))
    result = result + three_products(two_parts(coefs[:, 3 * M :]), (high_ref[...], low_ref[...]), ((1,), (0,)))
    for y in range(8):
        field_ref[pl.ds(y, M, stride=8), :] = result[0:M, 128 * y : 128 * (y + 1)]
        resid_ref[pl.ds(y, M, stride=8), :] = result[M:, 128 * y : 128 * (y + 1)]


VMEM = pl.BlockSpec(memory_space=pltpu.VMEM)
SMEM = pl.BlockSpec(memory_space=pltpu.SMEM)


def f32(*shape):
    return jax.ShapeDtypeStruct(shape, jnp.float32)


def call(kernel, name, outs, specs, scratch=()):
    return pl.pallas_call(
        kernel,
        name=name,
        out_shape=outs,
        in_specs=specs,
        out_specs=tuple(VMEM for _ in outs) if isinstance(outs, tuple) else VMEM,
        scratch_shapes=list(scratch),
        compiler_params=pltpu.CompilerParams(vmem_limit_bytes=32 * 1024 * 1024),
    )


def from_sides(axis, up, down, by=1):
    count = lax.axis_size(axis)
    lower = lax.ppermute(up, axis, [(i, i + by) for i in range(count - by)])
    upper = lax.ppermute(down, axis, [(i + by, i) for i in range(count - by)])
    return lower, upper


def spread(values, axes):
    count = lax.axis_size(axes)
    return lax.all_to_all(jnp.broadcast_to(values, (count, *values.shape)), axes, 0, 0)


def in_hbm(values):
    return pltpu.with_memory_space_constraint(values, pltpu.HBM)


def other_core(values):
    count = lax.axis_size("gx")
    return lax.ppermute(values, "gx", [(i, i ^ 1) for i in range(count)])


def tiles(count):
    return f32(8 * count, 128)


def scratch(*counts):
    return [pltpu.VMEM((8 * count, 128), jnp.float32) for count in counts]


def per_device(right_side, velocity, decay_rate, perm_class, conductivity, well_cells, well_rate):
    sizes = (lax.axis_size("gx"), 8 * lax.axis_size("gy"), 128 * lax.axis_size("gz"))
    block_0 = right_side.reshape(8 * M, 128)
    any_space = pl.BlockSpec(memory_space=pltpu.HBM)

    send, keep = call(
        pack_kernel,
        "pack",
        (tiles(SLOT), tiles(SLOT)),
        [any_space] * 5,
        [
            pltpu.VMEM((8, 128), jnp.int32),
            pltpu.SMEM(conductivity.shape, jnp.float32),
            pltpu.SemaphoreType.DMA((6,)),
        ],
    )(
        in_hbm(block_0),
        in_hbm(velocity.reshape(24, 128)),
        in_hbm(decay_rate.reshape(8, 128)),
        in_hbm(perm_class.reshape(8, 128)),
        in_hbm(conductivity),
    )
    got = other_core(send)
    wells = call(functools.partial(wells_kernel, sizes), "wells", tiles(16), [SMEM, SMEM])(well_cells, well_rate)
    main, zmsg, to_left, to_right = call(
        zmsg_kernel, "zmsg", (tiles(2 * SLOT), tiles(NE), tiles(EARLY_TILES), tiles(EARLY_TILES)), [VMEM] * 2
    )(keep, got)
    left_main, right_main = from_sides("gx", to_right, to_left, 2)
    low, high = from_sides("gz", zmsg, zmsg)
    up, down, edge = call(ymsg_kernel, "ymsg", (tiles(YPAIRS), tiles(YPAIRS), tiles(NE)), [VMEM] * 3)(
        main, low, high
    )
    below, above = from_sides("gy", up, down)
    my, ey, to_left, to_right = call(
        xmsg_kernel, "xmsg", (tiles(2 * SLOT), tiles(NE), tiles(A_TILES), tiles(A_TILES)), [VMEM] * 3
    )(edge, below, above)
    left, right = from_sides("gx", to_right, to_left, 2)
    coef, keep, send, block_2, my, em, ey, to_left, to_right = call(
        functools.partial(first_two_kernel, sizes),
        "first_two",
        (
            tiles(4 * 28),
            tiles(2 * HALF),
            tiles(2 * HALF),
            tiles(M),
            tiles(M),
            tiles(2 * TG),
            tiles(2 * TG),
            tiles(B_TILES),
            tiles(B_TILES),
        ),
        [VMEM] * 9,
        scratch(24, 64, 6 * HALF, 6 * HALF, 6 * TG, 6 * TG, 4 * HALF, 4 * HALF, 4 * TG, 4 * TG),
    )(wells, main, edge, my, ey, right_main, left_main, left, right)
    left, right = from_sides("gx", to_right, to_left, 2)
    got = other_core(send)

    def rows(levels):
        return jax.ShapeDtypeStruct((levels * M, 1024), jnp.bfloat16)

    early_high, early_low, early_full = call(
        early_gram_kernel,
        "early_gram",
        (rows(3), rows(3), f32(3 * M, 3 * M)),
        [VMEM] * 3,
        [pltpu.VMEM((3 * M, 1024), jnp.float32)],
    )(block_0, keep, got)
    keep, send = call(
        last_two_kernel,
        "last_two",
        (tiles(2 * HALF), tiles(2 * HALF)),
        [VMEM] * 7 + [pl.BlockSpec(memory_space=pl.ANY)],
        scratch(6 * HALF, 6 * HALF, 6 * TG, 6 * TG, 4 * HALF, 4 * HALF, 4 * TG, 2 * HALF),
    )(coef, block_2, my, em, ey, left, right, early_full)
    got = other_core(send)
    high, low, gram = call(
        gram_kernel,
        "gram",
        (rows(2), rows(2), f32(8 * M, 128)),
        [VMEM] * 5,
        [pltpu.VMEM((2 * M, 1024), jnp.float32)],
    )(keep, got, early_high, early_low, early_full)

    plane = ("gz", "gy")
    count = lax.axis_size(plane)
    gram = lax.all_to_all(gram.reshape(count, -1, 128), plane, 0, 0)
    gram = jnp.sum(gram, axis=0)
    gram = jnp.sum(spread(gram, "gx"), axis=0)
    gram = spread(gram, plane).reshape(8 * M, 128)
    field, resid = call(
        final_kernel,
        "final",
        (f32(8 * M, 128), f32(8 * M, 128)),
        [VMEM] * 5,
        [pltpu.VMEM((LEVELS * M, LEVELS * M), jnp.float32)],
    )(gram, early_high, early_low, high, low)
    return field.reshape(right_side.shape), resid.reshape(right_side.shape)


def solution(mesh):
    placed = (
        P(None, "gx", "gy", "gz"),
        P(None, "gx", "gy", "gz"),
        P("gx", "gy", "gz"),
        P("gx", "gy", "gz"),
        P(),
        P(),
        P(),
    )
    return jax.shard_map(
        per_device,
        mesh=mesh,
        in_specs=placed,
        out_specs=(P(None, "gx", "gy", "gz"), P(None, "gx", "gy", "gz")),
        check_vma=False,
    )
```

```python
import functools

import jax
import jax.numpy as jnp
from jax import lax
from jax.experimental import pallas as pl
from jax.experimental.pallas import tpu as pltpu
from jax.sharding import PartitionSpec as P

SHIFT = 7.5
SCALE = 3.0
LEVELS = 5
M = 64
HALF = M // 2
NEXTRA = 5
SLOT = HALF + NEXTRA
GROUPS = 16
TG = HALF // GROUPS
NE = 2 * TG + 1
HI = lax.Precision.HIGHEST


def iota_row():
    return lax.broadcasted_iota(jnp.int32, (8, 128), 0)


def iota_lane():
    return lax.broadcasted_iota(jnp.int32, (8, 128), 1)


def roll_lane(tile, shift):
    shift = shift % 128
    return tile if shift == 0 else pltpu.roll(tile, shift, 1)


def roll_row(tile, shift):
    shift = shift % 8
    return tile if shift == 0 else pltpu.roll(tile, shift, 0)


def swap_shift(first, second, roll, shift, mask):
    first, second = roll(first, shift), roll(second, shift)
    return jnp.where(mask, second, first), jnp.where(mask, first, second)


def tile(ref, index):
    if isinstance(index, int):
        return ref[8 * index : 8 * index + 8, :]
    return ref[pl.ds(pl.multiple_of(index * 8, 8), 8), :]


def put(ref, index, value):
    if isinstance(index, int):
        ref[8 * index : 8 * index + 8, :] = value
    else:
        ref[pl.ds(pl.multiple_of(index * 8, 8), 8), :] = value


def group_mask(lane, q):
    at = (lane + (4 - 8 * q)) & 127
    return at < 8


def core():
    return lax.rem(lax.axis_index("gx"), 2)


def pack_kernel(right_hbm, vel_hbm, decay_hbm, class_hbm, table_hbm, send_ref, keep_ref, class_ref, table_ref, sems):
    mine = pl.multiple_of(core() * 8 * HALF, 8)
    other = pl.multiple_of((1 - core()) * 8 * HALF, 8)
    copies = [
        (class_hbm, class_ref),
        (table_hbm, table_ref),
        (vel_hbm, keep_ref.at[pl.ds(8 * HALF, 24), :]),
        (decay_hbm, keep_ref.at[pl.ds(8 * (HALF + 3), 8), :]),
        (right_hbm.at[pl.ds(mine, 8 * HALF), :], keep_ref.at[pl.ds(0, 8 * HALF), :]),
        (right_hbm.at[pl.ds(other, 8 * HALF), :], send_ref.at[pl.ds(0, 8 * HALF), :]),
    ]
    copies = [pltpu.make_async_copy(src, dst, sems.at[i]) for i, (src, dst) in enumerate(copies)]
    for copy in copies:
        copy.start()
    for copy in copies:
        copy.wait()
    classes = class_ref[...]
    conduct = jnp.zeros((8, 128), jnp.float32)
    for index in range(table_ref.shape[0]):
        conduct = jnp.where(classes == index, table_ref[index], conduct)
    put(keep_ref, HALF + 4, conduct)
    put(send_ref, HALF + 4, conduct)
    for e in range(4):
        put(send_ref, HALF + e, tile(keep_ref, HALF + e))


EARLY_TILES = SLOT + HALF + 1


def zmsg_kernel(keep_ref, got_ref, main_ref, zmsg_ref, to_left_ref, to_right_ref):
    lane = iota_lane()
    mine, other = core() * SLOT, (1 - core()) * SLOT
    for i in range(SLOT):
        put(main_ref, mine + i, tile(keep_ref, i))
        put(main_ref, other + i, tile(got_ref, i))

    def packed(indices):
        total = jnp.zeros((8, 128), jnp.float32)
        for q, index in enumerate(indices):
            total = jnp.where(group_mask(lane, q), roll_lane(tile(main_ref, index), 8 * q), total)
        return total

    for p in range(2):
        for t in range(TG):
            put(zmsg_ref, TG * p + t, packed([SLOT * p + GROUPS * t + q for q in range(GROUPS)]))
    put(zmsg_ref, NE - 1, packed([SLOT * p + HALF + e for p in range(2) for e in range(NEXTRA)]))
    for p, (adjacent, second) in enumerate(((to_left_ref, to_right_ref), (to_right_ref, to_left_ref))):
        for i in range(SLOT):
            value = tile(main_ref, SLOT * p + i)
            put(adjacent, i, value)
            if i < HALF or i == SLOT - 1:
                put(second, SLOT + min(i, HALF), value)


YPAIRS = (2 * SLOT + NE + 1) // 2


def ymsg_kernel(main_ref, low_ref, high_ref, up_ref, down_ref, edge_ref):
    row, lane = iota_row(), iota_lane()
    edges = []
    for t in range(NE):
        edge = jnp.where((lane & 7) >= 4, tile(low_ref, t), tile(high_ref, t))
        put(edge_ref, t, edge)
        edges.append(edge)

    def source(index):
        if index < 2 * SLOT:
            return tile(main_ref, index)
        return edges[min(index - 2 * SLOT, NE - 1)]

    lower = row < 4
    for g in range(YPAIRS):
        first, second = source(2 * g), roll_row(source(2 * g + 1), 4)
        put(up_ref, g, jnp.where(lower, second, first))
        put(down_ref, g, jnp.where(lower, first, second))


A_EXTRA = HALF // 4 * 3
A_SECOND = A_EXTRA + NEXTRA
A_EDGE = A_SECOND + HALF // 2 + 1
A_TILES = A_EDGE + 2 * NE
B_MY = HALF
B_EDGE = B_MY + HALF // 4
B_SECOND = B_EDGE + TG
B_TILES = B_SECOND + HALF


def xmsg_kernel(edge_ref, below_ref, above_ref, my_ref, ey_ref, to_left_ref, to_right_ref):
    row = iota_row()
    lower = row < 4
    keep_2 = (row < 2) | (row >= 6)
    for g in range(YPAIRS):
        below, above = tile(below_ref, g), tile(above_ref, g)
        pair = (jnp.where(lower, above, below), roll_row(jnp.where(lower, below, above), 4))
        for half in range(2):
            index = 2 * g + half
            if index < 2 * SLOT:
                put(my_ref, index, pair[half])
                p, i = divmod(index, SLOT)
                if i >= HALF:
                    put((to_left_ref, to_right_ref)[p], A_EXTRA + i - HALF, pair[half])
                if i == SLOT - 1:
                    put((to_right_ref, to_left_ref)[p], A_SECOND + HALF // 2, pair[half])
            elif index < 2 * SLOT + NE:
                put(ey_ref, index - 2 * SLOT, pair[half])
                for ref in (to_left_ref, to_right_ref):
                    put(ref, A_EDGE + NE + index - 2 * SLOT, pair[half])
    free = (row == 3) | (row == 4)
    for p, (adjacent, second) in enumerate(((to_left_ref, to_right_ref), (to_right_ref, to_left_ref))):
        for i in range(HALF // 4):
            first = SLOT * p + 4 * i
            fourth = tile(my_ref, first + 3)
            moved = (
                roll_row(fourth, 3),
                jnp.where(row < 4, roll_row(fourth, 1), roll_row(fourth, -1)),
                roll_row(fourth, -3),
            )
            for k in range(3):
                put(adjacent, 3 * i + k, jnp.where(free, moved[k], tile(my_ref, first + k)))
        for i in range(HALF // 2):
            value = jnp.where(
                keep_2,
                tile(my_ref, SLOT * p + 2 * i),
                roll_row(tile(my_ref, SLOT * p + 2 * i + 1), 4),
            )
            put(second, A_SECOND + i, value)
    for t in range(NE):
        value = tile(edge_ref, t)
        put(to_left_ref, A_EDGE + t, value)
        put(to_right_ref, A_EDGE + t, value)


def part_places():
    row, lane = iota_row(), iota_lane()
    at_y, at_z = lax.axis_index("gy"), lax.axis_index("gz")
    y_main = at_y * 8 + row
    y_my = at_y * 8 + jnp.where(row < 4, row + 8, row - 8)
    z_main = at_z * 128 + lane
    z_edge = at_z * 128 + jnp.where(lane < 64, lane + 128, lane - 128)
    return ((y_main, z_main), (y_my, z_main), (y_main, z_edge), (y_my, z_edge))


def wells_kernel(sizes, cells_ref, rate_ref, wells_ref):
    size_x, size_y, size_z = sizes
    first_x = lax.axis_index("gx") - core() - 1
    for part, (y_at, z_at) in enumerate(part_places()):
        flats = [((first_x + s) * size_y + y_at) * size_z + z_at for s in range(4)]
        wells = [jnp.zeros((8, 128), jnp.float32)] * 4
        for w in range(cells_ref.shape[0]):
            for s in range(4):
                wells[s] = wells[s] + jnp.where(flats[s] == cells_ref[w], rate_ref[w], 0.0)
        for s in range(4):
            put(wells_ref, s * 4 + part, wells[s])


def plane_coefficients(sizes, wells_ref, conduct_ref, given_ref, coef_ref):
    row, lane = iota_row(), iota_lane()
    size_x, size_y, size_z = sizes
    first_x = lax.axis_index("gx") - core() - 1
    where = part_places()

    def shift_y(four, shift, mask):
        main, my = swap_shift(four[0], four[1], roll_row, shift, mask)
        edge, ey = swap_shift(four[2], four[3], roll_row, shift, mask)
        return [main, my, edge, ey]

    def shift_z(four, shift, mask):
        main, edge = swap_shift(four[0], four[2], roll_lane, shift, mask)
        my, ey = swap_shift(four[1], four[3], roll_lane, shift, mask)
        return [main, my, edge, ey]

    def plane(s, carry):
        center = [tile(conduct_ref, (s + 1) * 4 + part) for part in range(4)]
        before = [tile(conduct_ref, s * 4 + part) for part in range(4)]
        after = [tile(conduct_ref, (s + 2) * 4 + part) for part in range(4)]
        plus = [after, shift_y(center, -1, row == 7), shift_z(center, -1, lane == 127)]
        minus = [before, shift_y(center, 1, row == 0), shift_z(center, 1, lane == 0)]
        at_x = first_x + s
        x_inside = (at_x >= 0) & (at_x < size_x)
        for part, (y_at, z_at) in enumerate(where):
            inside = (y_at >= 0) & (y_at < size_y) & (z_at >= 0) & (z_at < size_z) & x_inside
            if part >= 2:
                inside = inside & ((lane < 4) | (lane >= 124))
            given = [tile(given_ref, (s * 4 + e) * 4 + part) for e in range(4)]
            diagonal = given[3] + tile(wells_ref, s * 4 + part)
            values = []
            for d in range(3):
                plus_face = 0.5 * (center[part] + plus[d][part])
                minus_face = 0.5 * (center[part] + minus[d][part])
                diagonal = diagonal + (given[d] + plus_face + minus_face)
                values += [(given[d] + plus_face) * (-1.0 / SCALE), minus_face * (-1.0 / SCALE)]
            for index, value in enumerate([(diagonal - SHIFT) * (1.0 / SCALE)] + values):
                value = jnp.where(inside, value, 0.0)
                if part >= 2:
                    for shift in (8, 16, 32, 64):
                        value = value + roll_lane(value, shift)
                put(coef_ref, (s * 7 + index) * 4 + part, value)
        return carry

    lax.fori_loop(0, 4, plane, 0, unroll=True)


def step(source, target, coef_ref, first, count, coef_shift, out_shift, with_my=True, with_em=True, with_ey=True):
    main_ref, my_ref, em_ref, ey_ref = source
    row, lane = iota_row(), iota_lane()
    row_0, row_7 = row == 0, row == 7
    lane_0, lane_127 = lane == 0, lane == 127

    def block(i, carry):
        s, t = first + lax.div(i, TG), lax.rem(i, TG)

        def apply(part, center, after, before, y_plus, y_minus, z_plus, z_minus):
            def coef(index):
                return tile(coef_ref, ((s + coef_shift) * 7 + index) * 4 + part)

            total = coef(0) * center + (coef(1) * after + coef(2) * before)
            total = total + (coef(3) * y_plus + coef(4) * y_minus)
            return total + (coef(5) * z_plus + coef(6) * z_minus)

        at_field, at_edge = s * HALF + t * GROUPS, s * TG + t
        out_field, out_edge = (s + out_shift) * HALF + t * GROUPS, (s + out_shift) * TG + t
        em = tile(em_ref, at_edge)
        ey = tile(ey_ref, at_edge) if with_em or with_my else None
        near_m = jnp.zeros((8, 128), jnp.float32)
        near_y = jnp.zeros((8, 128), jnp.float32)
        for q in range(GROUPS):
            f = at_field + q
            main, my = tile(main_ref, f), tile(my_ref, f)
            beside = roll_lane(em, -8 * q)
            z_plus = roll_lane(jnp.where(lane_0, beside, main), -1)
            z_minus = roll_lane(jnp.where(lane_127, beside, main), 1)
            y_plus, my_plus = swap_shift(main, my, roll_row, -1, row_7)
            y_minus, my_minus = swap_shift(main, my, roll_row, 1, row_0)
            after, before = tile(main_ref, f + HALF), tile(main_ref, f - HALF)
            put(target[0], out_field + q, apply(0, main, after, before, y_plus, y_minus, z_plus, z_minus))
            at = ((lane + (1 - 8 * q)) & 127) < 2
            if with_em:
                near_m = jnp.where(at, roll_lane(main, 8 * q), near_m)
            if with_ey:
                near_y = jnp.where(at, roll_lane(my, 8 * q), near_y)
            if with_my:
                beside = roll_lane(ey, -8 * q)
                z_plus = roll_lane(jnp.where(lane_0, beside, my), -1)
                z_minus = roll_lane(jnp.where(lane_127, beside, my), 1)
                after, before = tile(my_ref, f + HALF), tile(my_ref, f - HALF)
                put(target[1], out_field + q, apply(1, my, after, before, my_plus, my_minus, z_plus, z_minus))
        seven, zero = (lane & 7) == 7, (lane & 7) == 0
        if with_em:
            em_plus, ey_plus = swap_shift(em, ey, roll_row, -1, row_7)
            em_minus, ey_minus = swap_shift(em, ey, roll_row, 1, row_0)
            z_plus = jnp.where(seven, roll_lane(near_m, -1), roll_lane(em, -1))
            z_minus = jnp.where(zero, roll_lane(near_m, 1), roll_lane(em, 1))
            after, before = tile(em_ref, at_edge + TG), tile(em_ref, at_edge - TG)
            put(target[2], out_edge, apply(2, em, after, before, em_plus, em_minus, z_plus, z_minus))
        if with_ey:
            z_plus = jnp.where(seven, roll_lane(near_y, -1), roll_lane(ey, -1))
            z_minus = jnp.where(zero, roll_lane(near_y, 1), roll_lane(ey, 1))
            after, before = tile(ey_ref, at_edge + TG), tile(ey_ref, at_edge - TG)
            put(target[3], out_edge, apply(3, ey, after, before, ey_plus, ey_minus, z_plus, z_minus))
        return carry

    lax.fori_loop(0, count * TG, block, 0)


def copy_tiles(source, at, target, to, count):
    for i in range(count):
        put(target, to + i, tile(source, at + i))


def first_two_kernel(
    sizes,
    wells_ref,
    main_ref,
    edge_ref,
    my_ref,
    ey_ref,
    right_main_ref,
    left_main_ref,
    right_ref,
    left_ref,
    coef_ref,
    keep_ref,
    send_ref,
    block_2_ref,
    my_2_ref,
    em_2_ref,
    ey_2_ref,
    to_left_ref,
    to_right_ref,
    conduct_ref,
    given_ref,
    main_0,
    my_0,
    em_0,
    ey_0,
    main_1,
    my_1,
    em_1,
    ey_1,
):
    row = iota_row()
    for p in range(2):
        copy_tiles(main_ref, SLOT * p, main_0, HALF * (2 + p), HALF)
        copy_tiles(my_ref, SLOT * p, my_0, HALF * (2 + p), HALF)
        copy_tiles(edge_ref, TG * p, em_0, TG * (2 + p), TG)
        copy_tiles(ey_ref, TG * p, ey_0, TG * (2 + p), TG)
    extras = {2: (main_ref, HALF, my_ref, HALF, edge_ref, NE - 1, ey_ref, NE - 1, 0)}
    extras[3] = (main_ref, SLOT + HALF, my_ref, SLOT + HALF, edge_ref, NE - 1, ey_ref, NE - 1, NEXTRA)
    for whole, ref, adjacent, second, p in ((left_main_ref, left_ref, 1, 0, 1), (right_main_ref, right_ref, 4, 5, 0)):
        copy_tiles(whole, 0, main_0, HALF * adjacent, HALF)
        copy_tiles(whole, SLOT, main_0, HALF * second, HALF)
        for i in range(HALF // 4):
            three = [tile(ref, 3 * i + k) for k in range(3)]
            for k in range(3):
                put(my_0, HALF * adjacent + 4 * i + k, three[k])
            fourth = jnp.where(row < 6, roll_row(three[1], 1), roll_row(three[2], 3))
            fourth = jnp.where(row < 4, roll_row(three[1], -1), fourth)
            fourth = jnp.where(row < 2, roll_row(three[0], -3), fourth)
            put(my_0, HALF * adjacent + 4 * i + 3, fourth)
        for i in range(HALF // 2):
            value = tile(ref, A_SECOND + i)
            put(my_0, HALF * second + 2 * i, value)
            put(my_0, HALF * second + 2 * i + 1, roll_row(value, 4))
        for plane, at in ((adjacent, p), (second, 1 - p)):
            copy_tiles(ref, A_EDGE + TG * at, em_0, TG * plane, TG)
            copy_tiles(ref, A_EDGE + NE + TG * at, ey_0, TG * plane, TG)
        em_at, ey_at = A_EDGE + NE - 1, A_EDGE + 2 * NE - 1
        extras[adjacent] = (whole, HALF, ref, A_EXTRA, ref, em_at, ref, ey_at, NEXTRA * p)
        for part, value in enumerate(
            (
                tile(whole, SLOT + HALF),
                tile(ref, A_SECOND + HALF // 2),
                roll_lane(tile(ref, em_at), -8 * (NEXTRA * (1 - p) + 4)),
                roll_lane(tile(ref, ey_at), -8 * (NEXTRA * (1 - p) + 4)),
            )
        ):
            put(conduct_ref, 4 * second + part, value)
    for plane, (a, a_at, b, b_at, c, c_at, d, d_at, q) in extras.items():
        for e in range(NEXTRA):
            values = (
                tile(a, a_at + e),
                tile(b, b_at + e),
                roll_lane(tile(c, c_at), -8 * (q + e)),
                roll_lane(tile(d, d_at), -8 * (q + e)),
            )
            for part, value in enumerate(values):
                if e == NEXTRA - 1:
                    put(conduct_ref, 4 * plane + part, value)
                else:
                    put(given_ref, ((plane - 1) * 4 + e) * 4 + part, value)
    plane_coefficients(sizes, wells_ref, conduct_ref, given_ref, coef_ref)
    step((main_0, my_0, em_0, ey_0), (main_1, my_1, em_1, ey_1), coef_ref, 1, 4, -1, -1)
    step((main_1, my_1, em_1, ey_1), (block_2_ref, my_2_ref, em_2_ref, ey_2_ref), coef_ref, 1, 2, 0, -1)
    for p, (adjacent, second) in enumerate(((to_left_ref, to_right_ref), (to_right_ref, to_left_ref))):
        for i in range(HALF):
            value = tile(block_2_ref, HALF * p + i)
            put(adjacent, i, value)
            put(second, B_SECOND + i, value)
        for i in range(HALF // 4):
            value = tile(my_2_ref, HALF * p + 4 * i)
            for k in range(1, 4):
                at_row = ((row + (1 - 2 * k)) & 7) < 2
                value = jnp.where(at_row, roll_row(tile(my_2_ref, HALF * p + 4 * i + k), 2 * k), value)
            put(adjacent, B_MY + i, value)
        copy_tiles(em_2_ref, TG * p, adjacent, B_EDGE, TG)
    by_plane(((main_1, HALF), (block_2_ref, 0)), keep_ref, send_ref)


def by_plane(levels, keep_ref, send_ref):
    mine, other = core() * HALF, (1 - core()) * HALF
    for level, (ref, base) in enumerate(levels):
        for i in range(HALF):
            put(keep_ref, HALF * level + i, tile(ref, base + mine + i))
            put(send_ref, HALF * level + i, tile(ref, base + other + i))


def last_two_kernel(
    coef_ref,
    block_2_ref,
    my_2_ref,
    em_2_ref,
    ey_2_ref,
    left_ref,
    right_ref,
    _,
    keep_ref,
    send_ref,
    main_2,
    my_2,
    em_2,
    ey_2,
    main_3,
    my_3,
    em_3,
    main_4,
):
    copy_tiles(block_2_ref, 0, main_2, 2 * HALF, 2 * HALF)
    copy_tiles(my_2_ref, 0, my_2, 2 * HALF, 2 * HALF)
    copy_tiles(em_2_ref, 0, em_2, 2 * TG, 2 * TG)
    copy_tiles(ey_2_ref, 0, ey_2, 2 * TG, 2 * TG)
    for ref, adjacent, second in ((left_ref, 1, 0), (right_ref, 4, 5)):
        copy_tiles(ref, 0, main_2, HALF * adjacent, HALF)
        for i in range(HALF // 4):
            value = tile(ref, B_MY + i)
            for k in range(4):
                put(my_2, HALF * adjacent + 4 * i + k, roll_row(value, -2 * k))
        copy_tiles(ref, B_EDGE, em_2, TG * adjacent, TG)
        copy_tiles(ref, B_SECOND, main_2, HALF * second, HALF)
    source, target = (main_2, my_2, em_2, ey_2), (main_3, my_3, em_3, None)
    for plane in (1, 4):
        step(source, target, coef_ref, plane, 1, -1, -1, False, False, False)
    step(source, target, coef_ref, 2, 2, -1, -1, True, True, False)
    step((main_3, my_3, em_3, None), (main_4, None, None, None), coef_ref, 1, 2, 0, -1, False, False, False)
    by_plane(((main_3, HALF), (main_4, 0)), keep_ref, send_ref)


PAIRS = (
    ((0, 0), (0, 1)),
    ((0, 2), (0, 3)),
    ((1, 1), (1, 2)),
    ((1, 3), (1, 4)),
    ((2, 2), (2, 3)),
    ((3, 3), (3, 4)),
    ((4, 4), (2, 4)),
    ((0, 4), None),
)


def two_parts(values):
    high = values.astype(jnp.bfloat16)
    return high, (values - high.astype(jnp.float32)).astype(jnp.bfloat16)


def three_products(first, second, dims):
    def dot(a, b):
        return lax.dot_general(a, b, (dims, ((), ())), preferred_element_type=jnp.float32)

    return dot(first[0], second[0]) + (dot(first[0], second[1]) + dot(first[1], second[0]))


def dot_tn(first, second):
    return lax.dot_general(first, second, (((0,), (0,)), ((), ())), precision=HI, preferred_element_type=jnp.float32)


def dot_nn(first, second):
    return lax.dot_general(first, second, (((1,), (0,)), ((), ())), precision=HI, preferred_element_type=jnp.float32)


def fill_levels(keep_ref, got_ref, basis_ref, base):
    mine, other = core() * HALF, (1 - core()) * HALF
    for y in range(8):
        lanes = slice(128 * y, 128 * (y + 1))
        for level in range(2):
            at = pl.ds(8 * HALF * level + y, HALF, stride=8)
            rows = base + M * level
            basis_ref[pl.ds(pl.multiple_of(rows + mine, 8), HALF), lanes] = keep_ref[at, :]
            basis_ref[pl.ds(pl.multiple_of(rows + other, 8), HALF), lanes] = got_ref[at, :]


def early_gram_kernel(block_0, keep_ref, got_ref, high_ref, low_ref, full_ref, basis_ref):
    for y in range(8):
        basis_ref[0:M, 128 * y : 128 * (y + 1)] = block_0[pl.ds(y, M, stride=8), :]
    fill_levels(keep_ref, got_ref, basis_ref, M)
    parts = two_parts(basis_ref[...])
    high_ref[...], low_ref[...] = parts
    full_ref[...] = three_products(parts, parts, ((1,), (1,)))


def gram_kernel(keep_ref, got_ref, early_high, early_low, early_full, high_ref, low_ref, gram_ref, basis_ref):
    fill_levels(keep_ref, got_ref, basis_ref, 0)
    parts = two_parts(basis_ref[...])
    high_ref[...], low_ref[...] = parts
    among = three_products(parts, parts, ((1,), (1,)))
    across = three_products((early_high[...], early_low[...]), parts, ((1,), (1,)))
    for index, pair in enumerate(PAIRS):
        for half, at in enumerate(pair):
            if at is None:
                value = jnp.zeros((M, M), jnp.float32)
            else:
                first, second = (slice(M * k, M * k + M) for k in at)
                if at[1] < 3:
                    value = early_full[first, second]
                else:
                    source, shift = (among, 3 * M) if at[0] >= 3 else (across, 0)
                    value = source[first.start - shift : first.stop - shift, second.start - 3 * M : second.stop - 3 * M]
            gram_ref[M * index : M * (index + 1), M * half : M * (half + 1)] = value


def eliminate(matrix, wanted):
    both = jnp.concatenate([matrix, wanted], axis=1)
    tiles = [both[8 * i : 8 * i + 8, :] for i in range(M // 8)]
    rows = iota_row()

    def column(value, at):
        return jnp.broadcast_to(value[:, at : at + 1], (8, 128))

    def block(_, tiles):
        tiles = list(tiles)
        columns = [column(tiles[0], b) for b in range(8)]
        row = [jnp.broadcast_to(tiles[0][a : a + 1, :], (8, 128)) for a in range(8)]
        small = [[jnp.broadcast_to(columns[b][a : a + 1, :], (8, 128)) for b in range(8)] for a in range(8)]
        for p in range(8):
            inverse = 1.0 / small[p][p]
            for a in range(p + 1, 8):
                factor = small[p][a] * inverse
                row[a] = row[a] - factor * row[p]
                for b in range(a, 8):
                    small[a][b] = small[a][b] - factor * small[p][b]
            row[p] = row[p] * inverse
            for b in range(p + 1, 8):
                small[p][b] = small[p][b] * inverse
        for p in range(7, 0, -1):
            for a in range(p):
                row[a] = row[a] - small[a][p] * row[p]
        for j in range(1, M // 8):
            value = tiles[j]
            for b in range(8):
                value = value - column(tiles[j], b) * row[b]
            tiles[j] = value
        value = row[0]
        for b in range(1, 8):
            value = jnp.where(rows == b, row[b], value)
        tiles[0] = value
        return tuple(roll_lane(t, -8) for t in tiles[1:] + tiles[:1])

    tiles = lax.fori_loop(0, M // 8, block, tuple(tiles), unroll=1)
    return jnp.concatenate(tiles, axis=0)[:, :M]


def apply_levels(blocks):
    out = [SHIFT * b for b in blocks] + [None]
    for j, b in enumerate(blocks):
        out[j + 1] = SCALE * b if out[j + 1] is None else out[j + 1] + SCALE * b
    return out


def pad_levels(blocks, count):
    return list(blocks) + [jnp.zeros((M, M), jnp.float32)] * (count - len(blocks))


def final_kernel(gram_ref, early_high, early_low, high_ref, low_ref, field_ref, resid_ref, full_ref):
    for index, pair in enumerate(PAIRS):
        for half, at in enumerate(pair):
            if at is None:
                continue
            value = gram_ref[M * index : M * (index + 1), M * half : M * (half + 1)]
            full_ref[M * at[0] : M * at[0] + M, M * at[1] : M * at[1] + M] = value
            if at[0] != at[1]:
                full_ref[M * at[1] : M * at[1] + M, M * at[0] : M * at[0] + M] = value.T
    eye = jnp.where(
        lax.broadcasted_iota(jnp.int32, (M, M), 0) == lax.broadcasted_iota(jnp.int32, (M, M), 1), 1.0, 0.0
    ).astype(jnp.float32)

    def gram(levels, blocks):
        count = M * levels
        return dot_nn(full_ref[0:count, 0 : M * len(blocks)], jnp.concatenate(blocks, axis=0))

    def minimal(half, second):
        levels = len(second)
        product = gram(levels, second)
        cross = sum(product[M * j : M * j + M] * b for j, b in enumerate(half))
        square = sum(product[M * j : M * j + M] * b for j, b in enumerate(second))
        def total(values):
            return jnp.sum(jnp.sum(values, axis=0, keepdims=True), axis=1, keepdims=True)

        return total(cross) / total(square), product[0:M]

    image_gram = SHIFT * full_ref[0:M, 0:M] + SCALE * full_ref[0:M, M : 2 * M]
    inverse = eliminate(dot_tn(image_gram, image_gram), image_gram.T)
    alpha = dot_nn(inverse, full_ref[0:M, 0:M])
    half = [eye - SHIFT * alpha, -SCALE * alpha]
    second = apply_levels(half)
    omega, second_gram = minimal(half, second)
    field = [alpha + omega * half[0], omega * half[1]]
    resid = [half[0] - omega * second[0], half[1] - omega * second[1], -omega * second[2]]
    beta = -dot_nn(inverse, second_gram)
    direct = [
        resid[0] + (1.0 - omega * SHIFT) * beta,
        resid[1] - (omega * SCALE) * beta,
        resid[2],
    ]
    image = apply_levels(direct)
    stacked = jnp.concatenate(
        [jnp.concatenate(image, axis=0), jnp.concatenate(pad_levels(resid, 4), axis=0)], axis=1
    )
    both = dot_nn(full_ref[0:M, 0 : 4 * M], stacked)
    image_gram, resid_gram = both[:, 0:M], both[:, M:]
    inverse = eliminate(dot_tn(image_gram, image_gram), image_gram.T)
    alpha = dot_nn(inverse, resid_gram)
    product = dot_nn(jnp.concatenate(image + direct, axis=0), alpha)
    half = [r - product[M * j : M * j + M] for j, r in enumerate(pad_levels(resid, 4))]
    second = apply_levels(half)
    omega, _ = minimal(half, second)
    field = pad_levels(field, 4)
    moved = [product[M * (4 + j) : M * (5 + j)] for j in range(3)] + [None]
    field = [
        f + omega * h + (0.0 if m is None else m) for f, h, m in zip(field, half, moved)
    ]
    field = pad_levels(field, 5)
    resid = [h - omega * s for h, s in zip(pad_levels(half, 5), second)]
    coefs = jnp.concatenate([jnp.concatenate(field, axis=0), jnp.concatenate(resid, axis=0)], axis=1)
    coefs = coefs.T
    result = three_products(two_parts(coefs[:, 0 : 3 * M]), (early_high[...], early_low[...]), ((1,), (0,)))
    result = result + three_products(two_parts(coefs[:, 3 * M :]), (high_ref[...], low_ref[...]), ((1,), (0,)))
    for y in range(8):
        field_ref[pl.ds(y, M, stride=8), :] = result[0:M, 128 * y : 128 * (y + 1)]
        resid_ref[pl.ds(y, M, stride=8), :] = result[M:, 128 * y : 128 * (y + 1)]


VMEM = pl.BlockSpec(memory_space=pltpu.VMEM)
SMEM = pl.BlockSpec(memory_space=pltpu.SMEM)


def f32(*shape):
    return jax.ShapeDtypeStruct(shape, jnp.float32)


def call(kernel, name, outs, specs, scratch=()):
    return pl.pallas_call(
        kernel,
        name=name,
        out_shape=outs,
        in_specs=specs,
        out_specs=tuple(VMEM for _ in outs) if isinstance(outs, tuple) else VMEM,
        scratch_shapes=list(scratch),
        compiler_params=pltpu.CompilerParams(vmem_limit_bytes=32 * 1024 * 1024),
    )


def from_sides(axis, up, down, by=1):
    count = lax.axis_size(axis)
    lower = lax.ppermute(up, axis, [(i, i + by) for i in range(count - by)])
    upper = lax.ppermute(down, axis, [(i + by, i) for i in range(count - by)])
    return lower, upper


def spread(values, axes):
    count = lax.axis_size(axes)
    return lax.all_to_all(jnp.broadcast_to(values, (count, *values.shape)), axes, 0, 0)


def in_hbm(values):
    return pltpu.with_memory_space_constraint(values, pltpu.HBM)


def other_core(values):
    count = lax.axis_size("gx")
    return lax.ppermute(values, "gx", [(i, i ^ 1) for i in range(count)])


def tiles(count):
    return f32(8 * count, 128)


def scratch(*counts):
    return [pltpu.VMEM((8 * count, 128), jnp.float32) for count in counts]


def per_device(right_side, velocity, decay_rate, perm_class, conductivity, well_cells, well_rate):
    sizes = (lax.axis_size("gx"), 8 * lax.axis_size("gy"), 128 * lax.axis_size("gz"))
    block_0 = right_side.reshape(8 * M, 128)
    any_space = pl.BlockSpec(memory_space=pltpu.HBM)

    send, keep = call(
        pack_kernel,
        "pack",
        (tiles(SLOT), tiles(SLOT)),
        [any_space] * 5,
        [
            pltpu.VMEM((8, 128), jnp.int32),
            pltpu.SMEM(conductivity.shape, jnp.float32),
            pltpu.SemaphoreType.DMA((6,)),
        ],
    )(
        in_hbm(block_0),
        in_hbm(velocity.reshape(24, 128)),
        in_hbm(decay_rate.reshape(8, 128)),
        in_hbm(perm_class.reshape(8, 128)),
        in_hbm(conductivity),
    )
    got = other_core(send)
    wells = call(functools.partial(wells_kernel, sizes), "wells", tiles(16), [SMEM, SMEM])(well_cells, well_rate)
    main, zmsg, to_left, to_right = call(
        zmsg_kernel, "zmsg", (tiles(2 * SLOT), tiles(NE), tiles(EARLY_TILES), tiles(EARLY_TILES)), [VMEM] * 2
    )(keep, got)
    left_main, right_main = from_sides("gx", to_right, to_left, 2)
    low, high = from_sides("gz", zmsg, zmsg)
    up, down, edge = call(ymsg_kernel, "ymsg", (tiles(YPAIRS), tiles(YPAIRS), tiles(NE)), [VMEM] * 3)(
        main, low, high
    )
    below, above = from_sides("gy", up, down)
    my, ey, to_left, to_right = call(
        xmsg_kernel, "xmsg", (tiles(2 * SLOT), tiles(NE), tiles(A_TILES), tiles(A_TILES)), [VMEM] * 3
    )(edge, below, above)
    left, right = from_sides("gx", to_right, to_left, 2)
    coef, keep, send, block_2, my, em, ey, to_left, to_right = call(
        functools.partial(first_two_kernel, sizes),
        "first_two",
        (
            tiles(4 * 28),
            tiles(2 * HALF),
            tiles(2 * HALF),
            tiles(M),
            tiles(M),
            tiles(2 * TG),
            tiles(2 * TG),
            tiles(B_TILES),
            tiles(B_TILES),
        ),
        [VMEM] * 9,
        scratch(24, 64, 6 * HALF, 6 * HALF, 6 * TG, 6 * TG, 4 * HALF, 4 * HALF, 4 * TG, 4 * TG),
    )(wells, main, edge, my, ey, right_main, left_main, right, left)
    left, right = from_sides("gx", to_right, to_left, 2)
    got = other_core(send)

    def rows(levels):
        return jax.ShapeDtypeStruct((levels * M, 1024), jnp.bfloat16)

    early_high, early_low, early_full = call(
        early_gram_kernel,
        "early_gram",
        (rows(3), rows(3), f32(3 * M, 3 * M)),
        [VMEM] * 3,
        [pltpu.VMEM((3 * M, 1024), jnp.float32)],
    )(block_0, keep, got)
    keep, send = call(
        last_two_kernel,
        "last_two",
        (tiles(2 * HALF), tiles(2 * HALF)),
        [VMEM] * 7 + [pl.BlockSpec(memory_space=pl.ANY)],
        scratch(6 * HALF, 6 * HALF, 6 * TG, 6 * TG, 4 * HALF, 4 * HALF, 4 * TG, 2 * HALF),
    )(coef, block_2, my, em, ey, left, right, early_full)
    got = other_core(send)
    high, low, gram = call(
        gram_kernel,
        "gram",
        (rows(2), rows(2), f32(8 * M, 128)),
        [VMEM] * 5,
        [pltpu.VMEM((2 * M, 1024), jnp.float32)],
    )(keep, got, early_high, early_low, early_full)

    plane = ("gz", "gy")
    count = lax.axis_size(plane)
    gram = lax.all_to_all(gram.reshape(count, -1, 128), plane, 0, 0)
    gram = jnp.sum(gram, axis=0)
    gram = jnp.sum(spread(gram, "gx"), axis=0)
    gram = spread(gram, plane).reshape(8 * M, 128)
    field, resid = call(
        final_kernel,
        "final",
        (f32(8 * M, 128), f32(8 * M, 128)),
        [VMEM] * 5,
        [pltpu.VMEM((LEVELS * M, LEVELS * M), jnp.float32)],
    )(gram, early_high, early_low, high, low)
    return field.reshape(right_side.shape), resid.reshape(right_side.shape)


def solution(mesh):
    placed = (
        P(None, "gx", "gy", "gz"),
        P(None, "gx", "gy", "gz"),
        P("gx", "gy", "gz"),
        P("gx", "gy", "gz"),
        P(),
        P(),
        P(),
    )
    return jax.shard_map(
        per_device,
        mesh=mesh,
        in_specs=placed,
        out_specs=(P(None, "gx", "gy", "gz"), P(None, "gx", "gy", "gz")),
        check_vma=False,
    )
```
